32 devices in a mesh: group: 4 (over y, x), patch: 8 (over z, core).
Axes of the slice: x: 2, y: 2, z: 4, core: 2. Of those that a mesh axis runs over, the one named last changes fastest.
Arguments:
- node_tape: bfloat16 [4, 8192, 512], P('group', 'patch'), may hold values from -6 to 6
- edge_tape: bfloat16 [4, 8192, 512], P('group', 'patch'), may hold values from -6 to 6
- node_cot: bfloat16 [4, 8192, 512], P('group', 'patch'), may hold values from -6 to 6
- edge_cot: bfloat16 [4, 8192, 512], P('group', 'patch'), may hold values from -6 to 6
- w_edge_in: bfloat16 [1536, 512], replicated, may hold values from -0.15625 to 0.15625
- w_edge_out: bfloat16 [512, 512], replicated, may hold values from -0.25 to 0.25
- gain_edge: float32 [512], replicated, may hold values from 0.1 to 1.9
- w_node_in: bfloat16 [1024, 512], replicated, may hold values from -0.1875 to 0.1875
- w_node_out: bfloat16 [512, 512], replicated, may hold values from -0.25 to 0.25
- gain_node: float32 [512], replicated, may hold values from 0.1 to 1.9
- senders: int32 [64, 128], P('patch'), may hold values from 0 to 1279
- receivers: int32 [64, 128], P('patch'), may hold values from 0 to 1023
- tile_count: int32 [8], P('patch'), may hold values from 1 to 8, as said below
- send_rows: int32 [8, 256], P('patch'), may hold values from 0 to 1023
Outputs:
- edge_grad: bfloat16 [4, 8192, 512], P('group', 'patch')
- node_grad: bfloat16 [4, 8192, 512], P('group', 'patch')
- grad_edge_in: float32 [1536, 512], P('patch')
- grad_edge_out: float32 [512, 512], P('patch')
- grad_gain_edge: float32 [512], P('patch')
- grad_node_in: float32 [1024, 512], P('patch')
- grad_node_out: float32 [512, 512], P('patch')
- grad_gain_node: float32 [512], P('patch')
The draws below stay inside these ranges and needn't reach their ends.
Inputs may be any that keep to these rules, and one draw needn't show every extreme that they name: Tiles 0 to tile_count - 1 of a patch's 8 slots hold edges, the rest are padding; some patch has all 8 live. `senders`: A value s below 1024 is a node of the edge's own patch; 1024 + k is the k-th halo row that patch receives, rows p * 32 to (p + 1) * 32 - 1 coming from patch p. `receivers`: A node of the edge's own patch. `send_rows`: entry p * 32 + j of patch q's list is the own node whose latent is the j-th halo row patch p receives from q; every patch sends exactly 32 rows to every patch.
All inputs are finite; a program needn't handle non-finite values.
Results may differ from the reference program's by a relative error of at most 0.014.
Values may be sent and summed in bfloat16 or wider, within the bound.
A program may use at most 128 MiB of HBM per device.

```python
import jax
import jax.numpy as jnp
from jax import lax

L = 512
NODE_DEV = 1024
TCAP = 8
TILE = 128
HALO_DEV = 256
NODES = 8192
TILES = 64
EDGES = 8192
N_GROUP = 4
N_PATCH = 8


def draw_tile_count(key, part):
    devices = TILES // TCAP
    first_key, second_key, third_key = jax.random.split(jax.random.fold_in(key, 11), 3)
    lowest = jax.random.randint(first_key, (devices,), 1, TCAP // 2 + 1)
    crowded = jax.random.randint(second_key, (devices,), 0, 4) == 0
    chosen = jax.random.randint(third_key, (), 0, devices)
    filled = crowded | (jnp.arange(devices) == chosen)
    return jnp.where(filled, TCAP, lowest).astype(jnp.int32)


def set_ends(drawn, rng, smallest, top_value):
    longest = drawn.shape.index(max(drawn.shape))
    spots = []
    for shift in (0, 1):
        where = [jax.random.randint(jax.random.fold_in(rng, axis), (), 0, length) for axis, length in enumerate(drawn.shape)]
        where[longest] = (where[longest] + shift) % drawn.shape[longest]
        spots.append(tuple(where))
    return drawn.at[spots[0]].set(smallest).at[spots[1]].set(top_value)


def with_spikes(result, own_key, source, target, blocks, factor):
    def block_of(dim):
        return (jnp.arange(result.shape[dim]) // (result.shape[dim] // blocks)).reshape((-1,) + (1,) * (result.ndim - 1 - dim))

    first = jax.random.permutation(own_key, blocks)[block_of(target)]
    second = (block_of(target) + blocks // 2) % blocks
    return jnp.where((block_of(source) == first) | (block_of(source) == second), factor * result, result)


def block_levels(key, extent, cuts, least, largest):
    def one(position, shards_of):
        steps = jax.random.uniform(jax.random.fold_in(jax.random.fold_in(key, 6), position), (shards_of,), jnp.float32, least / len(cuts), largest / len(cuts))
        return jnp.repeat(jnp.exp(steps), extent[position] // shards_of).reshape((-1,) + (1,) * (len(extent) - position - 1))

    gain = one(*cuts[0])
    for cut in cuts[1:]:
        gain = gain * one(*cut)
    return gain


def bell_draw(key, shape, width, bound, cuts=(), kind=jnp.bfloat16):
    entries = jax.random.normal(key, shape, jnp.float32) * width
    if len(cuts) > 0:
        entries = block_levels(key, shape, cuts, -0.22, 0.18) * entries
    return jnp.clip(entries, min=-bound, max=bound).astype(kind)


def gaussian_with(own_key, extent, deviation, most, pieces, heavy, kind=jnp.bfloat16):
    values = deviation * jax.random.normal(own_key, extent, jnp.float32)
    if pieces:
        values = values * block_levels(own_key, extent, pieces, -0.22, 0.18)
    return jnp.clip(with_spikes(values, jax.random.fold_in(own_key, 3), *heavy), -most, most).astype(kind)


def setup_inputs(seed: int = 0) -> dict:
    arg_keys = jax.random.split(jax.random.key(seed), 15)
    node_tape = bell_draw(arg_keys[0], (N_GROUP, NODES, L), 1.0, 6.0, ((0, 4), (1, 8)))
    edge_tape = gaussian_with(arg_keys[1], (N_GROUP, EDGES, L), 1.0, 6.0, ((0, 4), (1, 8)), (1, 2, 8, 2.0))
    node_cot = bell_draw(arg_keys[2], (N_GROUP, NODES, L), 1.0, 6.0, ((0, 4), (1, 8)))
    edge_cot = bell_draw(arg_keys[3], (N_GROUP, EDGES, L), 1.0, 6.0, ((0, 4), (1, 8)))
    w_edge_in = bell_draw(arg_keys[4], (3 * L, L), (3 * L) ** -0.5, 0.15625)
    w_edge_out = bell_draw(arg_keys[5], (L, L), L ** -0.5, 0.25)
    gain_edge = jnp.clip(1.0 + 0.18 * jax.random.normal(arg_keys[6], (L,), jnp.float32), 0.1, 1.9)
    w_node_in = bell_draw(arg_keys[7], (2 * L, L), (2 * L) ** -0.5, 0.1875)
    w_node_out = bell_draw(arg_keys[8], (L, L), L ** -0.5, 0.25)
    gain_node = jnp.clip(1.0 + 0.18 * jax.random.normal(arg_keys[9], (L,), jnp.float32), 0.1, 1.9)
    senders = set_ends(jax.random.randint(arg_keys[10], (TILES, TILE), 0, NODE_DEV + HALO_DEV), jax.random.fold_in(arg_keys[10], 1), 0, (NODE_DEV + HALO_DEV) - 1).astype(jnp.int32)
    receivers = set_ends(jax.random.randint(arg_keys[11], (TILES, TILE), 0, NODE_DEV), jax.random.fold_in(arg_keys[11], 1), 0, NODE_DEV - 1).astype(jnp.int32)
    tile_count = draw_tile_count(jax.random.fold_in(arg_keys[14], 71), 0)
    send_rows = set_ends(jax.random.randint(arg_keys[13], (N_PATCH, HALO_DEV), 0, NODE_DEV), jax.random.fold_in(arg_keys[13], 1), 0, NODE_DEV - 1).astype(jnp.int32)
    return dict(node_tape=node_tape, edge_tape=edge_tape, node_cot=node_cot, edge_cot=edge_cot, w_edge_in=w_edge_in, w_edge_out=w_edge_out, gain_edge=gain_edge, w_node_in=w_node_in, w_node_out=w_node_out, gain_node=gain_node, senders=senders, receivers=receivers, tile_count=tile_count, send_rows=send_rows)


epsilon = 1e-05

def product(left, right):
    return jnp.dot(left, right, preferred_element_type=jnp.float32)

def silu_slope(values):
    squash = jax.nn.sigmoid(values)
    return squash * (1.0 + values * (1.0 - squash))

def normalize(values):
    centred = values - lax.optimization_barrier(jnp.mean(values, axis=1, keepdims=True))
    inverse = lax.rsqrt(lax.optimization_barrier(jnp.mean(centred * centred, axis=1, keepdims=True)) + epsilon)
    return (centred * inverse, inverse)

def normalize_back(upstream, normed, inverse):
    return inverse * (upstream - lax.optimization_barrier(jnp.mean(upstream, axis=1, keepdims=True)) - normed * lax.optimization_barrier(jnp.mean(upstream * normed, axis=1, keepdims=True)))

def member(node_rows, edge_rows, node_back, edge_back, weights, send_index, recv_index, live_mask):
    w_edge_in, w_edge_out, gain_edge, w_node_in, w_node_out, gain_node = weights
    features = node_rows.shape[1]
    node_count = node_rows.shape[0]
    edge_input = jnp.concatenate([edge_rows, node_rows[send_index], node_rows[recv_index]], axis=1)
    edge_first = product(edge_input, w_edge_in)
    hidden = jax.nn.silu(edge_first).astype(jnp.bfloat16)
    second = product(hidden, w_edge_out)
    normed_edge, inverse_edge = normalize(second)
    message = live_mask * (gain_edge.astype(jnp.float32) * normed_edge)
    gathered = jax.ops.segment_sum(message, recv_index, num_segments=node_count).astype(jnp.bfloat16)
    joined = jnp.concatenate([node_rows, gathered], axis=1)
    node_first = product(joined, w_node_in)
    node_hidden = jax.nn.silu(node_first).astype(jnp.bfloat16)
    node_second = product(node_hidden, w_node_out)
    normed_node, inverse_node = normalize(node_second)
    node_upstream = node_back.astype(jnp.float32)
    part_gain_node = lax.optimization_barrier(jnp.sum(node_upstream * normed_node, axis=0))
    grad_second = normalize_back(node_upstream * gain_node.astype(jnp.float32), normed_node, inverse_node).astype(jnp.bfloat16)
    part_node_out = product(node_hidden.T, grad_second)
    grad_first = (product(grad_second, w_node_out.T) * silu_slope(node_first)).astype(jnp.bfloat16)
    part_node_in = product(joined.T, grad_first)
    grad_joined = product(grad_first, w_node_in.T)
    grad_message = live_mask * (edge_back.astype(jnp.float32) + grad_joined[:, features:][recv_index])
    part_gain_edge = lax.optimization_barrier(jnp.sum(grad_message * normed_edge, axis=0))
    grad_edge_second = normalize_back(grad_message * gain_edge.astype(jnp.float32), normed_edge, inverse_edge).astype(jnp.bfloat16)
    part_edge_out = product(hidden.T, grad_edge_second)
    grad_edge_first = (product(grad_edge_second, w_edge_out.T) * silu_slope(edge_first)).astype(jnp.bfloat16)
    part_edge_in = product(edge_input.T, grad_edge_first)
    grad_input = product(grad_edge_first, w_edge_in.T)
    edge_grad = (live_mask * edge_back.astype(jnp.float32) + grad_input[:, :features]).astype(jnp.bfloat16)
    from_send = jax.ops.segment_sum(grad_input[:, features:2 * features], send_index, num_segments=node_count)
    from_recv = jax.ops.segment_sum(grad_input[:, 2 * features:], recv_index, num_segments=node_count)
    node_grad = (node_upstream + grad_joined[:, :features] + from_send + from_recv).astype(jnp.bfloat16)
    return (edge_grad, node_grad, (part_edge_in, part_edge_out, part_gain_edge, part_node_in, part_node_out, part_gain_node))

def reference(node_tape, edge_tape, node_cot, edge_cot, w_edge_in, w_edge_out, gain_edge, w_node_in, w_node_out, gain_node, senders, receivers, tile_count, send_rows):
    edge_slots = TCAP * TILE
    peer_rows = HALO_DEV // N_PATCH
    flat_send = senders.reshape(-1).astype(jnp.int32)
    slot_ids = jnp.arange(EDGES, dtype=jnp.int32)
    owner_dev = slot_ids // edge_slots
    halo_pos = jnp.maximum(flat_send - NODE_DEV, 0)
    source = halo_pos // peer_rows
    column = owner_dev * peer_rows + halo_pos % peer_rows
    remote = source * NODE_DEV + send_rows[source, column]
    send_index = jnp.where(flat_send < NODE_DEV, owner_dev * NODE_DEV + flat_send, remote).astype(jnp.int32)
    recv_index = (owner_dev * NODE_DEV + receivers.reshape(-1)).astype(jnp.int32)
    tile_slot = slot_ids % edge_slots // TILE
    live_mask = (tile_slot < tile_count[owner_dev]).astype(jnp.float32)[:, None]
    weights = (w_edge_in, w_edge_out, gain_edge, w_node_in, w_node_out, gain_node)

    def run_member(inputs):
        return member(inputs[0], inputs[1], inputs[2], inputs[3], weights, send_index, recv_index, live_mask)
    edge_grad, node_grad, partials = lax.map(run_member, (node_tape, edge_tape, node_cot, edge_cot))
    factor = (N_GROUP * EDGES) ** (-0.5)
    sums = [lax.optimization_barrier(jnp.sum(stack, axis=0)) * factor for stack in partials]
    return (edge_grad, node_grad, sums[0], sums[1], sums[2], sums[3], sums[4], sums[5])
```

```python
import functools

import jax
import jax.numpy as jnp
from jax import lax
from jax.experimental import pallas as pl
from jax.experimental.pallas import tpu as pltpu
from jax.sharding import PartitionSpec as P

epsilon = 1e-05
BF = jnp.bfloat16
F32 = jnp.float32
LANES = 128
PACK = 16
MESH = pl.DeviceIdType.MESH


def dot(left, right):
    return jnp.dot(left, right, preferred_element_type=F32)


def dot_rt(left, right):
    return lax.dot_general(left, right, (((1,), (1,)), ((), ())), preferred_element_type=F32)


def dot_lt(left, right):
    return lax.dot_general(left, right, (((0,), (0,)), ((), ())), preferred_element_type=F32)


def silu_pair(values):
    squash = 0.5 * jnp.tanh(0.5 * values) + 0.5
    active = values * squash
    return (active, squash + active * (1.0 - squash))


def normalize(values):
    centred = values - jnp.mean(values, axis=1, keepdims=True)
    inverse = lax.rsqrt(jnp.mean(centred * centred, axis=1, keepdims=True) + epsilon)
    return (centred * inverse, inverse)


def normalize_back(upstream, normed, inverse):
    return inverse * (
        upstream
        - jnp.mean(upstream, axis=1, keepdims=True)
        - normed * jnp.mean(upstream * normed, axis=1, keepdims=True)
    )


def hot(index, shape, axis, base):
    return jnp.where(lax.broadcasted_iota(jnp.int32, shape, axis) + base == index, 1.0, 0.0).astype(
        BF
    )


class Copies:
    def __init__(self, send_sems, recv_sems):
        self.send_sems, self.recv_sems, self.used = send_sems, recv_sems, 0

    def start(self, source, target, device):
        copy = pltpu.make_async_remote_copy(
            src_ref=source,
            dst_ref=target,
            send_sem=self.send_sems.at[self.used],
            recv_sem=self.recv_sems.at[self.used],
            device_id=device,
            device_id_type=MESH,
        )
        self.used += 1
        copy.start()
        return copy


def wait_all(copies):
    for copy in copies:
        copy.wait()


class Place:
    def __init__(self, n_patch):
        self.gi = lax.axis_index("group")
        self.p = lax.axis_index("patch")
        self.core = lax.rem(self.p, 2)
        self.z = lax.div(self.p, 2)
        self.zs = n_patch // 2
        self.partner = {"group": self.gi, "patch": self.p + 1 - 2 * self.core}
        gx, gy = lax.rem(self.gi, 2), lax.div(self.gi, 2)
        flip_x, flip_y = 1 - 2 * gx, 2 - 4 * gy
        self.members = [self.gi + flip_x, self.gi + flip_y, self.gi + flip_x + flip_y]

    def member(self, order):
        return {"group": self.members[order], "patch": self.p}


class Reduction:
    def __init__(self, copies, refs, place):
        self.copies, self.place = copies, place
        self.g, self.rc, self.a, self.rx, self.c, self.r3, self.f = refs
        self.pairs, self.moves = [], []

    def put(self, k, row, size, value):
        value = value.astype(BF)
        for c in range(2):
            for quarter in range(4):
                self.g[c, k, quarter, row : row + size, :] = value[
                    c * size : (c + 1) * size, quarter * LANES : (quarter + 1) * LANES
                ]

    def pair(self, k):
        here = self.place
        self.pairs.append(
            self.copies.start(self.g.at[1 - here.core, k], self.rc.at[k], here.partner)
        )

    def spread(self, first, last):
        here = self.place
        for k in range(first, last):
            self.pairs[k].wait()
            for quarter in range(4):
                self.a[quarter, k] = (
                    self.g[here.core, k, quarter].astype(F32) + self.rc[k, quarter].astype(F32)
                ).astype(BF)
        span = pl.ds(first, last - first)
        for order in range(3):
            self.moves.append(
                self.copies.start(
                    self.a.at[here.members[order], span],
                    self.rx.at[order, span],
                    here.member(order),
                )
            )

    def along(self):
        here = self.place
        wait_all(self.moves)
        for k in range(here.zs):
            self.c[k] = (
                (self.a[here.gi, k].astype(F32) + self.rx[0, k].astype(F32))
                + (self.rx[1, k].astype(F32) + self.rx[2, k].astype(F32))
            ).astype(BF)
        self.moves = []
        for step in range(1, here.zs):
            there = lax.rem(here.z + step, here.zs)
            self.moves.append(
                self.copies.start(
                    self.c.at[there],
                    self.r3.at[step - 1],
                    {"group": here.gi, "patch": there * 2 + here.core},
                )
            )

    def share(self):
        here = self.place
        wait_all(self.moves)
        total = self.c[here.z].astype(F32)
        for step in range(1, here.zs):
            total += self.r3[step - 1].astype(F32)
        self.f[here.gi] = total.astype(BF)
        mine = self.f.at[here.gi]
        self.moves = [self.copies.start(mine, mine, here.member(order)) for order in range(3)]

    def finish(self, out):
        wait_all(self.moves)
        out[...] = self.f[...]


COUNT_SHARES = 7


def kernel(sizes, *refs):
    n_group, n_patch, padded, tile, tile_edges, fused, depths = sizes
    refs = list(refs)

    def take(count):
        got = refs[:count]
        del refs[:count]
        return got

    stored = take(14)
    edge_out, node_out = take(2)
    sums = take(3 if fused else 5)
    loaded = take(14)
    node, list_in, send_tiles, recv_tiles, edge, w_ei, w_eo, gain_e = loaded[:8]
    w_ni, w_no, gain_n, node_cot, edge_cot, count = loaded[8:]
    edge_grad, node_grad, load_sems, store_sems = take(4)
    send_col, send_row, recv_col, recv_row, list_col, list_row = take(6)
    outgoing, incoming, spread, returned = take(4)
    x_s, x_r, e_first, hidden, normed, inverse, message, joined = take(8)
    n_hidden, n_first, g_second, g_first, acc, gj, ge_second, ge_first, gs, gr, gains = take(11)
    send_sems, recv_sems = take(2)
    nodes, width = node.shape
    edges = edge.shape[0]
    halo = n_patch * padded
    place = Place(n_patch)
    gi, p = place.gi, place.p
    copies = Copies(send_sems, recv_sems)
    barrier = pltpu.get_barrier_semaphore()
    peers = [{"group": gi, "patch": lax.rem(p + d, n_patch)} for d in range(1, n_patch)]
    greeted = list(peers)
    if fused:
        greeted += [place.member(order) for order in range(3)]
    for peer in greeted:
        pl.semaphore_signal(barrier, inc=1, device_id=peer, device_id_type=MESH)
    loads = [
        pltpu.make_async_copy(source, target, load_sems.at[order])
        for order, (source, target) in enumerate(zip(stored, loaded))
    ]
    for load in loads:
        load.start()

    def column_of(line, column):
        for order in range(column.shape[0] // LANES):
            span = slice(order * LANES, (order + 1) * LANES)
            wide = jnp.broadcast_to(line[:, span].astype(F32), (8, LANES))
            column[span, :] = jnp.transpose(wide)[:, :1].astype(jnp.int32)

    loads[1].wait()
    list_row[...] = list_in[...]
    column_of(list_row, list_col)
    loads[0].wait()
    chosen = dot(hot(list_col[:halo, :], (halo, nodes), 1, 0), node[...]).astype(BF)
    outgoing[...] = chosen.reshape(n_patch, padded, width)
    pl.semaphore_wait(barrier, len(greeted))
    moving = [
        copies.start(outgoing.at[lax.rem(p + d, n_patch)], incoming.at[p], peers[d - 1])
        for d in range(1, n_patch)
    ]
    incoming[p] = outgoing[p]
    gains[...] = jnp.zeros_like(gains)

    loads[2].wait()
    loads[3].wait()
    for tiles, column, line in ((send_tiles, send_col, send_row), (recv_tiles, recv_col, recv_row)):
        turned = jnp.transpose(tiles[...].astype(F32)).astype(jnp.int32)
        for order in range(line.shape[1] // LANES):
            span = slice(order * LANES, (order + 1) * LANES)
            column[span, :] = turned[:, order : order + 1]
            line[:, span] = tiles[order : order + 1, :]

    loads[4].wait()
    loads[5].wait()

    def rows_of(k):
        return pl.ds(pl.multiple_of(k * tile, tile), tile)

    edge_tiles, node_tiles = edges // tile, nodes // tile

    @pl.loop(0, edge_tiles, unroll=fused)
    def _(k):
        rows = rows_of(k)
        latent = dot(hot(recv_col[rows, :], (tile, nodes), 1, 0), node[...]).astype(BF)
        x_r[rows, :] = latent
        e_first[rows, :] = dot(edge[rows, :], w_ei[:width, :]) + dot(latent, w_ei[2 * width :, :])


    @pl.loop(0, edge_tiles, unroll=fused)
    def _(k):
        rows = rows_of(k)
        x_s[rows, :] = dot(hot(send_col[rows, :], (tile, nodes), 1, 0), node[...]).astype(BF)

    loads[8].wait()

    @pl.loop(0, node_tiles, unroll=fused)
    def _(k):
        rows = rows_of(k)
        n_first[rows, :] = dot(node[rows, :], w_ni[:width, :])

    for load in loads[6:8] + loads[9:]:
        load.wait()
    wait_all(moving)

    def live_of(k):
        slot = lax.broadcasted_iota(jnp.int32, (tile, 1), 0) + k * tile
        return jnp.where(slot < count[0] * tile_edges, 1.0, 0.0)


    @pl.loop(0, edge_tiles, unroll=fused)
    def _(k):
        rows = rows_of(k)
        latent = dot(
            hot(send_col[rows, :], (tile, halo), 1, nodes), incoming[...].reshape(halo, width)
        )
        latent = x_s[rows, :] + latent.astype(BF)
        x_s[rows, :] = latent
        first = e_first[rows, :] + dot(latent, w_ei[width : 2 * width, :])
        active, slope = silu_pair(first)
        e_first[rows, :] = slope
        hid = active.astype(BF)
        hidden[rows, :] = hid
        norm, inv = normalize(dot(hid, w_eo[...]))
        normed[rows, :] = norm
        inverse[rows, :] = inv
        message[rows, :] = (live_of(k) * (gain_e[...] * norm)).astype(BF)


    @pl.loop(0, node_tiles, unroll=fused)
    def _(k):
        rows = rows_of(k)
        got = dot(hot(recv_row[...], (tile, edges), 0, k * tile), message[...]).astype(BF)
        joined[rows, :] = got
        first = n_first[rows, :] + dot(got, w_ni[width:, :])
        active, slope = silu_pair(first)
        hid = active.astype(BF)
        n_hidden[rows, :] = hid
        norm, inv = normalize(dot(hid, w_no[...]))
        up = node_cot[rows, :].astype(F32)
        gains[1:2, :] += jnp.sum(up * norm, axis=0, keepdims=True)
        second = normalize_back(up * gain_n[...], norm, inv).astype(BF)
        g_second[rows, :] = second
        grad = (dot_rt(second, w_no[...]) * slope).astype(BF)
        g_first[rows, :] = grad
        acc[rows, :] = up + dot_rt(grad, w_ni[:width, :])
        gj[rows, :] = dot_rt(grad, w_ni[width:, :]).astype(BF)

    def edge_back(k):
        rows = rows_of(k)
        taken = dot(hot(recv_col[rows, :], (tile, nodes), 1, 0), gj[...])
        live = live_of(k)
        norm = normed[rows, :]
        grad = live * (edge_cot[rows, :].astype(F32) + taken)
        gains[0:1, :] += jnp.sum(grad * norm, axis=0, keepdims=True)
        second = normalize_back(grad * gain_e[...], norm, inverse[rows, :]).astype(BF)
        ge_second[rows, :] = second
        ge_first[rows, :] = (dot_rt(second, w_eo[...]) * e_first[rows, :]).astype(BF)

    def rows_product(sources, start, stop, right):
        parts = []
        for order, source in enumerate(sources):
            low = max(start, order * width) - order * width
            high = min(stop, (order + 1) * width) - order * width
            if low < high:
                parts.append(dot_lt(source[:, low:high], right))
        return parts[0] if len(parts) == 1 else jnp.concatenate(parts, axis=0)

    if fused:
        zs = place.zs
        d_ei, d_eo, d_ni, d_no = depths
        red_n = Reduction(copies, take(COUNT_SHARES), place)
        red_e = Reduction(copies, take(COUNT_SHARES), place)
        red_o = Reduction(copies, take(COUNT_SHARES), place)
        for k in range(zs):
            start = 2 * k * d_ni
            red_n.put(
                k, 0, d_ni, rows_product((node, joined), start, start + 2 * d_ni, g_first[...])
            )
            red_n.put(
                k,
                d_ni,
                d_no,
                dot_lt(n_hidden[:, 2 * k * d_no : 2 * (k + 1) * d_no], g_second[...]),
            )
            red_n.pair(k)
            if k == zs - 2:
                red_n.spread(0, zs // 2)
        pl.loop(0, edge_tiles // 2, unroll=True)(edge_back)
        red_n.spread(zs // 2, zs)
        pl.loop(edge_tiles // 2, edge_tiles, unroll=True)(edge_back)
        for k in range(zs):
            start = 2 * k * d_ei
            red_e.put(
                k, 0, d_ei, rows_product((edge, x_s, x_r), start, start + 2 * d_ei, ge_first[...])
            )
            red_e.pair(k)
        red_e.spread(0, zs // 2)
    else:
        o_ei, o_eo, o_ni, o_no, o_gain = sums
        o_ni[:width, :] = dot_lt(node[...], g_first[...])
        o_ni[width:, :] = dot_lt(joined[...], g_first[...])
        o_no[...] = dot_lt(n_hidden[...], g_second[...])
        pl.loop(0, edge_tiles)(edge_back)
        o_ei[:width, :] = dot_lt(edge[...], ge_first[...])
        o_ei[width : 2 * width, :] = dot_lt(x_s[...], ge_first[...])
        o_ei[2 * width :, :] = dot_lt(x_r[...], ge_first[...])
        o_eo[...] = dot_lt(hidden[...], ge_second[...])
        o_gain[...] = gains[...]

    @pl.loop(0, edge_tiles, unroll=fused)
    def _(k):
        rows = rows_of(k)
        gs[rows, :] = dot_rt(ge_first[rows, :], w_ei[width : 2 * width, :]).astype(BF)

    back = dot(hot(send_row[...], (halo, edges), 0, nodes), gs[...]).astype(BF)
    spread[...] = back.reshape(n_patch, padded, width)
    moving = [
        copies.start(spread.at[lax.rem(p + d, n_patch)], returned.at[p], peers[d - 1])
        for d in range(1, n_patch)
    ]
    returned[p] = spread[p]
    if fused:
        red_e.spread(zs // 2, zs)
        for k in range(zs):
            red_o.put(
                k, 0, d_eo, dot_lt(hidden[:, 2 * k * d_eo : 2 * (k + 1) * d_eo], ge_second[...])
            )
            total = gains[...]
            red_o.put(k, d_eo, PACK, jnp.concatenate([total, total], axis=0))
            red_o.pair(k)

    @pl.loop(0, edge_tiles, unroll=fused)
    def _(k):
        rows = rows_of(k)
        gr[rows, :] = dot_rt(ge_first[rows, :], w_ei[2 * width :, :]).astype(BF)

    if fused:
        red_o.spread(0, zs)

    @pl.loop(0, edge_tiles, unroll=fused)
    def _(k):
        rows = rows_of(k)
        edge_grad[rows, :] = (
            live_of(k) * edge_cot[rows, :].astype(F32) + dot_rt(ge_first[rows, :], w_ei[:width, :])
        ).astype(BF)

    stores = [pltpu.make_async_copy(edge_grad, edge_out, store_sems.at[0])]
    stores[0].start()

    def gather_back(k):
        rows = rows_of(k)
        acc[rows, :] += dot(hot(send_row[...], (tile, edges), 0, k * tile), gs[...]) + dot(
            hot(recv_row[...], (tile, edges), 0, k * tile), gr[...]
        )

    if fused:
        red_n.along()
    pl.loop(0, node_tiles, unroll=fused)(gather_back)
    if fused:
        red_e.along()
        red_o.along()
    wait_all(moving)

    @pl.loop(0, node_tiles, unroll=fused)
    def _(k):
        rows = rows_of(k)
        node_grad[rows, :] = (
            acc[rows, :]
            + dot(
                hot(list_row[:, :halo], (tile, halo), 0, k * tile),
                returned[...].reshape(halo, width),
            )
        ).astype(BF)

    stores.append(pltpu.make_async_copy(node_grad, node_out, store_sems.at[1]))
    stores[1].start()
    if fused:
        red_n.share()
        red_e.share()
        red_o.share()
        red_n.finish(sums[0])
        red_e.finish(sums[1])
        red_o.finish(sums[2])
    for store in stores:
        store.wait()


def closing(factor, depths, *refs):
    edge_in, node_in, sum_n, sum_e, sum_o = refs[:5]
    edge_out, node_out, o_ei, o_eo, o_gain_e, o_ni, o_no, o_gain_n = refs[5:13]
    edge_hold, node_hold, load_sems, store_sems = refs[13:]
    d_ei, d_eo, d_ni, d_no = depths
    moves = [(edge_in, edge_hold, edge_out), (node_in, node_hold, node_out)]
    loads = [
        pltpu.make_async_copy(source, hold, load_sems.at[order])
        for order, (source, hold, _) in enumerate(moves)
    ]
    for load in loads:
        load.start()
    for quarter in range(4):
        span = slice(quarter * LANES, (quarter + 1) * LANES)
        o_ni[:, span] = sum_n[quarter, :d_ni].astype(F32) * factor
        o_no[:, span] = sum_n[quarter, d_ni:].astype(F32) * factor
        o_ei[:, span] = sum_e[quarter].astype(F32) * factor
        o_eo[:, span] = sum_o[quarter, :d_eo].astype(F32) * factor
    piece = o_gain_e.shape[1]
    p = lax.axis_index("patch")
    own = jnp.zeros((PACK, piece), F32)
    for quarter in range(4):
        lane = lax.broadcasted_iota(jnp.int32, (LANES, piece), 0) + quarter * LANES
        want = lax.broadcasted_iota(jnp.int32, (LANES, piece), 1) + p * piece
        pick = jnp.where(lane == want, 1.0, 0.0).astype(BF)
        own += dot(sum_o[quarter, d_eo:], pick)
    o_gain_e[...] = own[0:1] * factor
    o_gain_n[...] = own[1:2] * factor
    stores = []
    for order, (_, hold, out) in enumerate(moves):
        loads[order].wait()
        stores.append(pltpu.make_async_copy(hold, out, store_sems.at[order]))
        stores[order].start()
    for store in stores:
        store.wait()


def reduction_scratch(zs, depth):
    shapes = (
        (2, zs, 4, depth),
        (zs, 4, depth),
        (4, zs, depth),
        (3, zs, depth),
        (zs, depth),
        (zs - 1, depth),
        (4, depth),
    )
    return [pltpu.VMEM(shape + (LANES,), BF) for shape in shapes]


def local(
    n_group,
    n_patch,
    node_tape,
    edge_tape,
    node_cot,
    edge_cot,
    w_edge_in,
    w_edge_out,
    gain_edge,
    w_node_in,
    w_node_out,
    gain_node,
    senders,
    receivers,
    tile_count,
    send_rows,
):
    nodes, width = node_tape.shape[1:]
    edges = edge_tape.shape[1]
    listed = send_rows.shape[1]
    peer_rows = listed // n_patch
    padded = -(-peer_rows // PACK) * PACK
    halo = n_patch * padded
    tile = min(2 * LANES, nodes, edges)
    factor = float(n_group * n_patch * edges) ** (-0.5)

    if padded != peer_rows:
        beyond = senders - nodes
        beyond = beyond // peer_rows * padded + beyond % peer_rows
        senders = jnp.where(senders < nodes, senders, nodes + beyond)
        send_rows = jnp.pad(
            send_rows.reshape(n_patch, peer_rows),
            ((0, 0), (0, padded - peer_rows)),
            constant_values=-1,
        ).reshape(1, halo)
    slots = -(-halo // LANES) * LANES
    if slots != halo:
        send_rows = jnp.pad(send_rows, ((0, 0), (0, slots - halo)), constant_values=-1)

    def lane_rows(index):
        rows = -(-index.size // LANES)
        full = -(-rows // 8) * 8
        if index.shape == (full, LANES):
            return index
        return jnp.pad(index.reshape(-1), (0, full * LANES - index.size)).reshape(full, LANES)

    weights = (w_edge_in, w_edge_out, w_node_in, w_node_out)
    depths = [w.shape[0] // n_patch for w in weights]
    zs = n_patch // 2
    fused = (
        n_group == 4
        and n_patch % 4 == 0
        and width == 4 * LANES
        and all(d % PACK == 0 and 2 * d % LANES == 0 for d in depths)
    )
    operands = (
        node_tape[0],
        send_rows,
        lane_rows(senders),
        lane_rows(receivers),
        edge_tape[0],
        w_edge_in,
        w_edge_out,
        gain_edge[None],
        w_node_in,
        w_node_out,
        gain_node[None],
        node_cot[0],
        edge_cot[0],
        tile_count,
    )
    scratch = [pltpu.VMEM(operand.shape, operand.dtype) for operand in operands[:-1]]
    scratch += [pltpu.SMEM(tile_count.shape, tile_count.dtype)]
    scratch += [
        pltpu.VMEM((edges, width), BF),
        pltpu.VMEM((nodes, width), BF),
        pltpu.SemaphoreType.DMA((len(operands),)),
        pltpu.SemaphoreType.DMA((2,)),
    ]
    for length in (edges, edges, slots):
        scratch += [pltpu.VMEM((length, 1), jnp.int32), pltpu.VMEM((1, length), jnp.int32)]
    scratch += [pltpu.VMEM((n_patch, padded, width), BF)] * 4
    by_edge, by_node = pltpu.VMEM((edges, width), BF), pltpu.VMEM((nodes, width), BF)
    wide_edge, wide_node = pltpu.VMEM((edges, width), F32), pltpu.VMEM((nodes, width), F32)
    scratch += [by_edge, by_edge, wide_edge, by_edge, wide_edge, pltpu.VMEM((edges, 1), F32)]
    scratch += [by_edge, by_node]
    scratch += [by_node, wide_node, by_node, by_node, wide_node, by_node]
    scratch += [by_edge, by_edge, by_edge, by_edge, pltpu.VMEM((PACK, width), F32)]
    n_copies = 2 * (n_patch - 1)
    d_ei, d_eo, d_ni, d_no = depths
    reductions = []
    if fused:
        for depth, halves in ((d_ni + d_no, 2), (d_ei, 2), (d_eo + PACK, 1)):
            reductions += reduction_scratch(zs, depth)
            n_copies += zs + 3 * halves + zs - 1 + 3
        summed_shapes = [
            jax.ShapeDtypeStruct((4, depth, LANES), BF)
            for depth in (d_ni + d_no, d_ei, d_eo + PACK)
        ]
    else:
        summed_shapes = [jax.ShapeDtypeStruct((w.shape[0], width), F32) for w in weights]
        summed_shapes += [jax.ShapeDtypeStruct((PACK, width), F32)]
    scratch += [pltpu.SemaphoreType.DMA((n_copies,)), pltpu.SemaphoreType.DMA((n_copies,))]
    scratch += reductions

    vmem = pl.BlockSpec(memory_space=pltpu.VMEM)
    anywhere = pl.BlockSpec(memory_space=pl.ANY)
    sizes = (n_group, n_patch, padded, tile, senders.shape[1], fused, depths)
    edge_grad, node_grad, *sums = pl.pallas_call(
        functools.partial(kernel, sizes),
        out_shape=[
            jax.ShapeDtypeStruct((edges, width), BF),
            jax.ShapeDtypeStruct((nodes, width), BF),
        ]
        + summed_shapes,
        in_specs=[anywhere] * len(operands),
        out_specs=[anywhere] * 2 + [vmem] * len(summed_shapes),
        scratch_shapes=scratch,
        compiler_params=pltpu.CompilerParams(
            collective_id=0, has_side_effects=True, vmem_limit_bytes=63 * 1024 * 1024
        ),
    )(*operands)
    if fused:
        piece = width // n_patch
        rows_out = [jax.ShapeDtypeStruct((depth, width), F32) for depth in depths]
        gain_out = jax.ShapeDtypeStruct((1, piece), F32)
        o_ei, o_eo, o_ni, o_no = rows_out
        edge_grad, node_grad, o_ei, o_eo, gain_e, o_ni, o_no, gain_n = pl.pallas_call(
            functools.partial(closing, factor, depths),
            out_shape=[
                jax.ShapeDtypeStruct((edges, width), BF),
                jax.ShapeDtypeStruct((nodes, width), BF),
                o_ei,
                o_eo,
                gain_out,
                o_ni,
                o_no,
                gain_out,
            ],
            in_specs=[anywhere] * 2 + [vmem] * 3,
            out_specs=[anywhere] * 2 + [vmem] * 6,
            scratch_shapes=[
                pltpu.VMEM((edges, width), BF),
                pltpu.VMEM((nodes, width), BF),
                pltpu.SemaphoreType.DMA((2,)),
                pltpu.SemaphoreType.DMA((2,)),
            ],
            compiler_params=pltpu.CompilerParams(vmem_limit_bytes=16 * 1024 * 1024),
        )(edge_grad, node_grad, *sums)
        return (
            edge_grad[None],
            node_grad[None],
            o_ei,
            o_eo,
            gain_e.reshape(piece),
            o_ni,
            o_no,
            gain_n.reshape(piece),
        )
    p_ei, p_eo, p_ni, p_no, p_gain = sums

    def summed(value):
        part = lax.psum_scatter(value, "patch", scatter_dimension=0, tiled=True)
        return lax.psum(part.astype(BF), "group").astype(F32) * factor

    return (
        edge_grad[None],
        node_grad[None],
        summed(p_ei),
        summed(p_eo),
        summed(p_gain[0]),
        summed(p_ni),
        summed(p_no),
        summed(p_gain[1]),
    )


def solution(mesh):
    member = P("group", "patch", None)
    placed = (member,) * 4 + (P(),) * 6
    placed += (P("patch", None), P("patch", None), P("patch"), P("patch", None))
    rows = P("patch", None)
    return jax.shard_map(
        functools.partial(local, mesh.shape["group"], mesh.shape["patch"]),
        mesh=mesh,
        in_specs=placed,
        out_specs=(member, member, rows, rows, P("patch"), rows, rows, P("patch")),
        check_vma=False,
    )
```

```python
import functools

import jax
import jax.numpy as jnp
from jax import lax
from jax.experimental import pallas as pl
from jax.experimental.pallas import tpu as pltpu
from jax.sharding import PartitionSpec as P

epsilon = 1e-05
BF = jnp.bfloat16
F32 = jnp.float32
LANES = 128
PACK = 16
MESH = pl.DeviceIdType.MESH


def dot(left, right):
    return jnp.dot(left, right, preferred_element_type=F32)


def dot_rt(left, right):
    return lax.dot_general(left, right, (((1,), (1,)), ((), ())), preferred_element_type=F32)


def dot_lt(left, right):
    return lax.dot_general(left, right, (((0,), (0,)), ((), ())), preferred_element_type=F32)


def silu_pair(values):
    squash = 0.5 * jnp.tanh(0.5 * values) + 0.5
    active = values * squash
    return (active, squash + active * (1.0 - squash))


def normalize(values):
    centred = values - jnp.mean(values, axis=1, keepdims=True)
    inverse = lax.rsqrt(jnp.mean(centred * centred, axis=1, keepdims=True) + epsilon)
    return (centred * inverse, inverse)


def normalize_back(upstream, normed, inverse):
    return inverse * (
        upstream
        - jnp.mean(upstream, axis=1, keepdims=True)
        - normed * jnp.mean(upstream * normed, axis=1, keepdims=True)
    )


def hot(index, shape, axis, base):
    return jnp.where(lax.broadcasted_iota(jnp.int32, shape, axis) + base == index, 1.0, 0.0).astype(
        BF
    )


class Copies:
    def __init__(self, send_sems, recv_sems):
        self.send_sems, self.recv_sems, self.used = send_sems, recv_sems, 0

    def start(self, source, target, device):
        copy = pltpu.make_async_remote_copy(
            src_ref=source,
            dst_ref=target,
            send_sem=self.send_sems.at[self.used],
            recv_sem=self.recv_sems.at[self.used],
            device_id=device,
            device_id_type=MESH,
        )
        self.used += 1
        copy.start()
        return copy


def wait_all(copies):
    for copy in copies:
        copy.wait()


def staggered(count, stages, hooks=None, unrolled=True):
    if not unrolled:

        @pl.loop(0, count)
        def _(k):
            held = None
            for stage in stages:
                held = stage(k, held)

        return
    held = {}
    for step in range(count + len(stages) - 1):
        for order in range(len(stages)):
            k = step - order
            if 0 <= k < count:
                held[k] = stages[order](k, held.get(k))
        if hooks and step in hooks:
            hooks[step]()


def flipped(index, bits):
    for place in range(bits.bit_length()):
        if bits >> place & 1:
            index = index + (1 - 2 * lax.rem(lax.div(index, 1 << place), 2)) * (1 << place)
    return index


class Place:
    def __init__(self, n_patch):
        self.gi = lax.axis_index("group")
        self.p = lax.axis_index("patch")
        self.core = lax.rem(self.p, 2)
        self.z = lax.div(self.p, 2)
        self.zs = n_patch // 2
        self.partner = {"group": self.gi, "patch": self.p + 1 - 2 * self.core}
        self.gx, self.gy = lax.rem(self.gi, 2), lax.div(self.gi, 2)
        flip_x, flip_y = 1 - 2 * self.gx, 2 - 4 * self.gy
        self.members = [
            {"group": self.gi + flip, "patch": self.p} for flip in (flip_x, flip_y, flip_x + flip_y)
        ]
        self.x_peer, self.y_peer = self.members[:2]


class Reduction:
    def __init__(self, copies, refs, place):
        self.copies, self.place = copies, place
        self.g, self.rc, self.a, self.r1x, self.r1y, self.b0, self.b1 = refs[:7]
        self.r2x, self.r2y, self.c, self.r3, self.f = refs[7:]
        depth, middle = self.c.shape[1], self.r1x.shape[2]
        self.low, self.high = pl.ds(0, middle), pl.ds(middle, depth - middle)
        self.pairs, self.first, self.second = [], {}, []

    def put(self, k, row, size, value):
        value = value.astype(BF)
        for c in range(2):
            for quarter in range(4):
                self.g[c, k, quarter // 2, quarter % 2, row : row + size, :] = value[
                    c * size : (c + 1) * size, quarter * LANES : (quarter + 1) * LANES
                ]

    def pair(self, k):
        here = self.place
        self.pairs.append(
            self.copies.start(self.g.at[1 - here.core, k], self.rc.at[k], here.partner)
        )

    def step1(self, first, last):
        here = self.place
        for k in range(first, last):
            self.pairs[k].wait()
            for gy in range(2):
                for gx in range(2):
                    self.a[gy, gx, k] = (
                        self.g[here.core, k, gy, gx].astype(F32) + self.rc[k, gy, gx].astype(F32)
                    ).astype(BF)
        span = pl.ds(first, last - first)
        self.first[first] = [
            self.copies.start(
                self.a.at[:, 1 - here.gx, span, self.low], self.r1x.at[:, span], here.x_peer
            ),
            self.copies.start(
                self.a.at[1 - here.gy, :, span, self.high], self.r1y.at[:, span], here.y_peer
            ),
        ]

    def step2(self, first, last):
        here = self.place
        wait_all(self.first[first])
        for k in range(first, last):
            self.b0[k] = (
                self.a[1 - here.gy, here.gx, k, self.low].astype(F32)
                + self.r1x[1 - here.gy, k].astype(F32)
            ).astype(BF)
            self.b1[k] = (
                self.a[here.gy, 1 - here.gx, k, self.high].astype(F32)
                + self.r1y[1 - here.gx, k].astype(F32)
            ).astype(BF)
        span = pl.ds(first, last - first)
        self.second += [
            self.copies.start(self.b0.at[span], self.r2y.at[span], here.y_peer),
            self.copies.start(self.b1.at[span], self.r2x.at[span], here.x_peer),
        ]

    def along(self):
        here = self.place
        wait_all(self.second)
        for k in range(here.zs):
            self.c[k, self.low] = (
                self.a[here.gy, here.gx, k, self.low].astype(F32)
                + self.r1x[here.gy, k].astype(F32)
                + self.r2y[k].astype(F32)
            ).astype(BF)
            self.c[k, self.high] = (
                self.a[here.gy, here.gx, k, self.high].astype(F32)
                + self.r1y[here.gx, k].astype(F32)
                + self.r2x[k].astype(F32)
            ).astype(BF)
        self.moves = []
        for step in range(1, here.zs):
            there = lax.rem(here.z + step, here.zs)
            self.moves.append(
                self.copies.start(
                    self.c.at[there],
                    self.r3.at[step - 1],
                    {"group": here.gi, "patch": there * 2 + here.core},
                )
            )

    def share(self):
        here = self.place
        wait_all(self.moves)
        total = self.c[here.z].astype(F32)
        for step in range(1, here.zs):
            total += self.r3[step - 1].astype(F32)
        self.f[here.gi] = total.astype(BF)
        mine = self.f.at[here.gi]
        self.moves = [self.copies.start(mine, mine, member) for member in here.members]

    def finish(self, out):
        wait_all(self.moves)
        out[...] = self.f[...]


COUNT_SHARES = 12


def kernel(sizes, *refs):
    n_group, n_patch, padded, tile, tile_edges, fused, depths = sizes
    refs = list(refs)

    def take(count):
        got = refs[:count]
        del refs[:count]
        return got

    stored = take(14)
    edge_out, node_out = take(2)
    sums = take(3 if fused else 5)
    loaded = take(14)
    node, list_in, send_tiles, recv_tiles, edge, w_ei, w_eo, gain_e = loaded[:8]
    w_ni, w_no, gain_n, node_cot, edge_cot, count = loaded[8:]
    edge_grad, node_grad = (edge_out, node_out) if fused else take(2)
    load_sems, store_sems = take(2)
    send_col, send_row, recv_col, recv_row, list_col, list_row = take(6)
    outgoing, incoming, spread, returned = take(4)
    x_s, x_r, e_first, hidden, normed, inverse, message, joined = take(8)
    n_hidden, n_first, g_second, g_first, acc, gj, ge_second, ge_first, gs, gr, gains = take(11)
    send_sems, recv_sems = take(2)
    nodes, width = node.shape
    edges = edge.shape[0]
    halo = n_patch * padded
    place = Place(n_patch)
    gi, p = place.gi, place.p
    copies = Copies(send_sems, recv_sems)
    barrier = pltpu.get_barrier_semaphore()
    if fused and n_patch & (n_patch - 1) == 0:
        others = [flipped(p, d) for d in range(n_patch - 1, 0, -1)]
    else:
        others = [lax.rem(p + d, n_patch) for d in range(1, n_patch)]
    peers = [{"group": gi, "patch": other} for other in others]
    greeted = list(peers)
    if fused:
        greeted += place.members
    for peer in greeted:
        pl.semaphore_signal(barrier, inc=1, device_id=peer, device_id_type=MESH)
    loads = [
        pltpu.make_async_copy(source, target, load_sems.at[order])
        for order, (source, target) in enumerate(zip(stored, loaded))
    ]
    for load in loads:
        load.start()

    def column_of(line, column):
        for order in range(column.shape[0] // LANES):
            span = slice(order * LANES, (order + 1) * LANES)
            wide = jnp.broadcast_to(line[:, span].astype(F32), (8, LANES))
            column[span, :] = jnp.transpose(wide)[:, :1].astype(jnp.int32)

    loads[1].wait()
    list_row[...] = list_in[...]
    column_of(list_row, list_col)
    loads[0].wait()
    chosen = dot(hot(list_col[:halo, :], (halo, nodes), 1, 0), node[...]).astype(BF)
    outgoing[...] = chosen.reshape(n_patch, padded, width)
    pl.semaphore_wait(barrier, len(greeted))
    moving = [
        copies.start(outgoing.at[other], incoming.at[p], peer)
        for other, peer in zip(others, peers)
    ]
    incoming[p] = outgoing[p]
    gains[...] = jnp.zeros_like(gains)

    loads[2].wait()
    loads[3].wait()
    for tiles, column, line in ((send_tiles, send_col, send_row), (recv_tiles, recv_col, recv_row)):
        turned = jnp.transpose(tiles[...].astype(F32)).astype(jnp.int32)
        for order in range(line.shape[1] // LANES):
            span = slice(order * LANES, (order + 1) * LANES)
            column[span, :] = turned[:, order : order + 1]
            line[:, span] = tiles[order : order + 1, :]

    loads[4].wait()
    loads[5].wait()

    def rows_of(k, size=tile):
        return pl.ds(k * size if isinstance(k, int) else pl.multiple_of(k * size, size), size)

    long = 2 * tile if fused and edges % (2 * tile) == 0 and nodes % (2 * tile) == 0 else tile

    edge_tiles, node_tiles = edges // tile, nodes // tile

    @pl.loop(0, edges // long, unroll=fused)
    def _(k):
        rows = rows_of(k, long)
        latent = dot(hot(recv_col[rows, :], (long, nodes), 1, 0), node[...]).astype(BF)
        x_r[rows, :] = latent
        e_first[rows, :] = dot(edge[rows, :], w_ei[:width, :]) + dot(latent, w_ei[2 * width :, :])


    @pl.loop(0, edges // long, unroll=fused)
    def _(k):
        rows = rows_of(k, long)
        x_s[rows, :] = dot(hot(send_col[rows, :], (long, nodes), 1, 0), node[...]).astype(BF)

    loads[8].wait()

    @pl.loop(0, nodes // long, unroll=fused)
    def _(k):
        rows = rows_of(k, long)
        n_first[rows, :] = dot(node[rows, :], w_ni[:width, :])

    for load in loads[6:8] + loads[9:]:
        load.wait()
    wait_all(moving)

    def live_of(k, size=tile):
        slot = lax.broadcasted_iota(jnp.int32, (size, 1), 0) + k * size
        return jnp.where(slot < count[...] * tile_edges, 1.0, 0.0)


    def edge_first(k, _):
        rows = rows_of(k)
        latent = dot(
            hot(send_col[rows, :], (tile, halo), 1, nodes), incoming[...].reshape(halo, width)
        )
        latent = x_s[rows, :] + latent.astype(BF)
        x_s[rows, :] = latent
        return e_first[rows, :] + dot(latent, w_ei[width : 2 * width, :])

    def edge_hidden(k, first):
        rows = rows_of(k)
        active, slope = silu_pair(first)
        e_first[rows, :] = slope
        hid = active.astype(BF)
        hidden[rows, :] = hid
        return dot(hid, w_eo[...])

    def edge_message(k, second):
        rows = rows_of(k)
        norm, inv = normalize(second)
        normed[rows, :] = norm
        inverse[rows, :] = inv
        message[rows, :] = (live_of(k) * (gain_e[...] * norm)).astype(BF)

    staggered(edge_tiles, (edge_first, edge_hidden, edge_message), unrolled=fused)

    def node_first(k, _):
        rows = rows_of(k)
        got = dot(hot(recv_row[...], (tile, edges), 0, k * tile), message[...]).astype(BF)
        joined[rows, :] = got
        return n_first[rows, :] + dot(got, w_ni[width:, :])

    def node_hidden(k, first):
        rows = rows_of(k)
        active, slope = silu_pair(first)
        hid = active.astype(BF)
        n_hidden[rows, :] = hid
        return (slope, dot(hid, w_no[...]))

    def node_second(k, held):
        slope, second = held
        rows = rows_of(k)
        norm, inv = normalize(second)
        up = node_cot[rows, :].astype(F32)
        gains[1:2, :] += jnp.sum(up * norm, axis=0, keepdims=True)
        second = normalize_back(up * gain_n[...], norm, inv).astype(BF)
        g_second[rows, :] = second
        return (slope, dot_rt(second, w_no[...]))

    def node_back(k, held):
        slope, grad = held
        rows = rows_of(k)
        grad = (grad * slope).astype(BF)
        g_first[rows, :] = grad
        acc[rows, :] = node_cot[rows, :].astype(F32) + dot_rt(grad, w_ni[:width, :])
        gj[rows, :] = dot_rt(grad, w_ni[width:, :]).astype(BF)

    staggered(node_tiles, (node_first, node_hidden, node_second, node_back), unrolled=fused)

    def edge_taken(k, _):
        return dot(hot(recv_col[rows_of(k), :], (tile, nodes), 1, 0), gj[...])

    def edge_second(k, taken):
        rows = rows_of(k)
        norm = normed[rows, :]
        grad = live_of(k) * (edge_cot[rows, :].astype(F32) + taken)
        gains[0:1, :] += jnp.sum(grad * norm, axis=0, keepdims=True)
        second = normalize_back(grad * gain_e[...], norm, inverse[rows, :]).astype(BF)
        ge_second[rows, :] = second
        return dot_rt(second, w_eo[...])

    def edge_back(k, grad):
        rows = rows_of(k)
        ge_first[rows, :] = (grad * e_first[rows, :]).astype(BF)

    edge_stages = (edge_taken, edge_second, edge_back)

    def rows_product(sources, start, stop, right):
        parts = []
        for order, source in enumerate(sources):
            low = max(start, order * width) - order * width
            high = min(stop, (order + 1) * width) - order * width
            if low < high:
                parts.append(dot_lt(source[:, low:high], right))
        return parts[0] if len(parts) == 1 else jnp.concatenate(parts, axis=0)

    if fused:
        zs = place.zs
        half = zs // 2
        d_ei, d_eo, d_ni, d_no = depths
        red_n = Reduction(copies, take(COUNT_SHARES), place)
        red_e = Reduction(copies, take(COUNT_SHARES), place)
        red_o = Reduction(copies, take(COUNT_SHARES), place)
        for first in (0, half):
            for k in range(first, first + half):
                start = 2 * k * d_ni
                value = rows_product((node, joined), start, start + 2 * d_ni, g_first[...])
                red_n.put(k, 0, d_ni, value)
                value = dot_lt(n_hidden[:, 2 * k * d_no : 2 * (k + 1) * d_no], g_second[...])
                red_n.put(k, d_ni, d_no, value)
            for k in range(first, first + half):
                red_n.pair(k)
        red_n.step1(0, half)
        staggered(edge_tiles, edge_stages, hooks={2: lambda: red_n.step1(half, zs)})
        for first in (0, half):
            for k in range(first, first + half):
                start = 2 * k * d_ei
                value = rows_product((edge, x_s, x_r), start, start + 2 * d_ei, ge_first[...])
                red_e.put(k, 0, d_ei, value)
            for k in range(first, first + half):
                red_e.pair(k)
            if first == 0:
                red_n.step2(0, half)
        red_e.step1(0, half)
        red_n.step2(half, zs)
        total = gains[...].astype(BF)
        total = jnp.concatenate([total, total], axis=0)
        for k in range(zs):
            red_o.put(
                k, 0, d_eo, dot_lt(hidden[:, 2 * k * d_eo : 2 * (k + 1) * d_eo], ge_second[...])
            )
            red_o.put(k, d_eo, PACK, total)
        for k in range(zs):
            red_o.pair(k)
        red_e.step1(half, zs)
    else:
        o_ei, o_eo, o_ni, o_no, o_gain = sums
        o_ni[:width, :] = dot_lt(node[...], g_first[...])
        o_ni[width:, :] = dot_lt(joined[...], g_first[...])
        o_no[...] = dot_lt(n_hidden[...], g_second[...])
        staggered(edge_tiles, edge_stages, unrolled=False)
        o_ei[:width, :] = dot_lt(edge[...], ge_first[...])
        o_ei[width : 2 * width, :] = dot_lt(x_s[...], ge_first[...])
        o_ei[2 * width :, :] = dot_lt(x_r[...], ge_first[...])
        o_eo[...] = dot_lt(hidden[...], ge_second[...])
        o_gain[...] = gains[...]

    @pl.loop(0, edges // long, unroll=fused)
    def _(k):
        rows = rows_of(k, long)
        gs[rows, :] = dot_rt(ge_first[rows, :], w_ei[width : 2 * width, :]).astype(BF)

    back = dot(hot(send_row[...], (halo, edges), 0, nodes), gs[...]).astype(BF)
    spread[...] = back.reshape(n_patch, padded, width)
    moving = [
        copies.start(spread.at[other], returned.at[p], peer)
        for other, peer in zip(others, peers)
    ]
    returned[p] = spread[p]
    if fused:
        red_o.step1(0, zs)

    @pl.loop(0, edges // long, unroll=fused)
    def _(k):
        rows = rows_of(k, long)
        gr[rows, :] = dot_rt(ge_first[rows, :], w_ei[2 * width :, :]).astype(BF)

    if fused:
        red_n.along()

    @pl.loop(0, edges // long, unroll=fused)
    def _(k):
        rows = rows_of(k, long)
        edge_grad[rows, :] = (
            live_of(k, long) * edge_cot[rows, :].astype(F32)
            + dot_rt(ge_first[rows, :], w_ei[:width, :])
        ).astype(BF)

    stores = []
    if not fused:
        stores.append(pltpu.make_async_copy(edge_grad, edge_out, store_sems.at[0]))
        stores[0].start()

    def gather_back(k):
        rows = rows_of(k, long)
        acc[rows, :] += dot(hot(send_row[...], (long, edges), 0, k * long), gs[...]) + dot(
            hot(recv_row[...], (long, edges), 0, k * long), gr[...]
        )

    if fused:
        red_e.step2(0, half)
    gathers = nodes // long
    pl.loop(0, gathers // 2, unroll=fused)(gather_back)
    if fused:
        red_e.step2(half, zs)
        red_o.step2(0, zs)
    pl.loop(gathers // 2, gathers, unroll=fused)(gather_back)
    if fused:
        red_e.along()
        red_o.along()
        red_n.share()
    wait_all(moving)

    @pl.loop(0, node_tiles, unroll=fused)
    def _(k):
        rows = rows_of(k)
        node_grad[rows, :] = (
            acc[rows, :]
            + dot(
                hot(list_row[:, :halo], (tile, halo), 0, k * tile),
                returned[...].reshape(halo, width),
            )
        ).astype(BF)

    if not fused:
        stores.append(pltpu.make_async_copy(node_grad, node_out, store_sems.at[1]))
        stores[1].start()
    if fused:
        red_e.share()
        red_o.share()
        red_n.finish(sums[0])
        red_e.finish(sums[1])
        red_o.finish(sums[2])
    for store in stores:
        store.wait()


def closing(factor, depths, *refs):
    edge_in, node_in, sum_n, sum_e, sum_o = refs[:5]
    outs = refs[5:13]
    holds, store_sems = refs[13:19], refs[19]
    o_ei, o_eo, o_gain_e, o_ni, o_no, o_gain_n = holds
    d_ei, d_eo, d_ni, d_no = depths
    stores = [
        pltpu.make_async_copy(source, out, store_sems.at[order])
        for order, (source, out) in enumerate(zip((edge_in, node_in) + tuple(holds), outs))
    ]
    stores[0].start()
    stores[1].start()
    for quarter in range(4):
        span = slice(quarter * LANES, (quarter + 1) * LANES)
        o_ei[:, span] = sum_e[quarter].astype(F32) * factor
    stores[2].start()
    for quarter in range(4):
        span = slice(quarter * LANES, (quarter + 1) * LANES)
        o_ni[:, span] = sum_n[quarter, :d_ni].astype(F32) * factor
        o_no[:, span] = sum_n[quarter, d_ni:].astype(F32) * factor
        o_eo[:, span] = sum_o[quarter, :d_eo].astype(F32) * factor
    for order in (3, 5, 6):
        stores[order].start()
    piece = o_gain_e.shape[1]
    p = lax.axis_index("patch")
    own = jnp.zeros((PACK, piece), F32)
    for quarter in range(4):
        lane = lax.broadcasted_iota(jnp.int32, (LANES, piece), 0) + quarter * LANES
        want = lax.broadcasted_iota(jnp.int32, (LANES, piece), 1) + p * piece
        pick = jnp.where(lane == want, 1.0, 0.0).astype(BF)
        own += dot(sum_o[quarter, d_eo:], pick)
    o_gain_e[...] = own[0:1] * factor
    o_gain_n[...] = own[1:2] * factor
    for order in (4, 7):
        stores[order].start()
    for store in stores:
        store.wait()


def reduction_scratch(zs, depth):
    middle = depth // 2 // PACK * PACK
    rest = depth - middle
    shapes = (
        (2, zs, 2, 2, depth),
        (zs, 2, 2, depth),
        (2, 2, zs, depth),
        (2, zs, middle),
        (2, zs, rest),
        (zs, middle),
        (zs, rest),
        (zs, rest),
        (zs, middle),
        (zs, depth),
        (zs - 1, depth),
        (4, depth),
    )
    return [pltpu.VMEM(shape + (LANES,), BF) for shape in shapes]


def local(
    n_group,
    n_patch,
    node_tape,
    edge_tape,
    node_cot,
    edge_cot,
    w_edge_in,
    w_edge_out,
    gain_edge,
    w_node_in,
    w_node_out,
    gain_node,
    senders,
    receivers,
    tile_count,
    send_rows,
):
    nodes, width = node_tape.shape[1:]
    edges = edge_tape.shape[1]
    listed = send_rows.shape[1]
    peer_rows = listed // n_patch
    padded = -(-peer_rows // PACK) * PACK
    halo = n_patch * padded
    tile = min(2 * LANES, nodes, edges)
    factor = float(n_group * n_patch * edges) ** (-0.5)

    if padded != peer_rows:
        beyond = senders - nodes
        beyond = beyond // peer_rows * padded + beyond % peer_rows
        senders = jnp.where(senders < nodes, senders, nodes + beyond)
        send_rows = jnp.pad(
            send_rows.reshape(n_patch, peer_rows),
            ((0, 0), (0, padded - peer_rows)),
            constant_values=-1,
        ).reshape(1, halo)
    slots = -(-halo // LANES) * LANES
    if slots != halo:
        send_rows = jnp.pad(send_rows, ((0, 0), (0, slots - halo)), constant_values=-1)

    def lane_rows(index):
        rows = -(-index.size // LANES)
        full = -(-rows // 8) * 8
        if index.shape == (full, LANES):
            return index
        return jnp.pad(index.reshape(-1), (0, full * LANES - index.size)).reshape(full, LANES)

    weights = (w_edge_in, w_edge_out, w_node_in, w_node_out)
    depths = [w.shape[0] // n_patch for w in weights]
    zs = n_patch // 2
    fused = (
        n_group == 4
        and n_patch % 4 == 0
        and width == 4 * LANES
        and all(d % PACK == 0 and 2 * d % LANES == 0 for d in depths)
    )
    operands = (
        node_tape[0],
        send_rows,
        lane_rows(senders),
        lane_rows(receivers),
        edge_tape[0],
        w_edge_in,
        w_edge_out,
        gain_edge[None],
        w_node_in,
        w_node_out,
        gain_node[None],
        node_cot[0],
        edge_cot[0],
        tile_count[None],
    )
    scratch = [pltpu.VMEM(operand.shape, operand.dtype) for operand in operands]
    if not fused:
        scratch += [pltpu.VMEM((edges, width), BF), pltpu.VMEM((nodes, width), BF)]
    scratch += [
        pltpu.SemaphoreType.DMA((len(operands),)),
        pltpu.SemaphoreType.DMA((2,)),
    ]
    for length in (edges, edges, slots):
        scratch += [pltpu.VMEM((length, 1), jnp.int32), pltpu.VMEM((1, length), jnp.int32)]
    scratch += [pltpu.VMEM((n_patch, padded, width), BF)] * 4
    by_edge, by_node = pltpu.VMEM((edges, width), BF), pltpu.VMEM((nodes, width), BF)
    wide_edge, wide_node = pltpu.VMEM((edges, width), F32), pltpu.VMEM((nodes, width), F32)
    scratch += [by_edge, by_edge, wide_edge, by_edge, wide_edge, pltpu.VMEM((edges, 1), F32)]
    scratch += [by_edge, by_node]
    scratch += [by_node, wide_node, by_node, by_node, wide_node, by_node]
    scratch += [by_edge, by_edge, by_edge, by_edge, pltpu.VMEM((PACK, width), F32)]
    n_copies = 2 * (n_patch - 1)
    d_ei, d_eo, d_ni, d_no = depths
    reductions = []
    if fused:
        for depth, halves in ((d_ni + d_no, 2), (d_ei, 2), (d_eo + PACK, 1)):
            reductions += reduction_scratch(zs, depth)
            n_copies += zs + 4 * halves + zs - 1 + 3
        summed_shapes = [
            pltpu.VMEM((4, depth, LANES), BF)
            for depth in (d_ni + d_no, d_ei, d_eo + PACK)
        ]
    else:
        summed_shapes = [jax.ShapeDtypeStruct((w.shape[0], width), F32) for w in weights]
        summed_shapes += [jax.ShapeDtypeStruct((PACK, width), F32)]
    scratch += [pltpu.SemaphoreType.DMA((n_copies,)), pltpu.SemaphoreType.DMA((n_copies,))]
    scratch += reductions

    vmem = pl.BlockSpec(memory_space=pltpu.VMEM)
    big = pltpu.VMEM if fused else jax.ShapeDtypeStruct
    anywhere = pl.BlockSpec(memory_space=pl.ANY)
    sizes = (n_group, n_patch, padded, tile, senders.shape[1], fused, depths)
    edge_grad, node_grad, *sums = pl.pallas_call(
        functools.partial(kernel, sizes),
        out_shape=[big((edges, width), BF), big((nodes, width), BF)] + summed_shapes,
        in_specs=[anywhere] * len(operands),
        out_specs=[vmem if fused else anywhere] * 2 + [vmem] * len(summed_shapes),
        scratch_shapes=scratch,
        compiler_params=pltpu.CompilerParams(
            collective_id=0, has_side_effects=True, vmem_limit_bytes=54 * 1024 * 1024
        ),
    )(*operands)
    if fused:
        piece = width // n_patch
        rows_out = [jax.ShapeDtypeStruct((depth, width), F32) for depth in depths]
        gain_out = jax.ShapeDtypeStruct((1, piece), F32)
        o_ei, o_eo, o_ni, o_no = rows_out
        edge_grad, node_grad, o_ei, o_eo, gain_e, o_ni, o_no, gain_n = pl.pallas_call(
            functools.partial(closing, factor, depths),
            out_shape=[
                jax.ShapeDtypeStruct((edges, width), BF),
                jax.ShapeDtypeStruct((nodes, width), BF),
                o_ei,
                o_eo,
                gain_out,
                o_ni,
                o_no,
                gain_out,
            ],
            in_specs=[vmem] * 5,
            out_specs=[anywhere] * 8,
            scratch_shapes=[
                pltpu.VMEM((d_ei, width), F32),
                pltpu.VMEM((d_eo, width), F32),
                pltpu.VMEM((1, piece), F32),
                pltpu.VMEM((d_ni, width), F32),
                pltpu.VMEM((d_no, width), F32),
                pltpu.VMEM((1, piece), F32),
                pltpu.SemaphoreType.DMA((8,)),
            ],
            compiler_params=pltpu.CompilerParams(vmem_limit_bytes=16 * 1024 * 1024),
        )(*[pltpu.with_memory_space_constraint(x, pltpu.VMEM) for x in (edge_grad, node_grad, *sums)])
        return (
            edge_grad[None],
            node_grad[None],
            o_ei,
            o_eo,
            gain_e.reshape(piece),
            o_ni,
            o_no,
            gain_n.reshape(piece),
        )
    p_ei, p_eo, p_ni, p_no, p_gain = sums

    def summed(value):
        part = lax.psum_scatter(value, "patch", scatter_dimension=0, tiled=True)
        return lax.psum(part.astype(BF), "group").astype(F32) * factor

    return (
        edge_grad[None],
        node_grad[None],
        summed(p_ei),
        summed(p_eo),
        summed(p_gain[0]),
        summed(p_ni),
        summed(p_no),
        summed(p_gain[1]),
    )


def solution(mesh):
    member = P("group", "patch", None)
    placed = (member,) * 4 + (P(),) * 6
    placed += (P("patch", None), P("patch", None), P("patch"), P("patch", None))
    rows = P("patch", None)
    return jax.shard_map(
        functools.partial(local, mesh.shape["group"], mesh.shape["patch"]),
        mesh=mesh,
        in_specs=placed,
        out_specs=(member, member, rows, rows, P("patch"), rows, rows, P("patch")),
        check_vma=False,
    )
```

```python
import functools

import jax
import jax.numpy as jnp
from jax import lax
from jax.experimental import pallas as pl
from jax.experimental.pallas import tpu as pltpu
from jax.sharding import PartitionSpec as P

epsilon = 1e-05
BF = jnp.bfloat16
F32 = jnp.float32
LANES = 128
PACK = 16
MESH = pl.DeviceIdType.MESH


def dot(left, right):
    return jnp.dot(left, right, preferred_element_type=F32)


def dot_rt(left, right):
    return lax.dot_general(left, right, (((1,), (1,)), ((), ())), preferred_element_type=F32)


def dot_lt(left, right):
    return lax.dot_general(left, right, (((0,), (0,)), ((), ())), preferred_element_type=F32)


def silu_pair(values):
    squash = 0.5 * jnp.tanh(0.5 * values) + 0.5
    active = values * squash
    return (active, squash + active * (1.0 - squash))


def normalize(values, live=None):
    centred = values - jnp.mean(values, axis=1, keepdims=True)
    inverse = lax.rsqrt(jnp.mean(centred * centred, axis=1, keepdims=True) + epsilon)
    if live is not None:
        inverse = inverse * live
    return (centred * inverse, inverse)


def normalize_back(upstream, normed, inverse):
    product = upstream * normed
    second = inverse * (
        upstream
        - jnp.mean(upstream, axis=1, keepdims=True)
        - normed * jnp.mean(product, axis=1, keepdims=True)
    )
    return (second.astype(BF), jnp.sum(product, axis=0, keepdims=True))


def hot(index, shape, axis, base):
    return jnp.where(lax.broadcasted_iota(jnp.int32, shape, axis) + base == index, 1.0, 0.0).astype(
        BF
    )


class Waited:
    def __init__(self, copies, copy, slot):
        self.copies, self.copy, self.slot = copies, copy, slot

    def wait(self):
        self.copy.wait()
        self.copies.free.append(self.slot)


class Copies:
    def __init__(self, send_sems, recv_sems):
        self.send_sems, self.recv_sems, self.used = send_sems, recv_sems, 0
        self.free = list(range(send_sems.shape[0]))

    def start(self, source, target, device):
        slot = self.free.pop(0)
        copy = pltpu.make_async_remote_copy(
            src_ref=source,
            dst_ref=target,
            send_sem=self.send_sems.at[slot],
            recv_sem=self.recv_sems.at[self.used],
            device_id=device,
            device_id_type=MESH,
        )
        self.used += 1
        copy.start()
        return Waited(self, copy, slot)


def wait_all(copies):
    for copy in copies:
        copy.wait()


def staggered(count, stages, hooks=None, unrolled=True):
    if not unrolled:

        @pl.loop(0, count)
        def _(k):
            held = None
            for stage in stages:
                held = stage(k, held)

        return
    held = {}
    for step in range(count + len(stages) - 1):
        for order in range(len(stages)):
            k = step - order
            if 0 <= k < count:
                held[k] = stages[order](k, held.get(k))
        if hooks and step in hooks:
            hooks[step]()


def flipped(index, bits):
    for place in range(bits.bit_length()):
        if bits >> place & 1:
            index = index + (1 - 2 * lax.rem(lax.div(index, 1 << place), 2)) * (1 << place)
    return index


class Place:
    def __init__(self, n_patch):
        self.gi = lax.axis_index("group")
        self.p = lax.axis_index("patch")
        self.core = lax.rem(self.p, 2)
        self.z = lax.div(self.p, 2)
        self.zs = n_patch // 2
        self.partner = {"group": self.gi, "patch": self.p + 1 - 2 * self.core}
        self.gx, self.gy = lax.rem(self.gi, 2), lax.div(self.gi, 2)
        flip_x, flip_y = 1 - 2 * self.gx, 2 - 4 * self.gy
        self.members = [
            {"group": self.gi + flip, "patch": self.p} for flip in (flip_x, flip_y, flip_x + flip_y)
        ]
        self.x_peer, self.y_peer = self.members[:2]


class Reduction:
    def __init__(self, copies, refs, place):
        self.copies, self.place = copies, place
        self.g, self.rc, self.sx, self.sy, self.ox, self.oy = refs[:6]
        self.r1x, self.r1y, self.b0, self.b1, self.r2x, self.r2y, self.c, self.r3, self.f = refs[6:]
        depth, middle = self.c.shape[1], self.sx.shape[2]
        self.low, self.high = pl.ds(0, middle), pl.ds(middle, depth - middle)
        self.pairs, self.first, self.second = {}, {}, []

    def put(self, first, last, row, size, value, skip=0):
        value = value.astype(BF)
        each = value.shape[0] // (2 * (last - first))
        for k in range(first, last):
            for c in range(2):
                start = (2 * (k - first) + c) * each + skip
                for quarter in range(4):
                    self.g[c, k, quarter // 2, quarter % 2, row : row + size, :] = value[
                        start : start + size, quarter * LANES : (quarter + 1) * LANES
                    ]

    def pair(self, first, last):
        here = self.place
        span = pl.ds(first, last - first)
        self.pairs[first] = self.copies.start(
            self.g.at[1 - here.core, span], self.rc.at[span], here.partner
        )

    def joint(self, k, gy, gx, rows):
        own = self.g[self.place.core, k, gy, gx, rows].astype(F32)
        return (own + self.rc[k, gy, gx, rows].astype(F32)).astype(BF)

    def step1(self, first, last):
        here = self.place
        for k in range(first, last):
            if k in self.pairs:
                self.pairs[k].wait()
            for other in range(2):
                self.sx[k, other] = self.joint(k, other, 1 - here.gx, self.low)
                self.sy[k, other] = self.joint(k, 1 - here.gy, other, self.high)
        span = pl.ds(first, last - first)
        self.first[first] = [
            self.copies.start(self.sx.at[span], self.r1x.at[span], here.x_peer),
            self.copies.start(self.sy.at[span], self.r1y.at[span], here.y_peer),
        ]
        for k in range(first, last):
            for other in range(2):
                self.ox[k, other] = self.joint(k, other, here.gx, self.low)
                self.oy[k, other] = self.joint(k, here.gy, other, self.high)

    def step2(self, first, last):
        here = self.place
        wait_all(self.first[first])
        for k in range(first, last):
            self.b0[k] = (
                self.ox[k, 1 - here.gy].astype(F32) + self.r1x[k, 1 - here.gy].astype(F32)
            ).astype(BF)
            self.b1[k] = (
                self.oy[k, 1 - here.gx].astype(F32) + self.r1y[k, 1 - here.gx].astype(F32)
            ).astype(BF)
        span = pl.ds(first, last - first)
        self.second += [
            self.copies.start(self.b0.at[span], self.r2y.at[span], here.y_peer),
            self.copies.start(self.b1.at[span], self.r2x.at[span], here.x_peer),
        ]

    def along(self):
        here = self.place
        wait_all(self.second)
        for k in range(here.zs):
            self.c[k, self.low] = (
                self.ox[k, here.gy].astype(F32)
                + self.r1x[k, here.gy].astype(F32)
                + self.r2y[k].astype(F32)
            ).astype(BF)
            self.c[k, self.high] = (
                self.oy[k, here.gx].astype(F32)
                + self.r1y[k, here.gx].astype(F32)
                + self.r2x[k].astype(F32)
            ).astype(BF)
        self.moves = []
        for step in range(here.zs - 1, 0, -1):
            there = flipped(here.z, step)
            self.moves.append(
                self.copies.start(
                    self.c.at[there],
                    self.r3.at[step - 1],
                    {"group": here.gi, "patch": there * 2 + here.core},
                )
            )

    def share(self):
        here = self.place
        wait_all(self.moves)
        total = self.c[here.z].astype(F32)
        for step in range(1, here.zs):
            total += self.r3[step - 1].astype(F32)
        self.f[here.gi] = total.astype(BF)
        mine = self.f.at[here.gi]
        self.moves = [self.copies.start(mine, mine, member) for member in here.members]

    def finish(self, out):
        wait_all(self.moves)
        out[...] = self.f[...]


COUNT_SHARES = 15


def kernel(sizes, *refs):
    n_group, n_patch, padded, tile, tile_edges, fused, depths = sizes
    refs = list(refs)

    def take(count):
        got = refs[:count]
        del refs[:count]
        return got

    stored = take(14)
    edge_out, node_out = take(2)
    sums = take(5)
    loaded = take(14)
    node, list_in, send_tiles, recv_tiles, edge, w_ei, w_eo, gain_e = loaded[:8]
    w_ni, w_no, gain_n, node_cot, edge_cot, count = loaded[8:]
    edge_grad, node_grad = (edge_out, node_out) if fused else take(2)
    load_sems, store_sems = take(2)
    send_col, send_row, recv_col, recv_row, list_col, list_row = take(6)
    outgoing, incoming, spread, returned = take(4)
    x_s, x_r, e_first, hidden, normed, inverse, message, joined = take(8)
    n_hidden, n_first, g_second, g_first, acc, gj, ge_second, ge_first, gs, gr, gains = take(11)
    recv_hot = take(1)[0] if fused else None
    send_sems, recv_sems = take(2)
    nodes, width = node.shape
    edges = edge.shape[0]
    halo = n_patch * padded
    place = Place(n_patch)
    gi, p = place.gi, place.p
    copies = Copies(send_sems, recv_sems)
    barrier = pltpu.get_barrier_semaphore()
    if fused:
        others = [flipped(p, d) for d in range(n_patch - 1, 0, -1)]
    else:
        others = [lax.rem(p + d, n_patch) for d in range(1, n_patch)]
    peers = [{"group": gi, "patch": other} for other in others]
    greeted = list(peers)
    if fused:
        greeted += place.members
    for peer in greeted:
        pl.semaphore_signal(barrier, inc=1, device_id=peer, device_id_type=MESH)
    loads = [
        pltpu.make_async_copy(source, target, load_sems.at[order])
        for order, (source, target) in enumerate(zip(stored, loaded))
    ]
    first = (1, 0, 2, 3) if fused else range(len(loads))
    for order in first:
        loads[order].start()

    def column_of(line, column):
        for order in range(column.shape[0] // LANES):
            span = slice(order * LANES, (order + 1) * LANES)
            wide = jnp.broadcast_to(line[:, span].astype(F32), (8, LANES))
            column[span, :] = jnp.transpose(wide)[:, :1].astype(jnp.int32)

    loads[1].wait()
    for order in range(len(loads)):
        if order not in first:
            loads[order].start()
    list_row[...] = list_in[...]
    column_of(list_row, list_col)
    loads[0].wait()
    chosen = dot(hot(list_col[:halo, :], (halo, nodes), 1, 0), node[...]).astype(BF)
    outgoing[...] = chosen.reshape(n_patch, padded, width)
    pl.semaphore_wait(barrier, len(greeted))
    moving = [
        copies.start(outgoing.at[other], incoming.at[p], peer)
        for other, peer in zip(others, peers)
    ]
    incoming[p] = outgoing[p]
    gains[...] = jnp.zeros_like(gains)

    loads[2].wait()
    loads[3].wait()
    for tiles, column, line in ((send_tiles, send_col, send_row), (recv_tiles, recv_col, recv_row)):
        turned = jnp.transpose(tiles[...].astype(F32)).astype(jnp.int32)
        for order in range(line.shape[1] // LANES):
            span = slice(order * LANES, (order + 1) * LANES)
            column[span, :] = turned[:, order : order + 1]
            line[:, span] = tiles[order : order + 1, :]

    loads[4].wait()
    loads[5].wait()

    def rows_of(k, size=tile):
        return pl.ds(k * size if isinstance(k, int) else pl.multiple_of(k * size, size), size)

    long = 2 * tile if fused and edges % (2 * tile) == 0 and nodes % (2 * tile) == 0 else tile

    edge_tiles, node_tiles = edges // tile, nodes // tile

    @pl.loop(0, edges // long, unroll=fused)
    def _(k):
        rows = rows_of(k, long)
        chosen = hot(recv_col[rows, :], (long, nodes), 1, 0)
        if fused:
            recv_hot[rows, :] = chosen
        latent = dot(chosen, node[...]).astype(BF)
        x_r[rows, :] = latent
        e_first[rows, :] = dot(edge[rows, :], w_ei[:width, :]) + dot(latent, w_ei[2 * width :, :])


    @pl.loop(0, edges // long, unroll=fused)
    def _(k):
        rows = rows_of(k, long)
        x_s[rows, :] = dot(hot(send_col[rows, :], (long, nodes), 1, 0), node[...]).astype(BF)

    loads[8].wait()

    @pl.loop(0, nodes // long, unroll=fused)
    def _(k):
        rows = rows_of(k, long)
        n_first[rows, :] = dot(node[rows, :], w_ni[:width, :])

    for load in loads[6:8] + loads[9:]:
        load.wait()
    wait_all(moving)

    def live_of(k, size=tile):
        slot = lax.broadcasted_iota(jnp.int32, (size, 1), 0) + k * size
        return jnp.where(slot < count[...] * tile_edges, 1.0, 0.0)


    def edge_first(k, _):
        rows = rows_of(k)
        latent = dot(
            hot(send_col[rows, :], (tile, halo), 1, nodes), incoming[...].reshape(halo, width)
        )
        latent = x_s[rows, :] + latent.astype(BF)
        x_s[rows, :] = latent
        return e_first[rows, :] + dot(latent, w_ei[width : 2 * width, :])

    def edge_hidden(k, first):
        rows = rows_of(k)
        active, slope = silu_pair(first)
        e_first[rows, :] = slope
        hid = active.astype(BF)
        hidden[rows, :] = hid
        return dot(hid, w_eo[...])

    def edge_message(k, second):
        rows = rows_of(k)
        norm, inv = normalize(second, live_of(k))
        normed[rows, :] = norm
        inverse[rows, :] = inv
        message[rows, :] = (gain_e[...] * norm).astype(BF)

    staggered(edge_tiles, (edge_first, edge_hidden, edge_message), unrolled=fused)

    def node_first(k, _):
        rows = rows_of(k)
        got = dot(hot(recv_row[...], (tile, edges), 0, k * tile), message[...]).astype(BF)
        joined[rows, :] = got
        return n_first[rows, :] + dot(got, w_ni[width:, :])

    def node_hidden(k, first):
        rows = rows_of(k)
        active, slope = silu_pair(first)
        hid = active.astype(BF)
        n_hidden[rows, :] = hid
        return (slope, dot(hid, w_no[...]))

    def node_second(k, held):
        slope, second = held
        rows = rows_of(k)
        norm, inv = normalize(second)
        up = node_cot[rows, :].astype(F32)
        second, total = normalize_back(up * gain_n[...], norm, inv)
        gains[1:2, :] += total
        g_second[rows, :] = second
        return (slope, dot_rt(second, w_no[...]))

    def node_back(k, held):
        slope, grad = held
        g_first[rows_of(k), :] = (grad * slope).astype(BF)

    staggered(node_tiles, (node_first, node_hidden, node_second, node_back), unrolled=fused)

    def node_message():
        @pl.loop(0, nodes // long, unroll=fused)
        def _(k):
            rows = rows_of(k, long)
            gj[rows, :] = dot_rt(g_first[rows, :], w_ni[width:, :]).astype(BF)

    def edge_taken(k, _):
        if fused:
            return dot(recv_hot[rows_of(k), :], gj[...])
        return dot(hot(recv_col[rows_of(k), :], (tile, nodes), 1, 0), gj[...])

    def edge_second(k, taken):
        rows = rows_of(k)
        norm = normed[rows, :]
        grad = edge_cot[rows, :].astype(F32) + taken
        second, total = normalize_back(grad * gain_e[...], norm, inverse[rows, :])
        gains[0:1, :] += total
        ge_second[rows, :] = second
        return dot_rt(second, w_eo[...])

    def edge_back(k, grad):
        rows = rows_of(k)
        ge_first[rows, :] = (grad * e_first[rows, :]).astype(BF)

    edge_stages = (edge_taken, edge_second, edge_back)
    moving = []

    def send_back():
        @pl.loop(0, edges // long, unroll=fused)
        def _(k):
            rows = rows_of(k, long)
            gs[rows, :] = dot_rt(ge_first[rows, :], w_ei[width : 2 * width, :]).astype(BF)

        back = dot(hot(send_row[...], (halo, edges), 0, nodes), gs[...]).astype(BF)
        spread[...] = back.reshape(n_patch, padded, width)
        moving.extend(
            copies.start(spread.at[other], returned.at[p], peer)
            for other, peer in zip(others, peers)
        )
        returned[p] = spread[p]

    def rows_product(sources, start, stop, right):
        parts = []
        for order, source in enumerate(sources):
            low = max(start, order * width) - order * width
            high = min(stop, (order + 1) * width) - order * width
            if low < high:
                parts.append(dot_lt(source[:, low:high], right))
        return parts[0] if len(parts) == 1 else jnp.concatenate(parts, axis=0)

    if fused:
        zs = place.zs
        half = zs // 2
        d_ei, d_eo, d_ni, d_no = depths
        red_no, red_ni, red_ea, red_eb, red_o = [
            Reduction(copies, take(COUNT_SHARES), place) for _ in range(5)
        ]
        d_ea = d_ei // 2 // PACK * PACK
        red_no.put(0, zs, 0, d_no, dot_lt(n_hidden[...], g_second[...]))
        red_no.pair(0, zs)
        for first in (0, half):
            last = first + half
            value = rows_product((node, joined), 2 * first * d_ni, 2 * last * d_ni, g_first[...])
            red_ni.put(first, last, 0, d_ni, value)
            red_ni.pair(first, last)
            if first == 0:
                red_no.step1(0, zs)
        node_message()
        red_ni.step1(0, half)
        staggered(edge_tiles, edge_stages, hooks={2: lambda: red_ni.step1(half, zs)})
        red_no.step2(0, zs)
        gains[0:1, :] = gains[0:1, :] / gain_e[...]
        gains[1:2, :] = gains[1:2, :] / gain_n[...]
        total = gains[...].astype(BF)
        red_o.put(0, zs, 0, d_eo, dot_lt(hidden[...], ge_second[...]))
        red_o.put(0, zs, d_eo, PACK, jnp.concatenate([total] * (2 * zs), axis=0))
        red_o.pair(0, zs)
        red_ni.step2(0, half)
        for first in (0, half):
            last = first + half
            value = rows_product(
                (edge, x_s, x_r), 2 * first * d_ei, 2 * last * d_ei, ge_first[...]
            )
            red_ea.put(first, last, 0, d_ea, value)
            red_eb.put(first, last, 0, d_ei - d_ea, value, skip=d_ea)
            red_ea.pair(first, last)
            red_eb.pair(first, last)
        red_o.step1(0, zs)
        red_ni.step2(half, zs)
        send_back()
        red_ea.step1(0, zs)
        red_eb.step1(0, zs)
    else:
        o_ei, o_eo, o_ni, o_no, o_gain = sums
        o_ni[:width, :] = dot_lt(node[...], g_first[...])
        o_ni[width:, :] = dot_lt(joined[...], g_first[...])
        o_no[...] = dot_lt(n_hidden[...], g_second[...])
        node_message()
        staggered(edge_tiles, edge_stages, unrolled=False)
        o_ei[:width, :] = dot_lt(edge[...], ge_first[...])
        o_ei[width : 2 * width, :] = dot_lt(x_s[...], ge_first[...])
        o_ei[2 * width :, :] = dot_lt(x_r[...], ge_first[...])
        o_eo[...] = dot_lt(hidden[...], ge_second[...])
        o_gain[...] = gains[...]
        o_gain[0:1, :] = gains[0:1, :] / gain_e[...]
        o_gain[1:2, :] = gains[1:2, :] / gain_n[...]

    if not fused:
        send_back()

    @pl.loop(0, edges // long, unroll=fused)
    def _(k):
        rows = rows_of(k, long)
        gr[rows, :] = dot_rt(ge_first[rows, :], w_ei[2 * width :, :]).astype(BF)


    @pl.loop(0, edges // long, unroll=fused)
    def _(k):
        rows = rows_of(k, long)
        edge_grad[rows, :] = (
            live_of(k, long) * edge_cot[rows, :].astype(F32)
            + dot_rt(ge_first[rows, :], w_ei[:width, :])
        ).astype(BF)

    stores = []
    if not fused:
        stores.append(pltpu.make_async_copy(edge_grad, edge_out, store_sems.at[0]))
        stores[0].start()

    def gather_back(k):
        rows = rows_of(k, long)
        acc[rows, :] = (
            node_cot[rows, :].astype(F32)
            + dot_rt(g_first[rows, :], w_ni[:width, :])
            + dot(hot(send_row[...], (long, edges), 0, k * long), gs[...])
            + dot(hot(recv_row[...], (long, edges), 0, k * long), gr[...])
        )

    gathers = nodes // long
    pl.loop(0, gathers // 2, unroll=fused)(gather_back)
    if fused:
        red_o.step2(0, zs)
        red_no.along()
        red_ni.along()
    pl.loop(gathers // 2, gathers, unroll=fused)(gather_back)
    if fused:
        red_ea.step2(0, zs)
        red_eb.step2(0, zs)
        red_o.along()
        red_ea.along()
        red_eb.along()
        red_no.share()
        red_ni.share()
    wait_all(moving)

    @pl.loop(0, node_tiles, unroll=fused)
    def _(k):
        rows = rows_of(k)
        node_grad[rows, :] = (
            acc[rows, :]
            + dot(
                hot(list_row[:, :halo], (tile, halo), 0, k * tile),
                returned[...].reshape(halo, width),
            )
        ).astype(BF)

    if not fused:
        stores.append(pltpu.make_async_copy(node_grad, node_out, store_sems.at[1]))
        stores[1].start()
    if fused:
        red_o.share()
        red_ea.share()
        red_eb.share()
        red_no.finish(sums[0])
        red_ni.finish(sums[1])
        red_o.finish(sums[4])
        red_ea.finish(sums[2])
        red_eb.finish(sums[3])
    for store in stores:
        store.wait()


def closing(factor, depths, *refs):
    edge_in, node_in, sum_no, sum_ni, sum_ea, sum_eb, sum_o = refs[:7]
    outs = refs[7:15]
    holds, store_sems = refs[15:21], refs[21]
    o_ei, o_eo, o_gain_e, o_ni, o_no, o_gain_n = holds
    d_ei, d_eo, d_ni, d_no = depths
    stores = [
        pltpu.make_async_copy(source, out, store_sems.at[order])
        for order, (source, out) in enumerate(zip((edge_in, node_in) + tuple(holds), outs))
    ]
    stores[0].start()
    stores[1].start()
    for quarter in range(4):
        span = slice(quarter * LANES, (quarter + 1) * LANES)
        o_ei[: sum_ea.shape[1], span] = sum_ea[quarter].astype(F32) * factor
        o_ei[sum_ea.shape[1] :, span] = sum_eb[quarter].astype(F32) * factor
    stores[2].start()
    for quarter in range(4):
        span = slice(quarter * LANES, (quarter + 1) * LANES)
        o_ni[:, span] = sum_ni[quarter].astype(F32) * factor
        o_no[:, span] = sum_no[quarter].astype(F32) * factor
        o_eo[:, span] = sum_o[quarter, :d_eo].astype(F32) * factor
    for order in (3, 5, 6):
        stores[order].start()
    piece = o_gain_e.shape[1]
    p = lax.axis_index("patch")
    own = jnp.zeros((PACK, piece), F32)
    for quarter in range(4):
        lane = lax.broadcasted_iota(jnp.int32, (LANES, piece), 0) + quarter * LANES
        want = lax.broadcasted_iota(jnp.int32, (LANES, piece), 1) + p * piece
        pick = jnp.where(lane == want, 1.0, 0.0).astype(BF)
        own += dot(sum_o[quarter, d_eo:], pick)
    o_gain_e[...] = own[0:1] * factor
    o_gain_n[...] = own[1:2] * factor
    for order in (4, 7):
        stores[order].start()
    for store in stores:
        store.wait()


def reduction_scratch(zs, depth):
    middle = depth // 2 // PACK * PACK
    rest = depth - middle
    shapes = (
        (2, zs, 2, 2, depth),
        (zs, 2, 2, depth),
        (zs, 2, middle),
        (zs, 2, rest),
        (zs, 2, middle),
        (zs, 2, rest),
        (zs, 2, middle),
        (zs, 2, rest),
        (zs, middle),
        (zs, rest),
        (zs, rest),
        (zs, middle),
        (zs, depth),
        (zs - 1, depth),
        (4, depth),
    )
    return [pltpu.VMEM(shape + (LANES,), BF) for shape in shapes]


def local(
    n_group,
    n_patch,
    node_tape,
    edge_tape,
    node_cot,
    edge_cot,
    w_edge_in,
    w_edge_out,
    gain_edge,
    w_node_in,
    w_node_out,
    gain_node,
    senders,
    receivers,
    tile_count,
    send_rows,
):
    nodes, width = node_tape.shape[1:]
    edges = edge_tape.shape[1]
    listed = send_rows.shape[1]
    peer_rows = listed // n_patch
    padded = -(-peer_rows // PACK) * PACK
    halo = n_patch * padded
    tile = min(2 * LANES, nodes, edges)
    factor = float(n_group * n_patch * edges) ** (-0.5)

    if padded != peer_rows:
        beyond = senders - nodes
        beyond = beyond // peer_rows * padded + beyond % peer_rows
        senders = jnp.where(senders < nodes, senders, nodes + beyond)
        send_rows = jnp.pad(
            send_rows.reshape(n_patch, peer_rows),
            ((0, 0), (0, padded - peer_rows)),
            constant_values=-1,
        ).reshape(1, halo)
    slots = -(-halo // LANES) * LANES
    if slots != halo:
        send_rows = jnp.pad(send_rows, ((0, 0), (0, slots - halo)), constant_values=-1)

    def lane_rows(index):
        rows = -(-index.size // LANES)
        full = -(-rows // 8) * 8
        if index.shape == (full, LANES):
            return index
        return jnp.pad(index.reshape(-1), (0, full * LANES - index.size)).reshape(full, LANES)

    weights = (w_edge_in, w_edge_out, w_node_in, w_node_out)
    depths = [w.shape[0] // n_patch for w in weights]
    zs = n_patch // 2
    fused = (
        n_group == 4
        and n_patch % 4 == 0
        and n_patch & (n_patch - 1) == 0
        and width == 4 * LANES
        and all(d % PACK == 0 and 2 * d % LANES == 0 for d in depths)
        and depths[0] >= 2 * PACK
    )
    operands = (
        node_tape[0],
        send_rows,
        lane_rows(senders),
        lane_rows(receivers),
        edge_tape[0],
        w_edge_in,
        w_edge_out,
        gain_edge[None],
        w_node_in,
        w_node_out,
        gain_node[None],
        node_cot[0],
        edge_cot[0],
        tile_count[None],
    )
    scratch = [pltpu.VMEM(operand.shape, operand.dtype) for operand in operands]
    if not fused:
        scratch += [pltpu.VMEM((edges, width), BF), pltpu.VMEM((nodes, width), BF)]
    scratch += [
        pltpu.SemaphoreType.DMA((len(operands),)),
        pltpu.SemaphoreType.DMA((2,)),
    ]
    for length in (edges, edges, slots):
        scratch += [pltpu.VMEM((length, 1), jnp.int32), pltpu.VMEM((1, length), jnp.int32)]
    scratch += [pltpu.VMEM((n_patch, padded, width), BF)] * 4
    by_edge, by_node = pltpu.VMEM((edges, width), BF), pltpu.VMEM((nodes, width), BF)
    wide_edge, wide_node = pltpu.VMEM((edges, width), F32), pltpu.VMEM((nodes, width), F32)
    scratch += [by_edge, by_edge, wide_edge, by_edge, wide_edge, pltpu.VMEM((edges, 1), F32)]
    scratch += [by_edge, by_node]
    scratch += [by_node, wide_node, by_node, by_node, wide_node, by_node]
    scratch += [by_edge, by_edge, by_edge, by_edge, pltpu.VMEM((PACK, width), F32)]
    if fused:
        scratch += [pltpu.VMEM((edges, nodes), BF)]
    n_copies = 2 * (n_patch - 1)
    d_ei, d_eo, d_ni, d_no = depths
    reductions = []
    if fused:
        d_ea = d_ei // 2 // PACK * PACK
        shared = (d_no, d_ni, d_ea, d_ei - d_ea, d_eo + PACK)
        for depth, pairs, halves in zip(shared, (1, 2, 2, 2, 1), (1, 2, 1, 1, 1)):
            reductions += reduction_scratch(zs, depth)
            n_copies += pairs + 4 * halves + zs - 1 + 3
        summed_shapes = [pltpu.VMEM((4, depth, LANES), BF) for depth in shared]
    else:
        summed_shapes = [jax.ShapeDtypeStruct((w.shape[0], width), F32) for w in weights]
        summed_shapes += [jax.ShapeDtypeStruct((PACK, width), F32)]
    in_flight = n_copies // 2 + 4 if fused else n_copies
    scratch += [pltpu.SemaphoreType.DMA((in_flight,)), pltpu.SemaphoreType.DMA((n_copies,))]
    scratch += reductions

    vmem = pl.BlockSpec(memory_space=pltpu.VMEM)
    big = pltpu.VMEM if fused else jax.ShapeDtypeStruct
    anywhere = pl.BlockSpec(memory_space=pl.ANY)
    sizes = (n_group, n_patch, padded, tile, senders.shape[1], fused, depths)
    edge_grad, node_grad, *sums = pl.pallas_call(
        functools.partial(kernel, sizes),
        out_shape=[big((edges, width), BF), big((nodes, width), BF)] + summed_shapes,
        in_specs=[anywhere] * len(operands),
        out_specs=[vmem if fused else anywhere] * 2 + [vmem] * len(summed_shapes),
        scratch_shapes=scratch,
        compiler_params=pltpu.CompilerParams(
            collective_id=0, has_side_effects=True, vmem_limit_bytes=54 * 1024 * 1024
        ),
    )(*operands)
    if fused:
        piece = width // n_patch
        rows_out = [jax.ShapeDtypeStruct((depth, width), F32) for depth in depths]
        gain_out = jax.ShapeDtypeStruct((1, piece), F32)
        o_ei, o_eo, o_ni, o_no = rows_out
        edge_grad, node_grad, o_ei, o_eo, gain_e, o_ni, o_no, gain_n = pl.pallas_call(
            functools.partial(closing, factor, depths),
            out_shape=[
                jax.ShapeDtypeStruct((edges, width), BF),
                jax.ShapeDtypeStruct((nodes, width), BF),
                o_ei,
                o_eo,
                gain_out,
                o_ni,
                o_no,
                gain_out,
            ],
            in_specs=[vmem] * 7,
            out_specs=[anywhere] * 8,
            scratch_shapes=[
                pltpu.VMEM((d_ei, width), F32),
                pltpu.VMEM((d_eo, width), F32),
                pltpu.VMEM((1, piece), F32),
                pltpu.VMEM((d_ni, width), F32),
                pltpu.VMEM((d_no, width), F32),
                pltpu.VMEM((1, piece), F32),
                pltpu.SemaphoreType.DMA((8,)),
            ],
            compiler_params=pltpu.CompilerParams(vmem_limit_bytes=16 * 1024 * 1024),
        )(*[pltpu.with_memory_space_constraint(x, pltpu.VMEM) for x in (edge_grad, node_grad, *sums)])
        return (
            edge_grad[None],
            node_grad[None],
            o_ei,
            o_eo,
            gain_e.reshape(piece),
            o_ni,
            o_no,
            gain_n.reshape(piece),
        )
    p_ei, p_eo, p_ni, p_no, p_gain = sums

    def summed(value):
        part = lax.psum_scatter(value, "patch", scatter_dimension=0, tiled=True)
        return lax.psum(part.astype(BF), "group").astype(F32) * factor

    return (
        edge_grad[None],
        node_grad[None],
        summed(p_ei),
        summed(p_eo),
        summed(p_gain[0]),
        summed(p_ni),
        summed(p_no),
        summed(p_gain[1]),
    )


def solution(mesh):
    member = P("group", "patch", None)
    placed = (member,) * 4 + (P(),) * 6
    placed += (P("patch", None), P("patch", None), P("patch"), P("patch", None))
    rows = P("patch", None)
    return jax.shard_map(
        functools.partial(local, mesh.shape["group"], mesh.shape["patch"]),
        mesh=mesh,
        in_specs=placed,
        out_specs=(member, member, rows, rows, P("patch"), rows, rows, P("patch")),
        check_vma=False,
    )
```

```python
import functools

import jax
import jax.numpy as jnp
from jax import lax
from jax.experimental import pallas as pl
from jax.experimental.pallas import tpu as pltpu
from jax.sharding import PartitionSpec as P

epsilon = 1e-05
BF = jnp.bfloat16
F32 = jnp.float32
LANES = 128
PACK = 16
MESH = pl.DeviceIdType.MESH


def dot(left, right):
    return jnp.dot(left, right, preferred_element_type=F32)


def dot_rt(left, right):
    return lax.dot_general(left, right, (((1,), (1,)), ((), ())), preferred_element_type=F32)


def dot_lt(left, right):
    return lax.dot_general(left, right, (((0,), (0,)), ((), ())), preferred_element_type=F32)


def silu_pair(values):
    squash = 0.5 * jnp.tanh(0.5 * values) + 0.5
    active = values * squash
    return (active, squash + active * (1.0 - squash))


def normalize(values, live=None):
    centred = values - jnp.mean(values, axis=1, keepdims=True)
    inverse = lax.rsqrt(jnp.mean(centred * centred, axis=1, keepdims=True) + epsilon)
    if live is not None:
        inverse = inverse * live
    return (centred * inverse, inverse)


def normalize_back(upstream, normed, inverse):
    product = upstream * normed
    second = inverse * (
        upstream
        - jnp.mean(upstream, axis=1, keepdims=True)
        - normed * jnp.mean(product, axis=1, keepdims=True)
    )
    return (second.astype(BF), jnp.sum(product, axis=0, keepdims=True))


def hot(index, shape, axis, base):
    return jnp.where(lax.broadcasted_iota(jnp.int32, shape, axis) + base == index, 1.0, 0.0).astype(
        BF
    )


class Waited:
    def __init__(self, copies, copy, slot):
        self.copies, self.copy, self.slot = copies, copy, slot

    def wait(self):
        self.copy.wait()
        self.copies.free.append(self.slot)


class Copies:
    def __init__(self, send_sems, recv_sems):
        self.send_sems, self.recv_sems, self.used = send_sems, recv_sems, 0
        self.free = list(range(send_sems.shape[0]))

    def start(self, source, target, device):
        slot = self.free.pop(0)
        copy = pltpu.make_async_remote_copy(
            src_ref=source,
            dst_ref=target,
            send_sem=self.send_sems.at[slot],
            recv_sem=self.recv_sems.at[self.used],
            device_id=device,
            device_id_type=MESH,
        )
        self.used += 1
        copy.start()
        return Waited(self, copy, slot)


def wait_all(copies):
    for copy in copies:
        copy.wait()


def staggered(count, stages, hooks=None, unrolled=True):
    if not unrolled:

        @pl.loop(0, count)
        def _(k):
            held = None
            for stage in stages:
                held = stage(k, held)

        return
    held = {}
    for step in range(count + len(stages) - 1):
        for order in range(len(stages)):
            k = step - order
            if 0 <= k < count:
                held[k] = stages[order](k, held.get(k))
        if hooks and step in hooks:
            hooks[step]()


def flipped(index, bits):
    for place in range(bits.bit_length()):
        if bits >> place & 1:
            index = index + (1 - 2 * lax.rem(lax.div(index, 1 << place), 2)) * (1 << place)
    return index


class Place:
    def __init__(self, n_patch):
        self.gi = lax.axis_index("group")
        self.p = lax.axis_index("patch")
        self.core = lax.rem(self.p, 2)
        self.z = lax.div(self.p, 2)
        self.zs = n_patch // 2
        self.partner = {"group": self.gi, "patch": self.p + 1 - 2 * self.core}
        self.gx, self.gy = lax.rem(self.gi, 2), lax.div(self.gi, 2)
        flip_x, flip_y = 1 - 2 * self.gx, 2 - 4 * self.gy
        self.members = [
            {"group": self.gi + flip, "patch": self.p} for flip in (flip_x, flip_y, flip_x + flip_y)
        ]
        self.x_peer, self.y_peer = self.members[:2]


class Reduction:
    def __init__(self, copies, refs, place):
        self.copies, self.place = copies, place
        self.g, self.rc, self.sx, self.sy, self.ox, self.oy = refs[:6]
        self.r1x, self.r1y, self.b0, self.b1, self.r2x, self.r2y, self.c, self.r3, self.f = refs[6:]
        depth, middle = self.c.shape[1], self.sx.shape[2]
        self.low, self.high = pl.ds(0, middle), pl.ds(middle, depth - middle)
        self.pairs, self.first, self.second = {}, {}, []

    def put(self, first, last, row, size, value, skip=0):
        value = value.astype(BF)
        each = value.shape[0] // (2 * (last - first))
        for k in range(first, last):
            for c in range(2):
                start = (2 * (k - first) + c) * each + skip
                for quarter in range(4):
                    self.g[c, k, quarter // 2, quarter % 2, row : row + size, :] = value[
                        start : start + size, quarter * LANES : (quarter + 1) * LANES
                    ]

    def pair(self, first, last):
        here = self.place
        span = pl.ds(first, last - first)
        self.pairs[first] = self.copies.start(
            self.g.at[1 - here.core, span], self.rc.at[span], here.partner
        )

    def joint(self, k, gy, gx, rows):
        own = self.g[self.place.core, k, gy, gx, rows].astype(F32)
        return (own + self.rc[k, gy, gx, rows].astype(F32)).astype(BF)

    def step1(self, first, last):
        here = self.place
        for k in range(first, last):
            if k in self.pairs:
                self.pairs[k].wait()
            for other in range(2):
                self.sx[k, other] = self.joint(k, other, 1 - here.gx, self.low)
                self.sy[k, other] = self.joint(k, 1 - here.gy, other, self.high)
        span = pl.ds(first, last - first)
        self.first[first] = [
            self.copies.start(self.sx.at[span], self.r1x.at[span], here.x_peer),
            self.copies.start(self.sy.at[span], self.r1y.at[span], here.y_peer),
        ]
        for k in range(first, last):
            for other in range(2):
                self.ox[k, other] = self.joint(k, other, here.gx, self.low)
                self.oy[k, other] = self.joint(k, here.gy, other, self.high)

    def step2(self, first, last):
        here = self.place
        wait_all(self.first[first])
        for k in range(first, last):
            self.b0[k] = (
                self.ox[k, 1 - here.gy].astype(F32) + self.r1x[k, 1 - here.gy].astype(F32)
            ).astype(BF)
            self.b1[k] = (
                self.oy[k, 1 - here.gx].astype(F32) + self.r1y[k, 1 - here.gx].astype(F32)
            ).astype(BF)
        span = pl.ds(first, last - first)
        self.second += [
            self.copies.start(self.b0.at[span], self.r2y.at[span], here.y_peer),
            self.copies.start(self.b1.at[span], self.r2x.at[span], here.x_peer),
        ]

    def along(self):
        here = self.place
        wait_all(self.second)
        for k in range(here.zs):
            self.c[k, self.low] = (
                self.ox[k, here.gy].astype(F32)
                + self.r1x[k, here.gy].astype(F32)
                + self.r2y[k].astype(F32)
            ).astype(BF)
            self.c[k, self.high] = (
                self.oy[k, here.gx].astype(F32)
                + self.r1y[k, here.gx].astype(F32)
                + self.r2x[k].astype(F32)
            ).astype(BF)
        self.moves = []
        for step in range(here.zs - 1, 0, -1):
            there = flipped(here.z, step)
            self.moves.append(
                self.copies.start(
                    self.c.at[there],
                    self.r3.at[step - 1],
                    {"group": here.gi, "patch": there * 2 + here.core},
                )
            )

    def share(self):
        here = self.place
        wait_all(self.moves)
        total = self.c[here.z].astype(F32)
        for step in range(1, here.zs):
            total += self.r3[step - 1].astype(F32)
        self.f[here.gi] = total.astype(BF)
        mine = self.f.at[here.gi]
        self.moves = [self.copies.start(mine, mine, member) for member in here.members]

    def finish(self, out):
        wait_all(self.moves)
        out[...] = self.f[...]


class GainSum:
    def __init__(self, copies, refs, place):
        self.copies, self.place = copies, place
        self.own, self.got = refs

    def send(self, order, first, devices):
        self.order, self.first = order, first
        self.moves = [
            self.copies.start(self.own.at[order], self.got.at[first + slot], device)
            for slot, device in enumerate(devices)
        ]

    def gather(self):
        wait_all(self.moves)
        total = self.own[self.order]
        for slot in range(len(self.moves)):
            total += self.got[self.first + slot]
        return total

    def start(self, gains):
        for row in range(2):
            for quarter in range(4):
                line = 4 * row + quarter
                self.own[0, line : line + 1, :] = gains[
                    row : row + 1, quarter * LANES : (quarter + 1) * LANES
                ]
        self.send(0, 0, [self.place.partner])

    def members(self):
        self.own[1] = self.gather()
        self.send(1, 1, self.place.members)

    def along(self):
        here = self.place
        self.own[2] = self.gather()
        chips = [flipped(here.z, step) for step in range(1, here.zs)]
        self.send(
            2, 4, [{"group": here.gi, "patch": chip * 2 + here.core} for chip in chips]
        )

    def finish(self, out):
        out[...] = self.gather()


COUNT_SHARES = 15


def kernel(sizes, *refs):
    n_group, n_patch, padded, tile, tile_edges, fused, depths = sizes
    refs = list(refs)

    def take(count):
        got = refs[:count]
        del refs[:count]
        return got

    stored = take(14)
    edge_out, node_out = take(2)
    sums = take(6 if fused else 5)
    loaded = take(14)
    node, list_in, send_tiles, recv_tiles, edge, w_ei, w_eo, gain_e = loaded[:8]
    w_ni, w_no, gain_n, node_cot, edge_cot, count = loaded[8:]
    edge_grad, node_grad = (edge_out, node_out) if fused else take(2)
    load_sems, store_sems = take(2)
    send_col, send_row, recv_col, recv_row, list_col, list_row = take(6)
    outgoing, incoming, spread, returned = take(4)
    x_s, x_r, e_first, hidden, normed, inverse, message, joined = take(8)
    n_hidden, n_first, g_second, g_first, acc, gj, ge_second, ge_first, gs, gr, gains = take(11)
    recv_hot = take(1)[0] if fused else None
    send_sems, recv_sems = take(2)
    nodes, width = node.shape
    edges = edge.shape[0]
    halo = n_patch * padded
    place = Place(n_patch)
    gi, p = place.gi, place.p
    copies = Copies(send_sems, recv_sems)
    barrier = pltpu.get_barrier_semaphore()
    if fused:
        others = [flipped(p, d) for d in range(n_patch - 1, 0, -1)]
    else:
        others = [lax.rem(p + d, n_patch) for d in range(1, n_patch)]
    peers = [{"group": gi, "patch": other} for other in others]
    greeted = list(peers)
    if fused:
        greeted += place.members
    for peer in greeted:
        pl.semaphore_signal(barrier, inc=1, device_id=peer, device_id_type=MESH)
    loads = [
        pltpu.make_async_copy(source, target, load_sems.at[order])
        for order, (source, target) in enumerate(zip(stored, loaded))
    ]
    first = (1, 0, 2, 3) if fused else range(len(loads))
    for order in first:
        loads[order].start()

    def column_of(line, column):
        for order in range(column.shape[0] // LANES):
            span = slice(order * LANES, (order + 1) * LANES)
            wide = jnp.broadcast_to(line[:, span].astype(F32), (8, LANES))
            column[span, :] = jnp.transpose(wide)[:, :1].astype(jnp.int32)

    loads[1].wait()
    for order in range(len(loads)):
        if order not in first:
            loads[order].start()
    list_row[...] = list_in[...]
    column_of(list_row, list_col)
    loads[0].wait()
    chosen = dot(hot(list_col[:halo, :], (halo, nodes), 1, 0), node[...]).astype(BF)
    outgoing[...] = chosen.reshape(n_patch, padded, width)
    pl.semaphore_wait(barrier, len(greeted))
    moving = [
        copies.start(outgoing.at[other], incoming.at[p], peer)
        for other, peer in zip(others, peers)
    ]
    incoming[p] = outgoing[p]
    gains[...] = jnp.zeros_like(gains)

    loads[2].wait()
    loads[3].wait()
    for tiles, column, line in ((send_tiles, send_col, send_row), (recv_tiles, recv_col, recv_row)):
        turned = jnp.transpose(tiles[...].astype(F32)).astype(jnp.int32)
        for order in range(line.shape[1] // LANES):
            span = slice(order * LANES, (order + 1) * LANES)
            column[span, :] = turned[:, order : order + 1]
            line[:, span] = tiles[order : order + 1, :]

    loads[4].wait()
    loads[5].wait()

    def rows_of(k, size=tile):
        return pl.ds(k * size if isinstance(k, int) else pl.multiple_of(k * size, size), size)

    long = 2 * tile if fused and edges % (2 * tile) == 0 and nodes % (2 * tile) == 0 else tile

    edge_tiles = edges // tile

    @pl.loop(0, edges // long, unroll=fused)
    def _(k):
        rows = rows_of(k, long)
        chosen = hot(recv_col[rows, :], (long, nodes), 1, 0)
        if fused:
            recv_hot[rows, :] = chosen
        latent = dot(chosen, node[...]).astype(BF)
        x_r[rows, :] = latent
        e_first[rows, :] = dot(edge[rows, :], w_ei[:width, :]) + dot(latent, w_ei[2 * width :, :])


    @pl.loop(0, edges // long, unroll=fused)
    def _(k):
        rows = rows_of(k, long)
        x_s[rows, :] = dot(hot(send_col[rows, :], (long, nodes), 1, 0), node[...]).astype(BF)

    loads[8].wait()

    @pl.loop(0, nodes // long, unroll=fused)
    def _(k):
        rows = rows_of(k, long)
        n_first[rows, :] = dot(node[rows, :], w_ni[:width, :])

    for load in loads[6:8] + loads[9:]:
        load.wait()
    wait_all(moving)

    def live_of(k, size=tile):
        slot = lax.broadcasted_iota(jnp.int32, (size, 1), 0) + k * size
        return jnp.where(slot < count[...] * tile_edges, 1.0, 0.0)


    def edge_first(k, _):
        rows = rows_of(k)
        latent = dot(
            hot(send_col[rows, :], (tile, halo), 1, nodes), incoming[...].reshape(halo, width)
        )
        latent = x_s[rows, :] + latent.astype(BF)
        x_s[rows, :] = latent
        return e_first[rows, :] + dot(latent, w_ei[width : 2 * width, :])

    def edge_hidden(k, first):
        rows = rows_of(k)
        active, slope = silu_pair(first)
        e_first[rows, :] = slope
        hid = active.astype(BF)
        hidden[rows, :] = hid
        return dot(hid, w_eo[...])

    def edge_message(k, second):
        rows = rows_of(k)
        norm, inv = normalize(second, live_of(k))
        normed[rows, :] = norm
        inverse[rows, :] = inv
        message[rows, :] = (gain_e[...] * norm).astype(BF)

    staggered(edge_tiles, (edge_first, edge_hidden, edge_message), unrolled=fused)

    def node_first(k, _):
        rows = rows_of(k, long)
        got = dot(hot(recv_row[...], (long, edges), 0, k * long), message[...]).astype(BF)
        joined[rows, :] = got
        return n_first[rows, :] + dot(got, w_ni[width:, :])

    def node_hidden(k, first):
        rows = rows_of(k, long)
        active, slope = silu_pair(first)
        hid = active.astype(BF)
        n_hidden[rows, :] = hid
        return (slope, dot(hid, w_no[...]))

    def node_second(k, held):
        slope, second = held
        rows = rows_of(k, long)
        norm, inv = normalize(second)
        up = node_cot[rows, :].astype(F32)
        second, total = normalize_back(up * gain_n[...], norm, inv)
        gains[1:2, :] += total
        g_second[rows, :] = second
        return (slope, dot_rt(second, w_no[...]))

    def node_back(k, held):
        slope, grad = held
        g_first[rows_of(k, long), :] = (grad * slope).astype(BF)

    staggered(nodes // long, (node_first, node_hidden, node_second, node_back), unrolled=fused)

    def node_message():
        @pl.loop(0, nodes // long, unroll=fused)
        def _(k):
            rows = rows_of(k, long)
            gj[rows, :] = dot_rt(g_first[rows, :], w_ni[width:, :]).astype(BF)

    def edge_taken(k, _):
        if fused:
            return dot(recv_hot[rows_of(k), :], gj[...])
        return dot(hot(recv_col[rows_of(k), :], (tile, nodes), 1, 0), gj[...])

    def edge_second(k, taken):
        rows = rows_of(k)
        norm = normed[rows, :]
        grad = edge_cot[rows, :].astype(F32) + taken
        second, total = normalize_back(grad * gain_e[...], norm, inverse[rows, :])
        gains[0:1, :] += total
        ge_second[rows, :] = second
        return dot_rt(second, w_eo[...])

    def edge_back(k, grad):
        rows = rows_of(k)
        ge_first[rows, :] = (grad * e_first[rows, :]).astype(BF)

    edge_stages = (edge_taken, edge_second, edge_back)
    moving = []

    def send_rows_back():
        @pl.loop(0, edges // long, unroll=fused)
        def _(k):
            rows = rows_of(k, long)
            gs[rows, :] = dot_rt(ge_first[rows, :], w_ei[width : 2 * width, :]).astype(BF)

    def send_back():
        back = dot(hot(send_row[...], (halo, edges), 0, nodes), ge_first[...]).astype(BF)
        back = dot_rt(back, w_ei[width : 2 * width, :]).astype(BF)
        spread[...] = back.reshape(n_patch, padded, width)
        moving.extend(
            copies.start(spread.at[other], returned.at[p], peer)
            for other, peer in zip(others, peers)
        )
        returned[p] = spread[p]

    def rows_product(sources, start, stop, right):
        parts = []
        for order, source in enumerate(sources):
            low = max(start, order * width) - order * width
            high = min(stop, (order + 1) * width) - order * width
            if low < high:
                parts.append(dot_lt(source[:, low:high], right))
        return parts[0] if len(parts) == 1 else jnp.concatenate(parts, axis=0)

    if fused:
        zs = place.zs
        half = zs // 2
        d_ei, d_eo, d_ni, d_no = depths
        red_no, red_ni, red_ea, red_eb, red_o = [
            Reduction(copies, take(COUNT_SHARES), place) for _ in range(5)
        ]
        gain_sum = GainSum(copies, take(2), place)
        d_ea = d_ei // 2 // PACK * PACK
        red_no.put(0, zs, 0, d_no, dot_lt(n_hidden[...], g_second[...]))
        red_no.pair(0, zs)
        for first in (0, half):
            last = first + half
            value = rows_product((node, joined), 2 * first * d_ni, 2 * last * d_ni, g_first[...])
            red_ni.put(first, last, 0, d_ni, value)
            red_ni.pair(first, last)
            if first == 0:
                red_no.step1(0, zs)
        node_message()
        red_ni.step1(0, half)
        staggered(edge_tiles, edge_stages, hooks={2: lambda: red_ni.step1(half, zs)})
        send_back()
        red_no.step2(0, zs)
        gains[0:1, :] = gains[0:1, :] / gain_e[...]
        gains[1:2, :] = gains[1:2, :] / gain_n[...]
        gain_sum.start(gains)
        red_o.put(0, zs, 0, d_eo, dot_lt(hidden[...], ge_second[...]))
        red_o.pair(0, zs)
        red_ni.step2(0, half)
        for first in (0, half):
            last = first + half
            value = rows_product(
                (edge, x_s, x_r), 2 * first * d_ei, 2 * last * d_ei, ge_first[...]
            )
            red_ea.put(first, last, 0, d_ea, value)
            red_eb.put(first, last, 0, d_ei - d_ea, value, skip=d_ea)
            red_ea.pair(first, last)
            red_eb.pair(first, last)
            if first == 0:
                red_o.step1(0, zs)
                gain_sum.members()
        red_ni.step2(half, zs)
        send_rows_back()
        red_ea.step1(0, zs)
        red_eb.step1(0, zs)
    else:
        o_ei, o_eo, o_ni, o_no, o_gain = sums
        o_ni[:width, :] = dot_lt(node[...], g_first[...])
        o_ni[width:, :] = dot_lt(joined[...], g_first[...])
        o_no[...] = dot_lt(n_hidden[...], g_second[...])
        node_message()
        staggered(edge_tiles, edge_stages, unrolled=False)
        o_ei[:width, :] = dot_lt(edge[...], ge_first[...])
        o_ei[width : 2 * width, :] = dot_lt(x_s[...], ge_first[...])
        o_ei[2 * width :, :] = dot_lt(x_r[...], ge_first[...])
        o_eo[...] = dot_lt(hidden[...], ge_second[...])
        o_gain[...] = gains[...]
        o_gain[0:1, :] = gains[0:1, :] / gain_e[...]
        o_gain[1:2, :] = gains[1:2, :] / gain_n[...]

    if not fused:
        send_back()
        send_rows_back()

    @pl.loop(0, edges // long, unroll=fused)
    def _(k):
        rows = rows_of(k, long)
        gr[rows, :] = dot_rt(ge_first[rows, :], w_ei[2 * width :, :]).astype(BF)


    @pl.loop(0, edges // long, unroll=fused)
    def _(k):
        rows = rows_of(k, long)
        edge_grad[rows, :] = (
            live_of(k, long) * edge_cot[rows, :].astype(F32)
            + dot_rt(ge_first[rows, :], w_ei[:width, :])
        ).astype(BF)

    stores = []
    if not fused:
        stores.append(pltpu.make_async_copy(edge_grad, edge_out, store_sems.at[0]))
        stores[0].start()

    def gather_back(k):
        rows = rows_of(k, long)
        acc[rows, :] = (
            node_cot[rows, :].astype(F32)
            + dot_rt(g_first[rows, :], w_ni[:width, :])
            + dot(hot(send_row[...], (long, edges), 0, k * long), gs[...])
            + dot(hot(recv_row[...], (long, edges), 0, k * long), gr[...])
        )

    gathers = nodes // long
    if fused:
        red_no.along()
        red_ni.along()
        red_o.step2(0, zs)
        gain_sum.along()
    pl.loop(0, gathers // 2, unroll=fused)(gather_back)
    if fused:
        red_ea.step2(0, zs)
    pl.loop(gathers // 2, gathers, unroll=fused)(gather_back)
    if fused:
        red_eb.step2(0, zs)
        red_o.along()
        red_ea.along()
        red_eb.along()
        red_no.share()
        red_ni.share()
    wait_all(moving)

    @pl.loop(0, nodes // tile, unroll=fused)
    def _(k):
        rows = rows_of(k)
        node_grad[rows, :] = (
            acc[rows, :]
            + dot(
                hot(list_row[:, :halo], (tile, halo), 0, k * tile),
                returned[...].reshape(halo, width),
            )
        ).astype(BF)

    if not fused:
        stores.append(pltpu.make_async_copy(node_grad, node_out, store_sems.at[1]))
        stores[1].start()
    if fused:
        red_o.share()
        red_ea.share()
        red_eb.share()
        red_no.finish(sums[0])
        red_ni.finish(sums[1])
        red_o.finish(sums[4])
        gain_sum.finish(sums[5])
        red_ea.finish(sums[2])
        red_eb.finish(sums[3])
    for store in stores:
        store.wait()


def closing(factor, depths, *refs):
    edge_in, node_in, sum_no, sum_ni, sum_ea, sum_eb, sum_o, sum_gain = refs[:8]
    outs = refs[8:16]
    holds, store_sems = refs[16:22], refs[22]
    o_ei, o_eo, o_gain_e, o_ni, o_no, o_gain_n = holds
    d_ei, d_eo, d_ni, d_no = depths
    stores = [
        pltpu.make_async_copy(source, out, store_sems.at[order])
        for order, (source, out) in enumerate(zip((edge_in, node_in) + tuple(holds), outs))
    ]
    stores[0].start()
    stores[1].start()
    for quarter in range(4):
        span = slice(quarter * LANES, (quarter + 1) * LANES)
        o_ei[: sum_ea.shape[1], span] = sum_ea[quarter].astype(F32) * factor
        o_ei[sum_ea.shape[1] :, span] = sum_eb[quarter].astype(F32) * factor
    stores[2].start()
    for quarter in range(4):
        span = slice(quarter * LANES, (quarter + 1) * LANES)
        o_ni[:, span] = sum_ni[quarter].astype(F32) * factor
        o_no[:, span] = sum_no[quarter].astype(F32) * factor
        o_eo[:, span] = sum_o[quarter].astype(F32) * factor
    for order in (3, 5, 6):
        stores[order].start()
    piece = o_gain_e.shape[1]
    p = lax.axis_index("patch")
    share = LANES // piece
    for row, hold in ((0, o_gain_e), (4, o_gain_n)):
        line = sum_gain[pl.ds(row + lax.div(p, share), 1), :]
        own = jnp.zeros((1, piece), F32)
        for part in range(share):
            own += jnp.where(lax.rem(p, share) == part, line[:, part * piece : (part + 1) * piece], 0.0)
        hold[...] = own * factor
    for order in (4, 7):
        stores[order].start()
    for store in stores:
        store.wait()


def reduction_scratch(zs, depth):
    middle = depth // 2 // PACK * PACK
    rest = depth - middle
    shapes = (
        (2, zs, 2, 2, depth),
        (zs, 2, 2, depth),
        (zs, 2, middle),
        (zs, 2, rest),
        (zs, 2, middle),
        (zs, 2, rest),
        (zs, 2, middle),
        (zs, 2, rest),
        (zs, middle),
        (zs, rest),
        (zs, rest),
        (zs, middle),
        (zs, depth),
        (zs - 1, depth),
        (4, depth),
    )
    return [pltpu.VMEM(shape + (LANES,), BF) for shape in shapes]


def local(
    n_group,
    n_patch,
    node_tape,
    edge_tape,
    node_cot,
    edge_cot,
    w_edge_in,
    w_edge_out,
    gain_edge,
    w_node_in,
    w_node_out,
    gain_node,
    senders,
    receivers,
    tile_count,
    send_rows,
):
    nodes, width = node_tape.shape[1:]
    edges = edge_tape.shape[1]
    listed = send_rows.shape[1]
    peer_rows = listed // n_patch
    padded = -(-peer_rows // PACK) * PACK
    halo = n_patch * padded
    tile = min(2 * LANES, nodes, edges)
    factor = float(n_group * n_patch * edges) ** (-0.5)

    if padded != peer_rows:
        beyond = senders - nodes
        beyond = beyond // peer_rows * padded + beyond % peer_rows
        senders = jnp.where(senders < nodes, senders, nodes + beyond)
        send_rows = jnp.pad(
            send_rows.reshape(n_patch, peer_rows),
            ((0, 0), (0, padded - peer_rows)),
            constant_values=-1,
        ).reshape(1, halo)
    slots = -(-halo // LANES) * LANES
    if slots != halo:
        send_rows = jnp.pad(send_rows, ((0, 0), (0, slots - halo)), constant_values=-1)

    def lane_rows(index):
        rows = -(-index.size // LANES)
        full = -(-rows // 8) * 8
        if index.shape == (full, LANES):
            return index
        return jnp.pad(index.reshape(-1), (0, full * LANES - index.size)).reshape(full, LANES)

    weights = (w_edge_in, w_edge_out, w_node_in, w_node_out)
    depths = [w.shape[0] // n_patch for w in weights]
    zs = n_patch // 2
    fused = (
        n_group == 4
        and n_patch % 4 == 0
        and n_patch & (n_patch - 1) == 0
        and width == 4 * LANES
        and all(d % PACK == 0 and 2 * d % LANES == 0 for d in depths)
        and min(depths) >= 2 * PACK
        and LANES * n_patch % width == 0
    )
    operands = (
        node_tape[0],
        send_rows,
        lane_rows(senders),
        lane_rows(receivers),
        edge_tape[0],
        w_edge_in,
        w_edge_out,
        gain_edge[None],
        w_node_in,
        w_node_out,
        gain_node[None],
        node_cot[0],
        edge_cot[0],
        tile_count[None],
    )
    scratch = [pltpu.VMEM(operand.shape, operand.dtype) for operand in operands]
    if not fused:
        scratch += [pltpu.VMEM((edges, width), BF), pltpu.VMEM((nodes, width), BF)]
    scratch += [
        pltpu.SemaphoreType.DMA((len(operands),)),
        pltpu.SemaphoreType.DMA((2,)),
    ]
    for length in (edges, edges, slots):
        scratch += [pltpu.VMEM((length, 1), jnp.int32), pltpu.VMEM((1, length), jnp.int32)]
    scratch += [pltpu.VMEM((n_patch, padded, width), BF)] * 4
    by_edge, by_node = pltpu.VMEM((edges, width), BF), pltpu.VMEM((nodes, width), BF)
    wide_edge, wide_node = pltpu.VMEM((edges, width), F32), pltpu.VMEM((nodes, width), F32)
    scratch += [by_edge, by_edge, wide_edge, by_edge, wide_edge, pltpu.VMEM((edges, 1), F32)]
    scratch += [by_edge, by_node]
    scratch += [by_node, wide_node, by_node, by_node, wide_node, by_node]
    scratch += [by_edge, by_edge, by_edge, by_edge, pltpu.VMEM((PACK, width), F32)]
    if fused:
        scratch += [pltpu.VMEM((edges, nodes), BF)]
    n_copies = 2 * (n_patch - 1)
    d_ei, d_eo, d_ni, d_no = depths
    reductions = []
    if fused:
        d_ea = d_ei // 2 // PACK * PACK
        shared = (d_no, d_ni, d_ea, d_ei - d_ea, d_eo)
        for depth, pairs, halves in zip(shared, (1, 2, 2, 2, 1), (1, 2, 1, 1, 1)):
            reductions += reduction_scratch(zs, depth)
            n_copies += pairs + 4 * halves + zs - 1 + 3
        reductions += [pltpu.VMEM((3, 8, LANES), F32), pltpu.VMEM((3 + zs, 8, LANES), F32)]
        n_copies += 3 + zs
        summed_shapes = [pltpu.VMEM((4, depth, LANES), BF) for depth in shared]
        summed_shapes += [pltpu.VMEM((8, LANES), F32)]
    else:
        summed_shapes = [jax.ShapeDtypeStruct((w.shape[0], width), F32) for w in weights]
        summed_shapes += [jax.ShapeDtypeStruct((PACK, width), F32)]
    in_flight = n_copies // 2 + 4 if fused else n_copies
    scratch += [pltpu.SemaphoreType.DMA((in_flight,)), pltpu.SemaphoreType.DMA((n_copies,))]
    scratch += reductions

    vmem = pl.BlockSpec(memory_space=pltpu.VMEM)
    big = pltpu.VMEM if fused else jax.ShapeDtypeStruct
    anywhere = pl.BlockSpec(memory_space=pl.ANY)
    sizes = (n_group, n_patch, padded, tile, senders.shape[1], fused, depths)
    edge_grad, node_grad, *sums = pl.pallas_call(
        functools.partial(kernel, sizes),
        out_shape=[big((edges, width), BF), big((nodes, width), BF)] + summed_shapes,
        in_specs=[anywhere] * len(operands),
        out_specs=[vmem if fused else anywhere] * 2 + [vmem] * len(summed_shapes),
        scratch_shapes=scratch,
        compiler_params=pltpu.CompilerParams(
            collective_id=0, has_side_effects=True, vmem_limit_bytes=54 * 1024 * 1024
        ),
    )(*operands)
    if fused:
        piece = width // n_patch
        rows_out = [jax.ShapeDtypeStruct((depth, width), F32) for depth in depths]
        gain_out = jax.ShapeDtypeStruct((1, piece), F32)
        o_ei, o_eo, o_ni, o_no = rows_out
        edge_grad, node_grad, o_ei, o_eo, gain_e, o_ni, o_no, gain_n = pl.pallas_call(
            functools.partial(closing, factor, depths),
            out_shape=[
                jax.ShapeDtypeStruct((edges, width), BF),
                jax.ShapeDtypeStruct((nodes, width), BF),
                o_ei,
                o_eo,
                gain_out,
                o_ni,
                o_no,
                gain_out,
            ],
            in_specs=[vmem] * 8,
            out_specs=[anywhere] * 8,
            scratch_shapes=[
                pltpu.VMEM((d_ei, width), F32),
                pltpu.VMEM((d_eo, width), F32),
                pltpu.VMEM((1, piece), F32),
                pltpu.VMEM((d_ni, width), F32),
                pltpu.VMEM((d_no, width), F32),
                pltpu.VMEM((1, piece), F32),
                pltpu.SemaphoreType.DMA((8,)),
            ],
            compiler_params=pltpu.CompilerParams(vmem_limit_bytes=16 * 1024 * 1024),
        )(*[pltpu.with_memory_space_constraint(x, pltpu.VMEM) for x in (edge_grad, node_grad, *sums)])
        return (
            edge_grad[None],
            node_grad[None],
            o_ei,
            o_eo,
            gain_e.reshape(piece),
            o_ni,
            o_no,
            gain_n.reshape(piece),
        )
    p_ei, p_eo, p_ni, p_no, p_gain = sums

    def summed(value):
        part = lax.psum_scatter(value, "patch", scatter_dimension=0, tiled=True)
        return lax.psum(part.astype(BF), "group").astype(F32) * factor

    return (
        edge_grad[None],
        node_grad[None],
        summed(p_ei),
        summed(p_eo),
        summed(p_gain[0]),
        summed(p_ni),
        summed(p_no),
        summed(p_gain[1]),
    )


def solution(mesh):
    member = P("group", "patch", None)
    placed = (member,) * 4 + (P(),) * 6
    placed += (P("patch", None), P("patch", None), P("patch"), P("patch", None))
    rows = P("patch", None)
    return jax.shard_map(
        functools.partial(local, mesh.shape["group"], mesh.shape["patch"]),
        mesh=mesh,
        in_specs=placed,
        out_specs=(member, member, rows, rows, P("patch"), rows, rows, P("patch")),
        check_vma=False,
    )
```

```python
import functools

import jax
import jax.numpy as jnp
from jax import lax
from jax.experimental import pallas as pl
from jax.experimental.pallas import tpu as pltpu
from jax.sharding import PartitionSpec as P

epsilon = 1e-05
BF = jnp.bfloat16
F32 = jnp.float32
LANES = 128
PACK = 16
PARTS = 3
MESH = pl.DeviceIdType.MESH


def dot(left, right):
    return jnp.dot(left, right, preferred_element_type=F32)


def dot_rt(left, right):
    return lax.dot_general(left, right, (((1,), (1,)), ((), ())), preferred_element_type=F32)


def dot_lt(left, right):
    return lax.dot_general(left, right, (((0,), (0,)), ((), ())), preferred_element_type=F32)


def silu_pair(values):
    squash = 0.5 * jnp.tanh(0.5 * values) + 0.5
    active = values * squash
    return (active, squash + active * (1.0 - squash))


def normalize(values, live=None):
    centred = values - jnp.mean(values, axis=1, keepdims=True)
    inverse = lax.rsqrt(jnp.mean(centred * centred, axis=1, keepdims=True) + epsilon)
    if live is not None:
        inverse = inverse * live
    return (centred * inverse, inverse)


def normalize_back(upstream, normed, inverse):
    product = upstream * normed
    second = inverse * (
        upstream
        - jnp.mean(upstream, axis=1, keepdims=True)
        - normed * jnp.mean(product, axis=1, keepdims=True)
    )
    return (second.astype(BF), jnp.sum(product, axis=0, keepdims=True))


def hot(index, shape, axis, base):
    return jnp.where(lax.broadcasted_iota(jnp.int32, shape, axis) + base == index, 1.0, 0.0).astype(
        BF
    )


class Waited:
    def __init__(self, copies, copy, slot):
        self.copies, self.copy, self.slot = copies, copy, slot

    def wait(self):
        self.copy.wait()
        self.copies.free.append(self.slot)


class Copies:
    def __init__(self, send_sems, recv_sems):
        self.send_sems, self.recv_sems, self.used = send_sems, recv_sems, 0
        self.free = list(range(send_sems.shape[0]))[::-1]

    def start(self, source, target, device):
        slot = self.free.pop()
        copy = pltpu.make_async_remote_copy(
            src_ref=source,
            dst_ref=target,
            send_sem=self.send_sems.at[slot],
            recv_sem=self.recv_sems.at[self.used],
            device_id=device,
            device_id_type=MESH,
        )
        self.used += 1
        copy.start()
        return Waited(self, copy, slot)


def wait_all(copies):
    for copy in copies:
        copy.wait()


def staggered(count, stages, hooks=None, unrolled=True):
    if not unrolled:

        @pl.loop(0, count)
        def _(k):
            held = None
            for stage in stages:
                held = stage(k, held)

        return
    held = {}
    for step in range(count + len(stages) - 1):
        for order in range(len(stages)):
            k = step - order
            if 0 <= k < count:
                held[k] = stages[order](k, held.get(k))
        if hooks and step in hooks:
            hooks[step]()


def parts_of(depth):
    each = -(-depth // PARTS // PACK) * PACK
    return [min(each, depth - start) for start in range(0, depth, each)]


def flipped(index, bits):
    for place in range(bits.bit_length()):
        if bits >> place & 1:
            index = index + (1 - 2 * lax.rem(lax.div(index, 1 << place), 2)) * (1 << place)
    return index


class Place:
    def __init__(self, n_patch):
        self.gi = lax.axis_index("group")
        self.p = lax.axis_index("patch")
        self.core = lax.rem(self.p, 2)
        self.z = lax.div(self.p, 2)
        self.zs = n_patch // 2
        self.partner = {"group": self.gi, "patch": self.p + 1 - 2 * self.core}
        self.gx, self.gy = lax.rem(self.gi, 2), lax.div(self.gi, 2)
        flip_x, flip_y = 1 - 2 * self.gx, 2 - 4 * self.gy
        self.members = [
            {"group": self.gi + flip, "patch": self.p} for flip in (flip_x, flip_y, flip_x + flip_y)
        ]
        self.x_peer, self.y_peer = self.members[:2]


class Reduction:
    def __init__(self, copies, refs, place):
        self.copies, self.place = copies, place
        self.g, self.rc, self.sx, self.sy, self.ox, self.oy = refs[:6]
        self.r1x, self.r1y, self.b0, self.b1, self.r2x, self.r2y, self.c, self.r3, self.f = refs[6:]
        depth, middle = self.c.shape[1], self.sx.shape[2]
        self.low, self.high = pl.ds(0, middle), pl.ds(middle, depth - middle)
        self.pairs, self.first, self.second = {}, {}, []

    def put(self, first, last, row, size, value, skip=0):
        value = value.astype(BF)
        each = value.shape[0] // (2 * (last - first))
        for k in range(first, last):
            for c in range(2):
                start = (2 * (k - first) + c) * each + skip
                for quarter in range(4):
                    self.g[c, k, quarter // 2, quarter % 2, row : row + size, :] = value[
                        start : start + size, quarter * LANES : (quarter + 1) * LANES
                    ]

    def pair(self, first, last):
        here = self.place
        span = pl.ds(first, last - first)
        self.pairs[first] = self.copies.start(
            self.g.at[1 - here.core, span], self.rc.at[span], here.partner
        )

    def joint(self, k, gy, gx, rows):
        own = self.g[self.place.core, k, gy, gx, rows].astype(F32)
        return (own + self.rc[k, gy, gx, rows].astype(F32)).astype(BF)

    def step1(self, first, last):
        here = self.place
        for k in range(first, last):
            if k in self.pairs:
                self.pairs[k].wait()
            for other in range(2):
                self.sx[k, other] = self.joint(k, other, 1 - here.gx, self.low)
                self.sy[k, other] = self.joint(k, 1 - here.gy, other, self.high)
        span = pl.ds(first, last - first)
        self.first[first] = [
            self.copies.start(self.sx.at[span], self.r1x.at[span], here.x_peer),
            self.copies.start(self.sy.at[span], self.r1y.at[span], here.y_peer),
        ]
        for k in range(first, last):
            for other in range(2):
                self.ox[k, other] = self.joint(k, other, here.gx, self.low)
                self.oy[k, other] = self.joint(k, here.gy, other, self.high)

    def step2(self, first, last):
        here = self.place
        wait_all(self.first[first])
        for k in range(first, last):
            self.b0[k] = (
                self.ox[k, 1 - here.gy].astype(F32) + self.r1x[k, 1 - here.gy].astype(F32)
            ).astype(BF)
            self.b1[k] = (
                self.oy[k, 1 - here.gx].astype(F32) + self.r1y[k, 1 - here.gx].astype(F32)
            ).astype(BF)
        span = pl.ds(first, last - first)
        self.second += [
            self.copies.start(self.b0.at[span], self.r2y.at[span], here.y_peer),
            self.copies.start(self.b1.at[span], self.r2x.at[span], here.x_peer),
        ]

    def along(self):
        here = self.place
        wait_all(self.second)
        for k in range(here.zs):
            self.c[k, self.low] = (
                self.ox[k, here.gy].astype(F32)
                + self.r1x[k, here.gy].astype(F32)
                + self.r2y[k].astype(F32)
            ).astype(BF)
            self.c[k, self.high] = (
                self.oy[k, here.gx].astype(F32)
                + self.r1y[k, here.gx].astype(F32)
                + self.r2x[k].astype(F32)
            ).astype(BF)
        self.moves = []
        for step in range(here.zs - 1, 0, -1):
            there = flipped(here.z, step)
            self.moves.append(
                self.copies.start(
                    self.c.at[there],
                    self.r3.at[step - 1],
                    {"group": here.gi, "patch": there * 2 + here.core},
                )
            )

    def share(self):
        here = self.place
        wait_all(self.moves)
        total = self.c[here.z].astype(F32)
        for step in range(1, here.zs):
            total += self.r3[step - 1].astype(F32)
        self.f[here.gi] = total.astype(BF)
        mine = self.f.at[here.gi]
        self.moves = [self.copies.start(mine, mine, member) for member in here.members]

    def finish(self, out):
        wait_all(self.moves)
        out[...] = self.f[...]


class GainSum:
    def __init__(self, copies, refs, place):
        self.copies, self.place = copies, place
        self.own, self.got = refs

    def send(self, order, first, devices):
        self.order, self.first = order, first
        self.moves = [
            self.copies.start(self.own.at[order], self.got.at[first + slot], device)
            for slot, device in enumerate(devices)
        ]

    def gather(self):
        wait_all(self.moves)
        total = self.own[self.order]
        for slot in range(len(self.moves)):
            total += self.got[self.first + slot]
        return total

    def start(self, gains):
        for row in range(2):
            for quarter in range(4):
                line = 4 * row + quarter
                self.own[0, line : line + 1, :] = gains[
                    row : row + 1, quarter * LANES : (quarter + 1) * LANES
                ]
        self.send(0, 0, [self.place.partner])

    def members(self):
        self.own[1] = self.gather()
        self.send(1, 1, self.place.members)

    def along(self):
        here = self.place
        self.own[2] = self.gather()
        chips = [flipped(here.z, step) for step in range(1, here.zs)]
        self.send(
            2, 4, [{"group": here.gi, "patch": chip * 2 + here.core} for chip in chips]
        )

    def finish(self, out):
        out[...] = self.gather()


COUNT_SHARES = 15


def kernel(sizes, *refs):
    n_group, n_patch, padded, tile, tile_edges, fused, depths = sizes
    refs = list(refs)

    def take(count):
        got = refs[:count]
        del refs[:count]
        return got

    stored = take(14)
    edge_out, node_out = take(2)
    sums = take(4 + len(parts_of(depths[0])) if fused else 5)
    loaded = take(14)
    node, list_in, send_tiles, recv_tiles, edge, w_ei, w_eo, gain_e = loaded[:8]
    w_ni, w_no, gain_n, node_cot, edge_cot, count = loaded[8:]
    edge_grad, node_grad = (edge_out, node_out) if fused else take(2)
    load_sems, store_sems = take(2)
    send_col, send_row, recv_col, recv_row, list_col, list_row = take(6)
    outgoing, incoming, spread, returned = take(4)
    x_s, x_r, e_first, hidden, normed, inverse, message, joined = take(8)
    n_hidden, n_first, g_second, g_first, acc, gj, ge_second, ge_first, gs, gr, gains = take(11)
    recv_hot, recv_turned, send_hot = take(3) if fused else [None] * 3
    send_sems, recv_sems = take(2)
    nodes, width = node.shape
    edges = edge.shape[0]
    halo = n_patch * padded
    place = Place(n_patch)
    gi, p = place.gi, place.p
    copies = Copies(send_sems, recv_sems)
    barrier = pltpu.get_barrier_semaphore()
    if fused:
        others = [flipped(p, d) for d in range(n_patch - 1, 0, -1)]
    else:
        others = [lax.rem(p + d, n_patch) for d in range(1, n_patch)]
    peers = [{"group": gi, "patch": other} for other in others]
    greeted = list(peers)
    if fused:
        greeted += place.members
    for peer in greeted:
        pl.semaphore_signal(barrier, inc=1, device_id=peer, device_id_type=MESH)
    loads = [
        pltpu.make_async_copy(source, target, load_sems.at[order])
        for order, (source, target) in enumerate(zip(stored, loaded))
    ]
    first = (1, 0, 2, 3) if fused else range(len(loads))
    for order in first:
        loads[order].start()

    def column_of(line, column):
        for order in range(column.shape[0] // LANES):
            span = slice(order * LANES, (order + 1) * LANES)
            wide = jnp.broadcast_to(line[:, span].astype(F32), (8, LANES))
            column[span, :] = jnp.transpose(wide)[:, :1].astype(jnp.int32)

    loads[1].wait()
    for order in range(len(loads)):
        if order not in first:
            loads[order].start()
    list_row[...] = list_in[...]
    column_of(list_row, list_col)
    loads[0].wait()
    chosen = dot(hot(list_col[:halo, :], (halo, nodes), 1, 0), node[...]).astype(BF)
    outgoing[...] = chosen.reshape(n_patch, padded, width)
    pl.semaphore_wait(barrier, len(greeted))
    moving = [
        copies.start(outgoing.at[other], incoming.at[p], peer)
        for other, peer in zip(others, peers)
    ]
    incoming[p] = outgoing[p]
    gains[...] = jnp.zeros_like(gains)

    loads[2].wait()
    loads[3].wait()
    for tiles, column, line in ((send_tiles, send_col, send_row), (recv_tiles, recv_col, recv_row)):
        turned = jnp.transpose(tiles[...].astype(F32)).astype(jnp.int32)
        for order in range(line.shape[1] // LANES):
            span = slice(order * LANES, (order + 1) * LANES)
            column[span, :] = turned[:, order : order + 1]
            line[:, span] = tiles[order : order + 1, :]

    loads[4].wait()
    loads[5].wait()

    def rows_of(k, size=tile):
        return pl.ds(k * size if isinstance(k, int) else pl.multiple_of(k * size, size), size)

    long = 2 * tile if fused and edges % (2 * tile) == 0 and nodes % (2 * tile) == 0 else tile

    edge_tiles = edges // tile

    @pl.loop(0, edges // long, unroll=fused)
    def _(k):
        rows = rows_of(k, long)
        chosen = hot(recv_col[rows, :], (long, nodes), 1, 0)
        if fused:
            recv_hot[rows, :] = chosen
        latent = dot(chosen, node[...]).astype(BF)
        x_r[rows, :] = latent
        e_first[rows, :] = dot(edge[rows, :], w_ei[:width, :]) + dot(latent, w_ei[2 * width :, :])


    @pl.loop(0, edges // long, unroll=fused)
    def _(k):
        rows = rows_of(k, long)
        x_s[rows, :] = dot(hot(send_col[rows, :], (long, nodes), 1, 0), node[...]).astype(BF)

    loads[8].wait()

    @pl.loop(0, nodes // long, unroll=fused)
    def _(k):
        rows = rows_of(k, long)
        n_first[rows, :] = dot(node[rows, :], w_ni[:width, :])

    def recv_rows(k):
        if fused:
            return recv_turned[rows_of(k, long), :]
        return hot(recv_row[...], (long, edges), 0, k * long)

    def send_halo(k):
        if fused:
            return send_hot[rows_of(k), :]
        return hot(send_col[rows_of(k), :], (tile, halo), 1, nodes)

    if fused:
        for k in range(nodes // long):
            recv_turned[rows_of(k, long), :] = hot(recv_row[...], (long, edges), 0, k * long)
        for k in range(edge_tiles):
            rows = rows_of(k)
            send_hot[rows, :] = hot(send_col[rows, :], (tile, halo), 1, nodes)
    for load in loads[6:8] + loads[9:]:
        load.wait()
    wait_all(moving)

    def live_of(k, size=tile):
        slot = lax.broadcasted_iota(jnp.int32, (size, 1), 0) + k * size
        return jnp.where(slot < count[...] * tile_edges, 1.0, 0.0)


    def edge_first(k, _):
        rows = rows_of(k)
        latent = dot(send_halo(k), incoming[...].reshape(halo, width))
        latent = x_s[rows, :] + latent.astype(BF)
        x_s[rows, :] = latent
        return e_first[rows, :] + dot(latent, w_ei[width : 2 * width, :])

    def edge_hidden(k, first):
        rows = rows_of(k)
        active, slope = silu_pair(first)
        e_first[rows, :] = slope
        hid = active.astype(BF)
        hidden[rows, :] = hid
        return dot(hid, w_eo[...])

    def edge_message(k, second):
        rows = rows_of(k)
        norm, inv = normalize(second, live_of(k))
        normed[rows, :] = norm
        inverse[rows, :] = inv
        message[rows, :] = (gain_e[...] * norm).astype(BF)

    staggered(edge_tiles, (edge_first, edge_hidden, edge_message), unrolled=fused)

    def node_first(k, _):
        rows = rows_of(k, long)
        got = dot(recv_rows(k), message[...]).astype(BF)
        joined[rows, :] = got
        return n_first[rows, :] + dot(got, w_ni[width:, :])

    def node_hidden(k, first):
        rows = rows_of(k, long)
        active, slope = silu_pair(first)
        hid = active.astype(BF)
        n_hidden[rows, :] = hid
        return (slope, dot(hid, w_no[...]))

    def node_second(k, held):
        slope, second = held
        rows = rows_of(k, long)
        norm, inv = normalize(second)
        up = node_cot[rows, :].astype(F32)
        second, total = normalize_back(up * gain_n[...], norm, inv)
        gains[1:2, :] += total
        g_second[rows, :] = second
        return (slope, dot_rt(second, w_no[...]))

    def node_back(k, held):
        slope, grad = held
        g_first[rows_of(k, long), :] = (grad * slope).astype(BF)

    staggered(nodes // long, (node_first, node_hidden, node_second, node_back), unrolled=fused)

    def node_message():
        @pl.loop(0, nodes // long, unroll=fused)
        def _(k):
            rows = rows_of(k, long)
            gj[rows, :] = dot_rt(g_first[rows, :], w_ni[width:, :]).astype(BF)

    def edge_taken(k, _):
        if fused:
            return dot(recv_hot[rows_of(k), :], gj[...])
        return dot(hot(recv_col[rows_of(k), :], (tile, nodes), 1, 0), gj[...])

    def edge_second(k, taken):
        rows = rows_of(k)
        norm = normed[rows, :]
        grad = edge_cot[rows, :].astype(F32) + taken
        second, total = normalize_back(grad * gain_e[...], norm, inverse[rows, :])
        gains[0:1, :] += total
        ge_second[rows, :] = second
        return dot_rt(second, w_eo[...])

    def edge_back(k, grad):
        rows = rows_of(k)
        ge_first[rows, :] = (grad * e_first[rows, :]).astype(BF)

    edge_stages = (edge_taken, edge_second, edge_back)
    moving = []

    def send_rows_back():
        @pl.loop(0, edges // long, unroll=fused)
        def _(k):
            rows = rows_of(k, long)
            gs[rows, :] = dot_rt(ge_first[rows, :], w_ei[width : 2 * width, :]).astype(BF)

    def send_back():
        back = dot(hot(send_row[...], (halo, edges), 0, nodes), ge_first[...]).astype(BF)
        back = dot_rt(back, w_ei[width : 2 * width, :]).astype(BF)
        spread[...] = back.reshape(n_patch, padded, width)
        moving.extend(
            copies.start(spread.at[other], returned.at[p], peer)
            for other, peer in zip(others, peers)
        )
        returned[p] = spread[p]

    def rows_product(sources, start, stop, right):
        parts = []
        for order, source in enumerate(sources):
            low = max(start, order * width) - order * width
            high = min(stop, (order + 1) * width) - order * width
            if low < high:
                parts.append(dot_lt(source[:, low:high], right))
        return parts[0] if len(parts) == 1 else jnp.concatenate(parts, axis=0)

    if fused:
        zs = place.zs
        half = zs // 2
        d_ei, d_eo, d_ni, d_no = depths
        e_depths = parts_of(d_ei)
        red_no, red_ni, red_o, *red_e = [
            Reduction(copies, take(COUNT_SHARES), place) for _ in range(3 + len(e_depths))
        ]
        gain_sum = GainSum(copies, take(2), place)
        red_no.put(0, zs, 0, d_no, dot_lt(n_hidden[...], g_second[...]))
        red_no.pair(0, zs)
        for first in (0, half):
            last = first + half
            value = rows_product((node, joined), 2 * first * d_ni, 2 * last * d_ni, g_first[...])
            red_ni.put(first, last, 0, d_ni, value)
            red_ni.pair(first, last)
            if first == 0:
                node_message()
                red_no.step1(0, zs)
        red_ni.step1(0, half)
        staggered(edge_tiles, edge_stages, hooks={2: lambda: red_ni.step1(half, zs)})
        send_back()
        red_no.step2(0, zs)
        gains[0:1, :] = gains[0:1, :] / gain_e[...]
        gains[1:2, :] = gains[1:2, :] / gain_n[...]
        gain_sum.start(gains)
        red_o.put(0, zs, 0, d_eo, dot_lt(hidden[...], ge_second[...]))
        red_o.pair(0, zs)
        red_ni.step2(0, half)
        for first in (0, half):
            last = first + half
            value = rows_product(
                (edge, x_s, x_r), 2 * first * d_ei, 2 * last * d_ei, ge_first[...]
            )
            skip = 0
            for red, depth in zip(red_e, e_depths):
                red.put(first, last, 0, depth, value, skip=skip)
                skip += depth
            for red in red_e:
                red.pair(first, last)
            if first == 0:
                red_o.step1(0, zs)
                gain_sum.members()
        red_ni.step2(half, zs)
        send_rows_back()
        for red in red_e:
            red.step1(0, zs)
    else:
        o_ei, o_eo, o_ni, o_no, o_gain = sums
        o_ni[:width, :] = dot_lt(node[...], g_first[...])
        o_ni[width:, :] = dot_lt(joined[...], g_first[...])
        o_no[...] = dot_lt(n_hidden[...], g_second[...])
        node_message()
        staggered(edge_tiles, edge_stages, unrolled=False)
        o_ei[:width, :] = dot_lt(edge[...], ge_first[...])
        o_ei[width : 2 * width, :] = dot_lt(x_s[...], ge_first[...])
        o_ei[2 * width :, :] = dot_lt(x_r[...], ge_first[...])
        o_eo[...] = dot_lt(hidden[...], ge_second[...])
        o_gain[...] = gains[...]
        o_gain[0:1, :] = gains[0:1, :] / gain_e[...]
        o_gain[1:2, :] = gains[1:2, :] / gain_n[...]

    if not fused:
        send_back()
        send_rows_back()

    @pl.loop(0, edges // long, unroll=fused)
    def _(k):
        rows = rows_of(k, long)
        gr[rows, :] = dot_rt(ge_first[rows, :], w_ei[2 * width :, :]).astype(BF)


    @pl.loop(0, edges // long, unroll=fused)
    def _(k):
        rows = rows_of(k, long)
        edge_grad[rows, :] = (
            live_of(k, long) * edge_cot[rows, :].astype(F32)
            + dot_rt(ge_first[rows, :], w_ei[:width, :])
        ).astype(BF)

    stores = []
    if not fused:
        stores.append(pltpu.make_async_copy(edge_grad, edge_out, store_sems.at[0]))
        stores[0].start()

    def gather_back(k):
        rows = rows_of(k, long)
        acc[rows, :] = (
            node_cot[rows, :].astype(F32)
            + dot_rt(g_first[rows, :], w_ni[:width, :])
            + dot(hot(send_row[...], (long, edges), 0, k * long), gs[...])
            + dot(recv_rows(k), gr[...])
        )

    gathers = nodes // long
    if fused:
        red_no.along()
        red_ni.along()
        red_o.step2(0, zs)
        gain_sum.along()
    pl.loop(0, gathers // 2, unroll=fused)(gather_back)
    if fused:
        red_e[0].step2(0, zs)
    pl.loop(gathers // 2, gathers, unroll=fused)(gather_back)
    if fused:
        for red in red_e[1:]:
            red.step2(0, zs)
        red_o.along()
        for red in red_e:
            red.along()
        red_no.share()
        red_ni.share()
    wait_all(moving)

    @pl.loop(0, nodes // tile, unroll=fused)
    def _(k):
        rows = rows_of(k)
        node_grad[rows, :] = (
            acc[rows, :]
            + dot(
                hot(list_row[:, :halo], (tile, halo), 0, k * tile),
                returned[...].reshape(halo, width),
            )
        ).astype(BF)

    if not fused:
        stores.append(pltpu.make_async_copy(node_grad, node_out, store_sems.at[1]))
        stores[1].start()
    if fused:
        red_o.share()
        for red in red_e:
            red.share()
        red_no.finish(sums[0])
        red_ni.finish(sums[1])
        red_o.finish(sums[2])
        gain_sum.finish(sums[3])
        for red, out in zip(red_e, sums[4:]):
            red.finish(out)
    for store in stores:
        store.wait()


def closing(factor, depths, *refs):
    refs = list(refs)
    edge_in, node_in, sum_no, sum_ni, sum_o, sum_gain = refs[:6]
    outs, holds, store_sems = refs[-15:-7], refs[-7:-1], refs[-1]
    sum_e = refs[6:-15]
    o_ei, o_eo, o_gain_e, o_ni, o_no, o_gain_n = holds
    d_ei, d_eo, d_ni, d_no = depths
    stores = [
        pltpu.make_async_copy(source, out, store_sems.at[order])
        for order, (source, out) in enumerate(zip((edge_in, node_in) + tuple(holds), outs))
    ]
    stores[0].start()
    stores[1].start()
    for quarter in range(4):
        span = slice(quarter * LANES, (quarter + 1) * LANES)
        row = 0
        for part in sum_e:
            o_ei[row : row + part.shape[1], span] = part[quarter].astype(F32) * factor
            row += part.shape[1]
    stores[2].start()
    for quarter in range(4):
        span = slice(quarter * LANES, (quarter + 1) * LANES)
        o_ni[:, span] = sum_ni[quarter].astype(F32) * factor
        o_no[:, span] = sum_no[quarter].astype(F32) * factor
        o_eo[:, span] = sum_o[quarter].astype(F32) * factor
    for order in (3, 5, 6):
        stores[order].start()
    piece = o_gain_e.shape[1]
    p = lax.axis_index("patch")
    share = LANES // piece
    for row, hold in ((0, o_gain_e), (4, o_gain_n)):
        line = sum_gain[pl.ds(row + lax.div(p, share), 1), :]
        own = jnp.zeros((1, piece), F32)
        for part in range(share):
            own += jnp.where(lax.rem(p, share) == part, line[:, part * piece : (part + 1) * piece], 0.0)
        hold[...] = own * factor
    for order in (4, 7):
        stores[order].start()
    for store in stores:
        store.wait()


def reduction_scratch(zs, depth):
    middle = depth // 2 // PACK * PACK
    rest = depth - middle
    shapes = (
        (2, zs, 2, 2, depth),
        (zs, 2, 2, depth),
        (zs, 2, middle),
        (zs, 2, rest),
        (zs, 2, middle),
        (zs, 2, rest),
        (zs, 2, middle),
        (zs, 2, rest),
        (zs, middle),
        (zs, rest),
        (zs, rest),
        (zs, middle),
        (zs, depth),
        (zs - 1, depth),
        (4, depth),
    )
    return [pltpu.VMEM(shape + (LANES,), BF) for shape in shapes]


def local(
    n_group,
    n_patch,
    node_tape,
    edge_tape,
    node_cot,
    edge_cot,
    w_edge_in,
    w_edge_out,
    gain_edge,
    w_node_in,
    w_node_out,
    gain_node,
    senders,
    receivers,
    tile_count,
    send_rows,
):
    nodes, width = node_tape.shape[1:]
    edges = edge_tape.shape[1]
    listed = send_rows.shape[1]
    peer_rows = listed // n_patch
    padded = -(-peer_rows // PACK) * PACK
    halo = n_patch * padded
    tile = min(2 * LANES, nodes, edges)
    factor = float(n_group * n_patch * edges) ** (-0.5)

    if padded != peer_rows:
        beyond = senders - nodes
        beyond = beyond // peer_rows * padded + beyond % peer_rows
        senders = jnp.where(senders < nodes, senders, nodes + beyond)
        send_rows = jnp.pad(
            send_rows.reshape(n_patch, peer_rows),
            ((0, 0), (0, padded - peer_rows)),
            constant_values=-1,
        ).reshape(1, halo)
    slots = -(-halo // LANES) * LANES
    if slots != halo:
        send_rows = jnp.pad(send_rows, ((0, 0), (0, slots - halo)), constant_values=-1)

    def lane_rows(index):
        rows = -(-index.size // LANES)
        full = -(-rows // 8) * 8
        if index.shape == (full, LANES):
            return index
        return jnp.pad(index.reshape(-1), (0, full * LANES - index.size)).reshape(full, LANES)

    weights = (w_edge_in, w_edge_out, w_node_in, w_node_out)
    depths = [w.shape[0] // n_patch for w in weights]
    zs = n_patch // 2
    fused = (
        n_group == 4
        and n_patch % 4 == 0
        and n_patch & (n_patch - 1) == 0
        and width == 4 * LANES
        and all(d % PACK == 0 and 2 * d % LANES == 0 for d in depths)
        and min(depths) >= 2 * PACK
        and LANES * n_patch % width == 0
    )
    operands = (
        node_tape[0],
        send_rows,
        lane_rows(senders),
        lane_rows(receivers),
        edge_tape[0],
        w_edge_in,
        w_edge_out,
        gain_edge[None],
        w_node_in,
        w_node_out,
        gain_node[None],
        node_cot[0],
        edge_cot[0],
        tile_count[None],
    )
    scratch = [pltpu.VMEM(operand.shape, operand.dtype) for operand in operands]
    if not fused:
        scratch += [pltpu.VMEM((edges, width), BF), pltpu.VMEM((nodes, width), BF)]
    scratch += [
        pltpu.SemaphoreType.DMA((len(operands),)),
        pltpu.SemaphoreType.DMA((2,)),
    ]
    for length in (edges, edges, slots):
        scratch += [pltpu.VMEM((length, 1), jnp.int32), pltpu.VMEM((1, length), jnp.int32)]
    scratch += [pltpu.VMEM((n_patch, padded, width), BF)] * 4
    by_edge, by_node = pltpu.VMEM((edges, width), BF), pltpu.VMEM((nodes, width), BF)
    wide_edge, wide_node = pltpu.VMEM((edges, width), F32), pltpu.VMEM((nodes, width), F32)
    scratch += [by_edge, by_edge, wide_edge, by_edge, wide_edge, pltpu.VMEM((edges, 1), F32)]
    scratch += [by_edge, by_node]
    scratch += [by_node, wide_node, by_node, by_node, wide_node, by_node]
    scratch += [by_edge, by_edge, by_edge, by_edge, pltpu.VMEM((PACK, width), F32)]
    if fused:
        scratch += [pltpu.VMEM(shape, BF) for shape in ((edges, nodes), (nodes, edges), (edges, halo))]
    n_copies = 2 * (n_patch - 1)
    d_ei, d_eo, d_ni, d_no = depths
    reductions = []
    if fused:
        e_depths = parts_of(d_ei)
        shared = [d_no, d_ni, d_eo] + e_depths
        pairs, halves = [1, 2, 1] + [2] * len(e_depths), [1, 2, 1] + [1] * len(e_depths)
        for depth, pair, half in zip(shared, pairs, halves):
            reductions += reduction_scratch(zs, depth)
            n_copies += pair + 4 * half + zs - 1 + 3
        reductions += [pltpu.VMEM((3, 8, LANES), F32), pltpu.VMEM((3 + zs, 8, LANES), F32)]
        n_copies += 3 + zs
        summed_shapes = [pltpu.VMEM((4, depth, LANES), BF) for depth in shared]
        summed_shapes.insert(3, pltpu.VMEM((8, LANES), F32))
    else:
        summed_shapes = [jax.ShapeDtypeStruct((w.shape[0], width), F32) for w in weights]
        summed_shapes += [jax.ShapeDtypeStruct((PACK, width), F32)]
    in_flight = n_copies // 3 + 1 if fused else n_copies
    scratch += [pltpu.SemaphoreType.DMA((in_flight,)), pltpu.SemaphoreType.DMA((n_copies,))]
    scratch += reductions

    vmem = pl.BlockSpec(memory_space=pltpu.VMEM)
    big = pltpu.VMEM if fused else jax.ShapeDtypeStruct
    anywhere = pl.BlockSpec(memory_space=pl.ANY)
    sizes = (n_group, n_patch, padded, tile, senders.shape[1], fused, depths)
    edge_grad, node_grad, *sums = pl.pallas_call(
        functools.partial(kernel, sizes),
        out_shape=[big((edges, width), BF), big((nodes, width), BF)] + summed_shapes,
        in_specs=[anywhere] * len(operands),
        out_specs=[vmem if fused else anywhere] * 2 + [vmem] * len(summed_shapes),
        scratch_shapes=scratch,
        compiler_params=pltpu.CompilerParams(
            collective_id=0, has_side_effects=True, vmem_limit_bytes=54 * 1024 * 1024
        ),
    )(*operands)
    if fused:
        piece = width // n_patch
        rows_out = [jax.ShapeDtypeStruct((depth, width), F32) for depth in depths]
        gain_out = jax.ShapeDtypeStruct((1, piece), F32)
        o_ei, o_eo, o_ni, o_no = rows_out
        edge_grad, node_grad, o_ei, o_eo, gain_e, o_ni, o_no, gain_n = pl.pallas_call(
            functools.partial(closing, factor, depths),
            out_shape=[
                jax.ShapeDtypeStruct((edges, width), BF),
                jax.ShapeDtypeStruct((nodes, width), BF),
                o_ei,
                o_eo,
                gain_out,
                o_ni,
                o_no,
                gain_out,
            ],
            in_specs=[vmem] * (2 + len(sums)),
            out_specs=[anywhere] * 8,
            scratch_shapes=[
                pltpu.VMEM((d_ei, width), F32),
                pltpu.VMEM((d_eo, width), F32),
                pltpu.VMEM((1, piece), F32),
                pltpu.VMEM((d_ni, width), F32),
                pltpu.VMEM((d_no, width), F32),
                pltpu.VMEM((1, piece), F32),
                pltpu.SemaphoreType.DMA((8,)),
            ],
            compiler_params=pltpu.CompilerParams(vmem_limit_bytes=16 * 1024 * 1024),
        )(*[pltpu.with_memory_space_constraint(x, pltpu.VMEM) for x in (edge_grad, node_grad, *sums)])
        return (
            edge_grad[None],
            node_grad[None],
            o_ei,
            o_eo,
            gain_e.reshape(piece),
            o_ni,
            o_no,
            gain_n.reshape(piece),
        )
    p_ei, p_eo, p_ni, p_no, p_gain = sums

    def summed(value):
        part = lax.psum_scatter(value, "patch", scatter_dimension=0, tiled=True)
        return lax.psum(part.astype(BF), "group").astype(F32) * factor

    return (
        edge_grad[None],
        node_grad[None],
        summed(p_ei),
        summed(p_eo),
        summed(p_gain[0]),
        summed(p_ni),
        summed(p_no),
        summed(p_gain[1]),
    )


def solution(mesh):
    member = P("group", "patch", None)
    placed = (member,) * 4 + (P(),) * 6
    placed += (P("patch", None), P("patch", None), P("patch"), P("patch", None))
    rows = P("patch", None)
    return jax.shard_map(
        functools.partial(local, mesh.shape["group"], mesh.shape["patch"]),
        mesh=mesh,
        in_specs=placed,
        out_specs=(member, member, rows, rows, P("patch"), rows, rows, P("patch")),
        check_vma=False,
    )
```

```python
import functools

import jax
import jax.numpy as jnp
from jax import lax
from jax.experimental import pallas as pl
from jax.experimental.pallas import tpu as pltpu
from jax.sharding import PartitionSpec as P

epsilon = 1e-05
BF = jnp.bfloat16
F32 = jnp.float32
LANES = 128
PACK = 16
MESH = pl.DeviceIdType.MESH


def dot(left, right):
    return jnp.dot(left, right, preferred_element_type=F32)


def dot_rt(left, right):
    return lax.dot_general(left, right, (((1,), (1,)), ((), ())), preferred_element_type=F32)


def dot_lt(left, right):
    return lax.dot_general(left, right, (((0,), (0,)), ((), ())), preferred_element_type=F32)


def silu_pair(values):
    squash = 0.5 * jnp.tanh(0.5 * values) + 0.5
    active = values * squash
    return (active, squash + active * (1.0 - squash))


def normalize(values, live=None):
    centred = values - jnp.mean(values, axis=1, keepdims=True)
    inverse = lax.rsqrt(jnp.mean(centred * centred, axis=1, keepdims=True) + epsilon)
    if live is not None:
        inverse = inverse * live
    return (centred * inverse, inverse)


def normalize_back(upstream, normed, inverse):
    product = upstream * normed
    second = inverse * (
        upstream
        - jnp.mean(upstream, axis=1, keepdims=True)
        - normed * jnp.mean(product, axis=1, keepdims=True)
    )
    return (second.astype(BF), jnp.sum(product, axis=0, keepdims=True))


def hot(index, shape, axis, base):
    return jnp.where(lax.broadcasted_iota(jnp.int32, shape, axis) + base == index, 1.0, 0.0).astype(
        BF
    )


class Waited:
    def __init__(self, copies, copy, slot):
        self.copies, self.copy, self.slot = copies, copy, slot

    def wait(self):
        self.copy.wait()
        self.copies.free.append(self.slot)


class Copies:
    def __init__(self, send_sems, recv_sems):
        self.send_sems, self.recv_sems, self.used = send_sems, recv_sems, 0
        self.free = list(range(send_sems.shape[0]))[::-1]

    def start(self, source, target, device):
        slot = self.free.pop()
        copy = pltpu.make_async_remote_copy(
            src_ref=source,
            dst_ref=target,
            send_sem=self.send_sems.at[slot],
            recv_sem=self.recv_sems.at[self.used],
            device_id=device,
            device_id_type=MESH,
        )
        self.used += 1
        copy.start()
        return Waited(self, copy, slot)


def wait_all(copies):
    for copy in copies:
        copy.wait()


def staggered(count, stages, hooks=None, unrolled=True):
    if not unrolled:

        @pl.loop(0, count)
        def _(k):
            held = None
            for stage in stages:
                held = stage(k, held)

        return
    held = {}
    for step in range(count + len(stages) - 1):
        for order in range(len(stages)):
            k = step - order
            if 0 <= k < count:
                held[k] = stages[order](k, held.get(k))
        if hooks and step in hooks:
            hooks[step]()


def flipped(index, bits):
    for place in range(bits.bit_length()):
        if bits >> place & 1:
            index = index + (1 - 2 * lax.rem(lax.div(index, 1 << place), 2)) * (1 << place)
    return index


class Place:
    def __init__(self, n_patch):
        self.gi = lax.axis_index("group")
        self.p = lax.axis_index("patch")
        self.core = lax.rem(self.p, 2)
        self.z = lax.div(self.p, 2)
        self.zs = n_patch // 2
        self.partner = {"group": self.gi, "patch": self.p + 1 - 2 * self.core}
        self.gx, self.gy = lax.rem(self.gi, 2), lax.div(self.gi, 2)
        flip_x, flip_y = 1 - 2 * self.gx, 2 - 4 * self.gy
        self.members = [
            {"group": self.gi + flip, "patch": self.p} for flip in (flip_x, flip_y, flip_x + flip_y)
        ]
        self.x_peer, self.y_peer = self.members[:2]


class Reduction:
    def __init__(self, copies, refs, place):
        self.copies, self.place = copies, place
        self.g, self.rc, self.sx, self.sy, self.ox, self.oy = refs[:6]
        self.r1x, self.r1y, self.b0, self.b1, self.r2x, self.r2y, self.c, self.r3, self.f = refs[6:]
        depth, middle = self.c.shape[1], self.sx.shape[2]
        self.low, self.high = pl.ds(0, middle), pl.ds(middle, depth - middle)
        self.pairs, self.first, self.second = {}, {}, []

    def put(self, first, last, row, size, value, skip=0):
        value = value.astype(BF)
        each = value.shape[0] // (2 * (last - first))
        for k in range(first, last):
            for c in range(2):
                start = (2 * (k - first) + c) * each + skip
                for quarter in range(4):
                    self.g[c, k, quarter // 2, quarter % 2, row : row + size, :] = value[
                        start : start + size, quarter * LANES : (quarter + 1) * LANES
                    ]

    def pair(self, first, last):
        here = self.place
        span = pl.ds(first, last - first)
        self.pairs[first] = self.copies.start(
            self.g.at[1 - here.core, span], self.rc.at[span], here.partner
        )

    def joint(self, k, gy, gx, rows):
        own = self.g[self.place.core, k, gy, gx, rows].astype(F32)
        return (own + self.rc[k, gy, gx, rows].astype(F32)).astype(BF)

    def step1(self, first, last):
        here = self.place
        for k in range(first, last):
            if k in self.pairs:
                self.pairs[k].wait()
            for other in range(2):
                self.sx[k, other] = self.joint(k, other, 1 - here.gx, self.low)
                self.sy[k, other] = self.joint(k, 1 - here.gy, other, self.high)
        span = pl.ds(first, last - first)
        self.first[first] = [
            self.copies.start(self.sx.at[span], self.r1x.at[span], here.x_peer),
            self.copies.start(self.sy.at[span], self.r1y.at[span], here.y_peer),
        ]
        for k in range(first, last):
            for other in range(2):
                self.ox[k, other] = self.joint(k, other, here.gx, self.low)
                self.oy[k, other] = self.joint(k, here.gy, other, self.high)

    def step2(self, first, last):
        here = self.place
        wait_all(self.first[first])
        for k in range(first, last):
            self.b0[k] = (
                self.ox[k, 1 - here.gy].astype(F32) + self.r1x[k, 1 - here.gy].astype(F32)
            ).astype(BF)
            self.b1[k] = (
                self.oy[k, 1 - here.gx].astype(F32) + self.r1y[k, 1 - here.gx].astype(F32)
            ).astype(BF)
        span = pl.ds(first, last - first)
        self.second += [
            self.copies.start(self.b0.at[span], self.r2y.at[span], here.y_peer),
            self.copies.start(self.b1.at[span], self.r2x.at[span], here.x_peer),
        ]

    def along(self):
        here = self.place
        wait_all(self.second)
        for k in range(here.zs):
            self.c[k, self.low] = (
                self.ox[k, here.gy].astype(F32)
                + self.r1x[k, here.gy].astype(F32)
                + self.r2y[k].astype(F32)
            ).astype(BF)
            self.c[k, self.high] = (
                self.oy[k, here.gx].astype(F32)
                + self.r1y[k, here.gx].astype(F32)
                + self.r2x[k].astype(F32)
            ).astype(BF)
        self.moves = []
        for step in range(here.zs - 1, 0, -1):
            there = flipped(here.z, step)
            self.moves.append(
                self.copies.start(
                    self.c.at[there],
                    self.r3.at[step - 1],
                    {"group": here.gi, "patch": there * 2 + here.core},
                )
            )

    def share(self):
        here = self.place
        wait_all(self.moves)
        total = self.c[here.z].astype(F32)
        for step in range(1, here.zs):
            total += self.r3[step - 1].astype(F32)
        self.f[here.gi] = total.astype(BF)
        mine = self.f.at[here.gi]
        self.moves = [self.copies.start(mine, mine, member) for member in here.members]

    def finish(self, out):
        wait_all(self.moves)
        out[...] = self.f[...]


class GainSum:
    def __init__(self, copies, refs, place):
        self.copies, self.place = copies, place
        self.own, self.got = refs

    def send(self, order, first, devices):
        self.order, self.first = order, first
        self.moves = [
            self.copies.start(self.own.at[order], self.got.at[first + slot], device)
            for slot, device in enumerate(devices)
        ]

    def gather(self):
        wait_all(self.moves)
        total = self.own[self.order]
        for slot in range(len(self.moves)):
            total += self.got[self.first + slot]
        return total

    def start(self, gains):
        for row in range(2):
            for quarter in range(4):
                line = 4 * row + quarter
                self.own[0, line : line + 1, :] = gains[
                    row : row + 1, quarter * LANES : (quarter + 1) * LANES
                ]
        self.send(0, 0, [self.place.partner])

    def members(self):
        self.own[1] = self.gather()
        self.send(1, 1, self.place.members)

    def along(self):
        here = self.place
        self.own[2] = self.gather()
        chips = [flipped(here.z, step) for step in range(1, here.zs)]
        self.send(
            2, 4, [{"group": here.gi, "patch": chip * 2 + here.core} for chip in chips]
        )

    def finish(self, out):
        out[...] = self.gather()


COUNT_SHARES = 15


def kernel(sizes, *refs):
    n_group, n_patch, padded, tile, tile_edges, fused, depths = sizes
    refs = list(refs)

    def take(count):
        got = refs[:count]
        del refs[:count]
        return got

    stored = take(14)
    edge_out, node_out = take(2)
    sums = take(6 if fused else 5)
    loaded = take(14)
    node, list_in, send_tiles, recv_tiles, edge, w_ei, w_eo, gain_e = loaded[:8]
    w_ni, w_no, gain_n, node_cot, edge_cot, count = loaded[8:]
    edge_grad, node_grad = (edge_out, node_out) if fused else take(2)
    load_sems, store_sems = take(2)
    send_col, send_row, recv_col, recv_row, list_col, list_row = take(6)
    outgoing, incoming, spread, returned = take(4)
    x_s, x_r, e_first, hidden, normed, inverse, message, joined = take(8)
    n_hidden, n_first, g_second, g_first, acc, gj, ge_second, ge_first, gs, gr, gains = take(11)
    recv_hot = take(1)[0] if fused else None
    send_sems, recv_sems = take(2)
    nodes, width = node.shape
    edges = edge.shape[0]
    halo = n_patch * padded
    place = Place(n_patch)
    gi, p = place.gi, place.p
    copies = Copies(send_sems, recv_sems)
    barrier = pltpu.get_barrier_semaphore()
    if fused:
        others = [flipped(p, d) for d in range(n_patch - 1, 0, -1)]
    else:
        others = [lax.rem(p + d, n_patch) for d in range(1, n_patch)]
    peers = [{"group": gi, "patch": other} for other in others]
    greeted = list(peers)
    if fused:
        greeted += place.members
    for peer in greeted:
        pl.semaphore_signal(barrier, inc=1, device_id=peer, device_id_type=MESH)
    loads = [
        pltpu.make_async_copy(source, target, load_sems.at[order])
        for order, (source, target) in enumerate(zip(stored, loaded))
    ]
    first = (1, 0, 2, 3) if fused else range(len(loads))
    for order in first:
        loads[order].start()

    def column_of(line, column):
        for order in range(column.shape[0] // LANES):
            span = slice(order * LANES, (order + 1) * LANES)
            wide = jnp.broadcast_to(line[:, span].astype(F32), (8, LANES))
            column[span, :] = jnp.transpose(wide)[:, :1].astype(jnp.int32)

    loads[1].wait()
    for order in range(len(loads)):
        if order not in first:
            loads[order].start()
    list_row[...] = list_in[...]
    column_of(list_row, list_col)
    loads[0].wait()
    chosen = dot(hot(list_col[:halo, :], (halo, nodes), 1, 0), node[...]).astype(BF)
    outgoing[...] = chosen.reshape(n_patch, padded, width)
    pl.semaphore_wait(barrier, len(greeted))
    moving = [
        copies.start(outgoing.at[other], incoming.at[p], peer)
        for other, peer in zip(others, peers)
    ]
    incoming[p] = outgoing[p]
    gains[...] = jnp.zeros_like(gains)

    loads[2].wait()
    loads[3].wait()
    for tiles, column, line in ((send_tiles, send_col, send_row), (recv_tiles, recv_col, recv_row)):
        turned = jnp.transpose(tiles[...].astype(F32)).astype(jnp.int32)
        for order in range(line.shape[1] // LANES):
            span = slice(order * LANES, (order + 1) * LANES)
            column[span, :] = turned[:, order : order + 1]
            line[:, span] = tiles[order : order + 1, :]

    loads[4].wait()
    loads[5].wait()

    def rows_of(k, size=tile):
        return pl.ds(k * size if isinstance(k, int) else pl.multiple_of(k * size, size), size)

    long = 2 * tile if fused and edges % (2 * tile) == 0 and nodes % (2 * tile) == 0 else tile

    edge_tiles = edges // tile

    @pl.loop(0, edges // long, unroll=fused)
    def _(k):
        rows = rows_of(k, long)
        chosen = hot(recv_col[rows, :], (long, nodes), 1, 0)
        if fused:
            recv_hot[rows, :] = chosen
        latent = dot(chosen, node[...]).astype(BF)
        x_r[rows, :] = latent
        e_first[rows, :] = dot(edge[rows, :], w_ei[:width, :]) + dot(latent, w_ei[2 * width :, :])


    @pl.loop(0, edges // long, unroll=fused)
    def _(k):
        rows = rows_of(k, long)
        x_s[rows, :] = dot(hot(send_col[rows, :], (long, nodes), 1, 0), node[...]).astype(BF)

    loads[8].wait()

    @pl.loop(0, nodes // long, unroll=fused)
    def _(k):
        rows = rows_of(k, long)
        n_first[rows, :] = dot(node[rows, :], w_ni[:width, :])

    for load in loads[6:8] + loads[9:]:
        load.wait()
    wait_all(moving)

    def live_of(k, size=tile):
        slot = lax.broadcasted_iota(jnp.int32, (size, 1), 0) + k * size
        return jnp.where(slot < count[...] * tile_edges, 1.0, 0.0)


    def edge_first(k, _):
        rows = rows_of(k)
        latent = dot(
            hot(send_col[rows, :], (tile, halo), 1, nodes), incoming[...].reshape(halo, width)
        )
        latent = x_s[rows, :] + latent.astype(BF)
        x_s[rows, :] = latent
        return e_first[rows, :] + dot(latent, w_ei[width : 2 * width, :])

    def edge_hidden(k, first):
        rows = rows_of(k)
        active, slope = silu_pair(first)
        e_first[rows, :] = slope
        hid = active.astype(BF)
        hidden[rows, :] = hid
        return dot(hid, w_eo[...])

    def edge_message(k, second):
        rows = rows_of(k)
        norm, inv = normalize(second, live_of(k))
        normed[rows, :] = norm
        inverse[rows, :] = inv
        message[rows, :] = (gain_e[...] * norm).astype(BF)

    staggered(edge_tiles, (edge_first, edge_hidden, edge_message), unrolled=fused)

    def node_first(k, _):
        rows = rows_of(k, long)
        got = dot(hot(recv_row[...], (long, edges), 0, k * long), message[...]).astype(BF)
        joined[rows, :] = got
        return n_first[rows, :] + dot(got, w_ni[width:, :])

    def node_hidden(k, first):
        rows = rows_of(k, long)
        active, slope = silu_pair(first)
        hid = active.astype(BF)
        n_hidden[rows, :] = hid
        return (slope, dot(hid, w_no[...]))

    def node_second(k, held):
        slope, second = held
        rows = rows_of(k, long)
        norm, inv = normalize(second)
        up = node_cot[rows, :].astype(F32)
        second, total = normalize_back(up * gain_n[...], norm, inv)
        gains[1:2, :] += total
        g_second[rows, :] = second
        return (slope, dot_rt(second, w_no[...]))

    def node_back(k, held):
        slope, grad = held
        g_first[rows_of(k, long), :] = (grad * slope).astype(BF)

    staggered(nodes // long, (node_first, node_hidden, node_second, node_back), unrolled=fused)

    def node_message():
        @pl.loop(0, nodes // long, unroll=fused)
        def _(k):
            rows = rows_of(k, long)
            gj[rows, :] = dot_rt(g_first[rows, :], w_ni[width:, :]).astype(BF)

    def edge_taken(k, _):
        if fused:
            return dot(recv_hot[rows_of(k), :], gj[...])
        return dot(hot(recv_col[rows_of(k), :], (tile, nodes), 1, 0), gj[...])

    def edge_second(k, taken):
        rows = rows_of(k)
        norm = normed[rows, :]
        grad = edge_cot[rows, :].astype(F32) + taken
        second, total = normalize_back(grad * gain_e[...], norm, inverse[rows, :])
        gains[0:1, :] += total
        ge_second[rows, :] = second
        return dot_rt(second, w_eo[...])

    def edge_back(k, grad):
        rows = rows_of(k)
        ge_first[rows, :] = (grad * e_first[rows, :]).astype(BF)

    edge_stages = (edge_taken, edge_second, edge_back)
    moving = []

    def send_rows_back():
        @pl.loop(0, edges // long, unroll=fused)
        def _(k):
            rows = rows_of(k, long)
            gs[rows, :] = dot_rt(ge_first[rows, :], w_ei[width : 2 * width, :]).astype(BF)

    def send_back():
        back = dot(hot(send_row[...], (halo, edges), 0, nodes), ge_first[...]).astype(BF)
        back = dot_rt(back, w_ei[width : 2 * width, :]).astype(BF)
        spread[...] = back.reshape(n_patch, padded, width)
        moving.extend(
            copies.start(spread.at[other], returned.at[p], peer)
            for other, peer in zip(others, peers)
        )
        returned[p] = spread[p]

    def rows_product(sources, start, stop, right):
        parts = []
        for order, source in enumerate(sources):
            low = max(start, order * width) - order * width
            high = min(stop, (order + 1) * width) - order * width
            if low < high:
                parts.append(dot_lt(source[:, low:high], right))
        return parts[0] if len(parts) == 1 else jnp.concatenate(parts, axis=0)

    if fused:
        zs = place.zs
        half = zs // 2
        d_ei, d_eo, d_ni, d_no = depths
        red_no, red_ni, red_ea, red_eb, red_o = [
            Reduction(copies, take(COUNT_SHARES), place) for _ in range(5)
        ]
        gain_sum = GainSum(copies, take(2), place)
        d_ea = d_ei // 2 // PACK * PACK
        red_no.put(0, zs, 0, d_no, dot_lt(n_hidden[...], g_second[...]))
        red_no.pair(0, zs)
        for first in (0, half):
            last = first + half
            value = rows_product((node, joined), 2 * first * d_ni, 2 * last * d_ni, g_first[...])
            red_ni.put(first, last, 0, d_ni, value)
            red_ni.pair(first, last)
            if first == 0:
                node_message()
                red_no.step1(0, zs)
        red_ni.step1(0, half)
        staggered(edge_tiles, edge_stages, hooks={2: lambda: red_ni.step1(half, zs)})
        send_back()
        red_no.step2(0, zs)
        gains[0:1, :] = gains[0:1, :] / gain_e[...]
        gains[1:2, :] = gains[1:2, :] / gain_n[...]
        gain_sum.start(gains)
        red_o.put(0, zs, 0, d_eo, dot_lt(hidden[...], ge_second[...]))
        red_o.pair(0, zs)
        red_ni.step2(0, half)
        for first in (0, half):
            last = first + half
            value = rows_product(
                (edge, x_s, x_r), 2 * first * d_ei, 2 * last * d_ei, ge_first[...]
            )
            red_ea.put(first, last, 0, d_ea, value)
            red_eb.put(first, last, 0, d_ei - d_ea, value, skip=d_ea)
            red_ea.pair(first, last)
            red_eb.pair(first, last)
            if first == 0:
                red_o.step1(0, zs)
                gain_sum.members()
        red_ni.step2(half, zs)
        send_rows_back()
        red_ea.step1(0, zs)
        red_eb.step1(0, zs)
    else:
        o_ei, o_eo, o_ni, o_no, o_gain = sums
        o_ni[:width, :] = dot_lt(node[...], g_first[...])
        o_ni[width:, :] = dot_lt(joined[...], g_first[...])
        o_no[...] = dot_lt(n_hidden[...], g_second[...])
        node_message()
        staggered(edge_tiles, edge_stages, unrolled=False)
        o_ei[:width, :] = dot_lt(edge[...], ge_first[...])
        o_ei[width : 2 * width, :] = dot_lt(x_s[...], ge_first[...])
        o_ei[2 * width :, :] = dot_lt(x_r[...], ge_first[...])
        o_eo[...] = dot_lt(hidden[...], ge_second[...])
        o_gain[...] = gains[...]
        o_gain[0:1, :] = gains[0:1, :] / gain_e[...]
        o_gain[1:2, :] = gains[1:2, :] / gain_n[...]

    if not fused:
        send_back()
        send_rows_back()

    @pl.loop(0, edges // long, unroll=fused)
    def _(k):
        rows = rows_of(k, long)
        gr[rows, :] = dot_rt(ge_first[rows, :], w_ei[2 * width :, :]).astype(BF)


    @pl.loop(0, edges // long, unroll=fused)
    def _(k):
        rows = rows_of(k, long)
        edge_grad[rows, :] = (
            live_of(k, long) * edge_cot[rows, :].astype(F32)
            + dot_rt(ge_first[rows, :], w_ei[:width, :])
        ).astype(BF)

    stores = []
    if not fused:
        stores.append(pltpu.make_async_copy(edge_grad, edge_out, store_sems.at[0]))
        stores[0].start()

    def gather_back(k):
        rows = rows_of(k, long)
        acc[rows, :] = (
            node_cot[rows, :].astype(F32)
            + dot_rt(g_first[rows, :], w_ni[:width, :])
            + dot(hot(send_row[...], (long, edges), 0, k * long), gs[...])
            + dot(hot(recv_row[...], (long, edges), 0, k * long), gr[...])
        )

    gathers = nodes // long
    if fused:
        red_no.along()
        red_ni.along()
        red_o.step2(0, zs)
        gain_sum.along()
    pl.loop(0, gathers // 2, unroll=fused)(gather_back)
    if fused:
        red_ea.step2(0, zs)
    pl.loop(gathers // 2, gathers, unroll=fused)(gather_back)
    if fused:
        red_eb.step2(0, zs)
        red_o.along()
        red_ea.along()
        red_eb.along()
        red_no.share()
        red_ni.share()
    wait_all(moving)

    @pl.loop(0, nodes // tile, unroll=fused)
    def _(k):
        rows = rows_of(k)
        node_grad[rows, :] = (
            acc[rows, :]
            + dot(
                hot(list_row[:, :halo], (tile, halo), 0, k * tile),
                returned[...].reshape(halo, width),
            )
        ).astype(BF)

    if not fused:
        stores.append(pltpu.make_async_copy(node_grad, node_out, store_sems.at[1]))
        stores[1].start()
    if fused:
        red_o.share()
        red_ea.share()
        red_eb.share()
        red_no.finish(sums[0])
        red_ni.finish(sums[1])
        red_o.finish(sums[4])
        gain_sum.finish(sums[5])
        red_ea.finish(sums[2])
        red_eb.finish(sums[3])
    for store in stores:
        store.wait()


def closing(factor, depths, *refs):
    edge_in, node_in, sum_no, sum_ni, sum_ea, sum_eb, sum_o, sum_gain = refs[:8]
    outs = refs[8:16]
    holds, store_sems = refs[16:22], refs[22]
    o_ei, o_eo, o_gain_e, o_ni, o_no, o_gain_n = holds
    d_ei, d_eo, d_ni, d_no = depths
    stores = [
        pltpu.make_async_copy(source, out, store_sems.at[order])
        for order, (source, out) in enumerate(zip((edge_in, node_in) + tuple(holds), outs))
    ]
    stores[0].start()
    stores[1].start()
    for quarter in range(4):
        span = slice(quarter * LANES, (quarter + 1) * LANES)
        o_ei[: sum_ea.shape[1], span] = sum_ea[quarter].astype(F32) * factor
        o_ei[sum_ea.shape[1] :, span] = sum_eb[quarter].astype(F32) * factor
    stores[2].start()
    for quarter in range(4):
        span = slice(quarter * LANES, (quarter + 1) * LANES)
        o_ni[:, span] = sum_ni[quarter].astype(F32) * factor
        o_no[:, span] = sum_no[quarter].astype(F32) * factor
        o_eo[:, span] = sum_o[quarter].astype(F32) * factor
    for order in (3, 5, 6):
        stores[order].start()
    piece = o_gain_e.shape[1]
    p = lax.axis_index("patch")
    share = LANES // piece
    for row, hold in ((0, o_gain_e), (4, o_gain_n)):
        line = sum_gain[pl.ds(row + lax.div(p, share), 1), :]
        own = jnp.zeros((1, piece), F32)
        for part in range(share):
            own += jnp.where(lax.rem(p, share) == part, line[:, part * piece : (part + 1) * piece], 0.0)
        hold[...] = own * factor
    for order in (4, 7):
        stores[order].start()
    for store in stores:
        store.wait()


def reduction_scratch(zs, depth):
    middle = depth // 2 // PACK * PACK
    rest = depth - middle
    shapes = (
        (2, zs, 2, 2, depth),
        (zs, 2, 2, depth),
        (zs, 2, middle),
        (zs, 2, rest),
        (zs, 2, middle),
        (zs, 2, rest),
        (zs, 2, middle),
        (zs, 2, rest),
        (zs, middle),
        (zs, rest),
        (zs, rest),
        (zs, middle),
        (zs, depth),
        (zs - 1, depth),
        (4, depth),
    )
    return [pltpu.VMEM(shape + (LANES,), BF) for shape in shapes]


def local(
    n_group,
    n_patch,
    node_tape,
    edge_tape,
    node_cot,
    edge_cot,
    w_edge_in,
    w_edge_out,
    gain_edge,
    w_node_in,
    w_node_out,
    gain_node,
    senders,
    receivers,
    tile_count,
    send_rows,
):
    nodes, width = node_tape.shape[1:]
    edges = edge_tape.shape[1]
    listed = send_rows.shape[1]
    peer_rows = listed // n_patch
    padded = -(-peer_rows // PACK) * PACK
    halo = n_patch * padded
    tile = min(2 * LANES, nodes, edges)
    factor = float(n_group * n_patch * edges) ** (-0.5)

    if padded != peer_rows:
        beyond = senders - nodes
        beyond = beyond // peer_rows * padded + beyond % peer_rows
        senders = jnp.where(senders < nodes, senders, nodes + beyond)
        send_rows = jnp.pad(
            send_rows.reshape(n_patch, peer_rows),
            ((0, 0), (0, padded - peer_rows)),
            constant_values=-1,
        ).reshape(1, halo)
    slots = -(-halo // LANES) * LANES
    if slots != halo:
        send_rows = jnp.pad(send_rows, ((0, 0), (0, slots - halo)), constant_values=-1)

    def lane_rows(index):
        rows = -(-index.size // LANES)
        full = -(-rows // 8) * 8
        if index.shape == (full, LANES):
            return index
        return jnp.pad(index.reshape(-1), (0, full * LANES - index.size)).reshape(full, LANES)

    weights = (w_edge_in, w_edge_out, w_node_in, w_node_out)
    depths = [w.shape[0] // n_patch for w in weights]
    zs = n_patch // 2
    fused = (
        n_group == 4
        and n_patch % 4 == 0
        and n_patch & (n_patch - 1) == 0
        and width == 4 * LANES
        and all(d % PACK == 0 and 2 * d % LANES == 0 for d in depths)
        and min(depths) >= 2 * PACK
        and LANES * n_patch % width == 0
    )
    operands = (
        node_tape[0],
        send_rows,
        lane_rows(senders),
        lane_rows(receivers),
        edge_tape[0],
        w_edge_in,
        w_edge_out,
        gain_edge[None],
        w_node_in,
        w_node_out,
        gain_node[None],
        node_cot[0],
        edge_cot[0],
        tile_count[None],
    )
    scratch = [pltpu.VMEM(operand.shape, operand.dtype) for operand in operands]
    if not fused:
        scratch += [pltpu.VMEM((edges, width), BF), pltpu.VMEM((nodes, width), BF)]
    scratch += [
        pltpu.SemaphoreType.DMA((len(operands),)),
        pltpu.SemaphoreType.DMA((2,)),
    ]
    for length in (edges, edges, slots):
        scratch += [pltpu.VMEM((length, 1), jnp.int32), pltpu.VMEM((1, length), jnp.int32)]
    scratch += [pltpu.VMEM((n_patch, padded, width), BF)] * 4
    by_edge, by_node = pltpu.VMEM((edges, width), BF), pltpu.VMEM((nodes, width), BF)
    wide_edge, wide_node = pltpu.VMEM((edges, width), F32), pltpu.VMEM((nodes, width), F32)
    scratch += [by_edge, by_edge, wide_edge, by_edge, wide_edge, pltpu.VMEM((edges, 1), F32)]
    scratch += [by_edge, by_node]
    scratch += [by_node, wide_node, by_node, by_node, wide_node, by_node]
    scratch += [by_edge, by_edge, by_edge, by_edge, pltpu.VMEM((PACK, width), F32)]
    if fused:
        scratch += [pltpu.VMEM((edges, nodes), BF)]
    n_copies = 2 * (n_patch - 1)
    d_ei, d_eo, d_ni, d_no = depths
    reductions = []
    if fused:
        d_ea = d_ei // 2 // PACK * PACK
        shared = (d_no, d_ni, d_ea, d_ei - d_ea, d_eo)
        for depth, pairs, halves in zip(shared, (1, 2, 2, 2, 1), (1, 2, 1, 1, 1)):
            reductions += reduction_scratch(zs, depth)
            n_copies += pairs + 4 * halves + zs - 1 + 3
        reductions += [pltpu.VMEM((3, 8, LANES), F32), pltpu.VMEM((3 + zs, 8, LANES), F32)]
        n_copies += 3 + zs
        summed_shapes = [pltpu.VMEM((4, depth, LANES), BF) for depth in shared]
        summed_shapes += [pltpu.VMEM((8, LANES), F32)]
    else:
        summed_shapes = [jax.ShapeDtypeStruct((w.shape[0], width), F32) for w in weights]
        summed_shapes += [jax.ShapeDtypeStruct((PACK, width), F32)]
    in_flight = n_copies // 3 + 1 if fused else n_copies
    scratch += [pltpu.SemaphoreType.DMA((in_flight,)), pltpu.SemaphoreType.DMA((n_copies,))]
    scratch += reductions

    vmem = pl.BlockSpec(memory_space=pltpu.VMEM)
    big = pltpu.VMEM if fused else jax.ShapeDtypeStruct
    anywhere = pl.BlockSpec(memory_space=pl.ANY)
    sizes = (n_group, n_patch, padded, tile, senders.shape[1], fused, depths)
    edge_grad, node_grad, *sums = pl.pallas_call(
        functools.partial(kernel, sizes),
        out_shape=[big((edges, width), BF), big((nodes, width), BF)] + summed_shapes,
        in_specs=[anywhere] * len(operands),
        out_specs=[vmem if fused else anywhere] * 2 + [vmem] * len(summed_shapes),
        scratch_shapes=scratch,
        compiler_params=pltpu.CompilerParams(
            collective_id=0, has_side_effects=True, vmem_limit_bytes=54 * 1024 * 1024
        ),
    )(*operands)
    if fused:
        piece = width // n_patch
        rows_out = [jax.ShapeDtypeStruct((depth, width), F32) for depth in depths]
        gain_out = jax.ShapeDtypeStruct((1, piece), F32)
        o_ei, o_eo, o_ni, o_no = rows_out
        edge_grad, node_grad, o_ei, o_eo, gain_e, o_ni, o_no, gain_n = pl.pallas_call(
            functools.partial(closing, factor, depths),
            out_shape=[
                jax.ShapeDtypeStruct((edges, width), BF),
                jax.ShapeDtypeStruct((nodes, width), BF),
                o_ei,
                o_eo,
                gain_out,
                o_ni,
                o_no,
                gain_out,
            ],
            in_specs=[vmem] * 8,
            out_specs=[anywhere] * 8,
            scratch_shapes=[
                pltpu.VMEM((d_ei, width), F32),
                pltpu.VMEM((d_eo, width), F32),
                pltpu.VMEM((1, piece), F32),
                pltpu.VMEM((d_ni, width), F32),
                pltpu.VMEM((d_no, width), F32),
                pltpu.VMEM((1, piece), F32),
                pltpu.SemaphoreType.DMA((8,)),
            ],
            compiler_params=pltpu.CompilerParams(vmem_limit_bytes=16 * 1024 * 1024),
        )(*[pltpu.with_memory_space_constraint(x, pltpu.VMEM) for x in (edge_grad, node_grad, *sums)])
        return (
            edge_grad[None],
            node_grad[None],
            o_ei,
            o_eo,
            gain_e.reshape(piece),
            o_ni,
            o_no,
            gain_n.reshape(piece),
        )
    p_ei, p_eo, p_ni, p_no, p_gain = sums

    def summed(value):
        part = lax.psum_scatter(value, "patch", scatter_dimension=0, tiled=True)
        return lax.psum(part.astype(BF), "group").astype(F32) * factor

    return (
        edge_grad[None],
        node_grad[None],
        summed(p_ei),
        summed(p_eo),
        summed(p_gain[0]),
        summed(p_ni),
        summed(p_no),
        summed(p_gain[1]),
    )


def solution(mesh):
    member = P("group", "patch", None)
    placed = (member,) * 4 + (P(),) * 6
    placed += (P("patch", None), P("patch", None), P("patch"), P("patch", None))
    rows = P("patch", None)
    return jax.shard_map(
        functools.partial(local, mesh.shape["group"], mesh.shape["patch"]),
        mesh=mesh,
        in_specs=placed,
        out_specs=(member, member, rows, rows, P("patch"), rows, rows, P("patch")),
        check_vma=False,
    )
```
